128 devices in a mesh: chan: 8 (over x, z_lo), facet: 16 (over y, z_hi, core).
Axes of the slice: x: 4, y: 4, z: 4 (z_hi: 2, z_lo: 2; z = z_hi * 2 + z_lo), core: 2. Of those that a mesh axis runs over, the one named last changes fastest.
Arguments:
- image_field: float32 [8, 2048, 2048], P('chan', 'facet'), may hold values from -6 to 6
- weights: bfloat16 [8, 2048, 2048], P('chan', None, 'facet'), may hold values from 0.049804688 to 1
- measured: bfloat16 [8, 2, 2048, 2048], P('chan', None, None, 'facet'), may hold values from -6 to 6
- dual_field: bfloat16 [8, 2, 2048, 2048], P(None, None, 'facet', 'chan'), may hold values from -3 to 3
Outputs:
- image_next: float32 [8, 2048, 2048], P(None, 'facet', 'chan')
- dual_next: bfloat16 [8, 2, 2048, 2048], P(None, None, 'facet', 'chan')
The draws below stay inside these ranges and needn't reach their ends.
All inputs are finite; a program needn't handle non-finite values.
Results may differ from the reference program's by a relative error of at most 0.001.
Values sent between devices are 32-bit elements; how exact they have to be, the bound alone decides.
No kernel may reach another device: no remote copies, remote signals or barrier semaphores. Data moves between devices by JAX's collectives and lax.ppermute only.
A program may use at most 64 MiB of HBM per device.

```python
import math
import jax
import jax.numpy as jnp
from jax import lax

GRID = 2048
CHANNELS = 8


def block_levels(key, dims, split, low, top_value):
    loudness = 1.0
    for axis_at, shards_of in split:
        steps = jax.random.uniform(jax.random.fold_in(jax.random.fold_in(key, 6), axis_at), (shards_of,), jnp.float32, low / len(split), top_value / len(split))
        loudness = loudness * jnp.repeat(jnp.exp(steps), dims[axis_at] // shards_of).reshape((-1,) + (1,) * (len(dims) - 1 - axis_at))
    return loudness


def gaussian(own_key, shape, width, reach, split=(), dtype=jnp.bfloat16):
    drawn = width * jax.random.normal(own_key, shape, jnp.float32)
    if split:
        drawn = drawn * block_levels(own_key, shape, split, -0.22, 0.18)
    return jnp.clip(drawn, -reach, reach).astype(dtype)


def setup_inputs(seed: int = 0) -> dict:
    key_of = jax.random.split(jax.random.key(seed), 5)
    return {
        "image_field": gaussian(key_of[0], (CHANNELS, GRID, GRID), 1.0, 6.0, ((0, 8), (1, 16)), jnp.float32),
        "weights": jnp.clip(jnp.exp(math.log(1.0) - 2.9996462 * jax.random.uniform(key_of[1], (CHANNELS, GRID, GRID), jnp.float32) ** block_levels(key_of[1], (CHANNELS, GRID, GRID), ((0, 8), (2, 16)), -0.2, 0.2)), 0.049804688, 1.0).astype(jnp.bfloat16),
        "measured": gaussian(key_of[2], (CHANNELS, 2, GRID, GRID), 1.0, 6.0, ((0, 8), (3, 16))),
        "dual_field": gaussian(key_of[3], (CHANNELS, 2, GRID, GRID), 0.5, 3.0, ((2, 16), (3, 8))),
    }


step_primal = 0.5
step_dual = 0.5
clip_radius = 4.0

def reference(image_field, weights, measured, dual_field):

    def channel_gradient(inputs):
        channel_image, channel_weight, channel_data = inputs
        spectrum = jnp.fft.fft2(channel_image) / GRID
        residual = channel_weight.astype(jnp.float32) * spectrum - (channel_data[0].astype(jnp.float32) + 1j * channel_data[1].astype(jnp.float32))
        return jnp.real(jnp.fft.ifft2(residual)) * GRID
    gradient = lax.map(channel_gradient, (image_field, weights, measured))
    dual_rows = dual_field[:, 0].astype(jnp.float32)
    dual_cols = dual_field[:, 1].astype(jnp.float32)
    prev_rows = jnp.pad(dual_rows, ((0, 0), (1, 0), (0, 0)))[:, :-1, :]
    prev_cols = jnp.pad(dual_cols, ((0, 0), (0, 0), (1, 0)))[:, :, :-1]
    adjoint = prev_rows - dual_rows + prev_cols - dual_cols
    image_next = image_field - step_primal * (gradient + adjoint)
    extrapolated = 2.0 * image_next - image_field
    diff_rows = jnp.pad(extrapolated, ((0, 0), (0, 1), (0, 0)))[:, 1:, :] - extrapolated
    diff_cols = jnp.pad(extrapolated, ((0, 0), (0, 0), (0, 1)))[:, :, 1:] - extrapolated
    first_part = dual_rows + step_dual * diff_rows
    second_part = dual_cols + step_dual * diff_cols
    magnitude = jnp.sqrt(lax.optimization_barrier(jnp.sum(first_part * first_part + second_part * second_part, axis=0)))
    factor = 1.0 / jnp.maximum(1.0, magnitude / clip_radius)
    dual_next = jnp.stack([first_part * factor, second_part * factor], axis=1).astype(jnp.bfloat16)
    return (image_next, dual_next)
```

```python
from functools import partial
import math

import jax
import jax.numpy as jnp
import ml_dtypes
import numpy as np
from jax import lax
from jax.experimental import pallas as pl
from jax.experimental.pallas import tpu as pltpu
from jax.sharding import PartitionSpec as P

GRID = 2048
RADIX = 16
LANES = 128
CHANNELS = 8

step_primal = 0.5
step_dual = 0.5
clip_radius = 4.0

PARAMS = pltpu.CompilerParams(vmem_limit_bytes=48 * 1024 * 1024)


def host_tables():
    index = np.arange(LANES)
    angle = 2.0 * np.pi * (index[:, None] * index[None, :] % LANES) / LANES
    cos, sin = np.cos(angle), np.sin(angle)
    forward = np.block([[cos, -sin], [sin, cos]])
    inverse = np.block([[cos, sin], [-sin, cos]])
    turn = 2.0 * np.pi * np.arange(RADIX)[:, None] * index[None, :] / GRID
    twiddle = np.stack([np.cos(turn), np.sin(turn)]).astype(np.float32)
    place = np.zeros((LANES, LANES))
    for at in range(LANES):
        place[at, 16 * (at % 8) + at // 8] = 1.0
    return forward, inverse, twiddle, place


def halves(table):
    high = table.astype(ml_dtypes.bfloat16)
    low = (table - high.astype(np.float64)).astype(ml_dtypes.bfloat16)
    return np.stack([high, low])


def c_add(a, b):
    return (a[0] + b[0], b[1] if a[1] is None else a[1] if b[1] is None else a[1] + b[1])


def c_sub(a, b):
    imag = None
    if a[1] is not None and b[1] is not None:
        imag = a[1] - b[1]
    elif a[1] is not None:
        imag = a[1]
    elif b[1] is not None:
        imag = -b[1]
    return (a[0] - b[0], imag)


def add_turned(a, b, sign):
    real = a[0] if b[1] is None else (a[0] - b[1] if sign > 0 else a[0] + b[1])
    if a[1] is None:
        imag = b[0] if sign > 0 else -b[0]
    else:
        imag = a[1] + b[0] if sign > 0 else a[1] - b[0]
    return (real, imag)


def four(a, b, c, d, sign):
    sum_even, diff_even = c_add(a, c), c_sub(a, c)
    sum_odd, diff_odd = c_add(b, d), c_sub(b, d)
    return (
        c_add(sum_even, sum_odd),
        add_turned(diff_even, diff_odd, sign),
        c_sub(sum_even, sum_odd),
        add_turned(diff_even, diff_odd, -sign),
    )


def turned(a, power, sign):
    power = power % 16
    if power == 0:
        return a
    cos, sin = math.cos(2 * math.pi * power / 16), sign * math.sin(2 * math.pi * power / 16)
    real, imag = a
    if imag is None:
        if power == 4:
            return (jnp.zeros_like(real), real if sign > 0 else -real)
        return (real * cos, real * sin)
    if power == 4:
        return (-imag, real) if sign > 0 else (imag, -real)
    if abs(abs(cos) - abs(sin)) < 1e-9:
        root = math.sqrt(0.5)
        cs, ss = (1 if cos > 0 else -1), (1 if sin > 0 else -1)
        new_real = (real if cs > 0 else -real) - (imag if ss > 0 else -imag)
        new_imag = (real if ss > 0 else -real) + (imag if cs > 0 else -imag)
        return (new_real * root, new_imag * root)
    return (real * cos - imag * sin, real * sin + imag * cos)


def sixteen(values, sign):
    inner = [four(*(values[n0 + 4 * n1] for n1 in range(4)), sign) for n0 in range(4)]
    out = [None] * 16
    for k1 in range(4):
        parts = [turned(inner[n0][k1], n0 * k1, sign) for n0 in range(4)]
        for k2, value in enumerate(four(*parts, sign)):
            out[k1 + 4 * k2] = value
    return out


def split(value):
    high = value.astype(jnp.bfloat16)
    low = (value - high.astype(jnp.float32)).astype(jnp.bfloat16)
    return high, low


def dot(a, b, dims):
    return lax.dot_general(a, b, (dims, ((), ())), preferred_element_type=jnp.float32)


def rows_forward(image, twiddle, table, out, held_high, held_low):
    chunk = 16

    def body(step, carry):
        at = pl.multiple_of(step * chunk, chunk)
        values = [
            (image[pl.ds(at, chunk), b * LANES : (b + 1) * LANES], None) for b in range(RADIX)
        ]
        mixed = sixteen(values, -1)
        for f in range(RADIX):
            real, imag = mixed[f]
            if imag is None:
                imag = jnp.zeros_like(real)
            cos, sin = twiddle[0, f : f + 1, :], twiddle[1, f : f + 1, :]
            high_r, low_r = split(real * cos + imag * sin)
            high_i, low_i = split(imag * cos - real * sin)
            rows = pl.ds(f * LANES + at, chunk)
            held_high[rows, :LANES] = high_r
            held_high[rows, LANES:] = high_i
            held_low[rows, :LANES] = low_r
            held_low[rows, LANES:] = low_i
        return carry

    lax.fori_loop(0, LANES // chunk, body, 0)
    high_t, low_t = table[0], table[1]
    dims = ((1,), (1,))
    for g in range(RADIX // 2):
        high, low = held_high[256 * g : 256 * g + 256, :], held_low[256 * g : 256 * g + 256, :]
        result = dot(high_t, high, dims) + dot(high_t, low, dims) + dot(low_t, high, dims)
        for h in range(2):
            for c in range(2):
                block = result[c * LANES : (c + 1) * LANES, h * LANES : (h + 1) * LANES]
                out[:, c, 2 * g + h] = block.reshape(RADIX, 8, LANES)


def data_prepared(weights, measured, place, out, held):
    for n in range(3):
        source = weights[...] if n == 0 else measured[n - 1]
        held[...] = source.astype(jnp.float32)
        for f in range(RADIX):
            rows = held[pl.ds(f, LANES, stride=RADIX), :].astype(jnp.bfloat16)
            out[n, f] = dot(place[...], rows, ((1,), (1,))).astype(jnp.bfloat16)


def columns(cols, data, twiddle, forward, inverse, out, held_high, held_low):
    chunk = 32
    rows_all = RADIX * chunk
    dims = ((1,), (0,))

    def store(f, real, imag):
        high_r, low_r = split(real)
        high_i, low_i = split(imag)
        rows = slice(f * chunk, (f + 1) * chunk)
        held_high[rows, :LANES] = high_r
        held_high[rows, LANES:] = high_i
        held_low[rows, :LANES] = low_r
        held_low[rows, LANES:] = low_i

    def product(table):
        high, low = held_high[...], held_low[...]
        return dot(high, table[0], dims) + dot(low, table[0], dims) + dot(high, table[1], dims)

    def body(step, carry):
        at = pl.multiple_of(step * chunk, chunk)
        here = pl.ds(at, chunk)
        mixed = sixteen([(cols[b, 0, here, :], cols[b, 1, here, :]) for b in range(RADIX)], -1)
        for f in range(RADIX):
            real, imag = mixed[f]
            cos, sin = twiddle[0, f : f + 1, :], twiddle[1, f : f + 1, :]
            store(f, real * cos + imag * sin, imag * cos - real * sin)
        spectrum = product(forward)
        for f in range(RADIX):
            piece = spectrum[f * chunk : (f + 1) * chunk]
            weight = data[0, f, here, :].astype(jnp.float32)
            real = weight * piece[:, :LANES] - data[1, f, here, :].astype(jnp.float32)
            imag = weight * piece[:, LANES:] - data[2, f, here, :].astype(jnp.float32)
            store(f, real, imag)
        back = product(inverse)
        values = []
        for f in range(RADIX):
            real = back[f * chunk : (f + 1) * chunk, :LANES]
            imag = back[f * chunk : (f + 1) * chunk, LANES:]
            cos, sin = twiddle[0, f : f + 1, :], twiddle[1, f : f + 1, :]
            values.append((real * cos - imag * sin, imag * cos + real * sin))
        mixed = sixteen(values, 1)
        for b in range(RADIX):
            out[b, 0, here, :] = mixed[b][0]
            out[b, 1, here, :] = mixed[b][1]
        return carry

    lax.fori_loop(0, LANES // chunk, body, 0)


def rows_back(lines, image, twiddle, table, out, held):
    dims = ((0,), (0,))
    high_t, low_t = table[0], table[1]
    for f in range(RADIX):
        real = lines[:, 0, f].reshape(LANES, LANES)
        imag = lines[:, 1, f].reshape(LANES, LANES)
        high, low = split(jnp.concatenate([real, imag], axis=0))
        held[f] = dot(high, high_t, dims) + dot(low, high_t, dims) + dot(high, low_t, dims)
    chunk = 16

    def body(step, carry):
        at = pl.multiple_of(step * chunk, chunk)
        here = pl.ds(at, chunk)
        values = []
        for f in range(RADIX):
            real, imag = held[f, here, :LANES], held[f, here, LANES:]
            cos, sin = twiddle[0, f : f + 1, :], twiddle[1, f : f + 1, :]
            values.append((real * cos - imag * sin, imag * cos + real * sin))
        mixed = sixteen(values, 1)
        for b in range(RADIX):
            low_lane = (b % 2) * LANES
            out[b // 2, 1, here, low_lane : low_lane + LANES] = mixed[b][0]
            out[b // 2, 0, here, low_lane : low_lane + LANES] = image[
                here, b * LANES : (b + 1) * LANES
            ]
        return carry

    lax.fori_loop(0, LANES // chunk, body, 0)


def dual_edges(dual, last_row, last_column):
    rows, cols = [], []
    for c in range(CHANNELS):
        rows.append(dual[c, 0, 112:128, :].astype(jnp.float32)[15:16, :])
        cols.append(dual[c, 1, :, LANES:].astype(jnp.float32)[:, LANES - 1 :])
    last_row[...] = jnp.concatenate(rows, axis=0)
    last_column[...] = jnp.concatenate(cols, axis=1).T


def primal(tile, dual, above, left, image_next, extrapolated, first_row, first_column):
    left_columns = left[...].T
    row_at = lax.broadcasted_iota(jnp.int32, (LANES, 2 * LANES), 0)
    lane_at = lax.broadcasted_iota(jnp.int32, (LANES, 2 * LANES), 1)
    rows, cols = [], []
    for c in range(CHANNELS):
        p = dual[c, 0].astype(jnp.float32)
        q = dual[c, 1].astype(jnp.float32)
        prev_p = jnp.where(row_at == 0, above[c : c + 1, :], pltpu.roll(p, 1, 0))
        prev_q = jnp.where(lane_at == 0, left_columns[:, c : c + 1], pltpu.roll(q, 1, 1))
        adjoint = prev_p - p + prev_q - q
        image = tile[c, 0]
        updated = image - step_primal * (tile[c, 1] + adjoint)
        ahead = 2.0 * updated - image
        image_next[c] = updated
        extrapolated[c] = ahead
        rows.append(ahead[0:1, :])
        cols.append(ahead[:, 0:1])
    first_row[...] = jnp.concatenate(rows, axis=0)
    first_column[...] = jnp.concatenate(cols, axis=1).T


def dual_step(extrapolated, dual, below, right, out):
    chunk = 16
    right_columns = right[...].T
    row_at = lax.broadcasted_iota(jnp.int32, (chunk, 2 * LANES), 0)
    lane_at = lax.broadcasted_iota(jnp.int32, (chunk, 2 * LANES), 1)
    for step in range(LANES // chunk):
        at = step * chunk
        here = slice(at, at + chunk)
        firsts, seconds, total = [], [], None
        for c in range(CHANNELS):
            ahead = extrapolated[c, here, :]
            if step + 1 < LANES // chunk:
                next_row = extrapolated[c, at + chunk : at + chunk + 1, :]
            else:
                next_row = below[c : c + 1, :]
            down = jnp.where(row_at == chunk - 1, next_row, pltpu.roll(ahead, chunk - 1, 0))
            beside = jnp.where(
                lane_at == 2 * LANES - 1,
                right_columns[here, c : c + 1],
                pltpu.roll(ahead, 2 * LANES - 1, 1),
            )
            first = dual[c, 0, here, :].astype(jnp.float32) + step_dual * (down - ahead)
            second = dual[c, 1, here, :].astype(jnp.float32) + step_dual * (beside - ahead)
            firsts.append(first)
            seconds.append(second)
            squares = first * first + second * second
            total = squares if total is None else total + squares
        factor = 1.0 / jnp.maximum(1.0, jnp.sqrt(total) / clip_radius)
        for c in range(CHANNELS):
            out[c, 0, here, :] = (firsts[c] * factor).astype(jnp.bfloat16)
            out[c, 1, here, :] = (seconds[c] * factor).astype(jnp.bfloat16)


def shape(dims, dtype=jnp.float32):
    return jax.ShapeDtypeStruct(dims, dtype)


def passed_along(x, axis, by):
    devices = lax.axis_size(axis)
    pairs = [(i, i + by) for i in range(devices) if 0 <= i + by < devices]
    return lax.ppermute(x, axis, pairs)


def shards(image_field, weights, measured, dual_field):
    forward, inverse, twiddle, place = host_tables()
    scale = 1.0 / GRID
    place = jnp.asarray(place, jnp.bfloat16)
    twiddle = jnp.asarray(twiddle)
    image = image_field[0]
    bf16 = jnp.bfloat16

    last_row, last_column = pl.pallas_call(
        dual_edges,
        out_shape=(shape((CHANNELS, 2 * LANES)), shape((CHANNELS, LANES))),
        name="dual_edges",
        compiler_params=PARAMS,
    )(dual_field)
    above = passed_along(last_row, "facet", 1)
    left = passed_along(last_column, "chan", 1)

    spread = pl.pallas_call(
        rows_forward,
        out_shape=shape((RADIX, 2, RADIX, 8, LANES)),
        scratch_shapes=[pltpu.VMEM((GRID, 256), bf16), pltpu.VMEM((GRID, 256), bf16)],
        name="rows_forward",
        compiler_params=PARAMS,
    )(image, twiddle, jnp.asarray(halves(forward.T * scale)))
    cols = lax.all_to_all(
        spread.reshape(RADIX, 2 * LANES, LANES), "facet", split_axis=0, concat_axis=0, tiled=True
    ).reshape(RADIX, 2, LANES, LANES)
    data = pl.pallas_call(
        data_prepared,
        out_shape=shape((3, RADIX, LANES, LANES), bf16),
        scratch_shapes=[pltpu.VMEM((GRID, LANES), jnp.float32)],
        name="data_prepared",
        compiler_params=PARAMS,
    )(weights[0], measured[0], place)
    back = pl.pallas_call(
        columns,
        out_shape=shape((RADIX, 2, LANES, LANES)),
        scratch_shapes=[pltpu.VMEM((RADIX * 32, 256), bf16), pltpu.VMEM((RADIX * 32, 256), bf16)],
        name="columns",
        compiler_params=PARAMS,
    )(cols, data, twiddle, jnp.asarray(halves(forward)), jnp.asarray(halves(inverse)))
    lines = lax.all_to_all(
        back.reshape(RADIX, 2 * LANES, LANES), "facet", split_axis=0, concat_axis=0, tiled=True
    ).reshape(RADIX, 2, RADIX, 8, LANES)
    tiles = pl.pallas_call(
        rows_back,
        out_shape=shape((CHANNELS, 2, LANES, 2 * LANES)),
        scratch_shapes=[pltpu.VMEM((RADIX, LANES, 256), jnp.float32)],
        name="rows_back",
        compiler_params=PARAMS,
    )(lines, image, twiddle, jnp.asarray(halves(inverse * scale)))
    tile = lax.all_to_all(
        tiles.reshape(CHANNELS, 2 * LANES, 2 * LANES),
        "chan",
        split_axis=0,
        concat_axis=0,
        tiled=True,
    ).reshape(CHANNELS, 2, LANES, 2 * LANES)
    image_next, extrapolated, first_row, first_column = pl.pallas_call(
        primal,
        out_shape=(
            shape((CHANNELS, LANES, 2 * LANES)),
            shape((CHANNELS, LANES, 2 * LANES)),
            shape((CHANNELS, 2 * LANES)),
            shape((CHANNELS, LANES)),
        ),
        name="primal",
        compiler_params=PARAMS,
    )(tile, dual_field, above, left)
    below = passed_along(first_row, "facet", -1)
    right = passed_along(first_column, "chan", -1)
    dual_next = pl.pallas_call(
        dual_step,
        out_shape=shape((CHANNELS, 2, LANES, 2 * LANES), bf16),
        name="dual_step",
        compiler_params=PARAMS,
    )(extrapolated, dual_field, below, right)
    return (image_next, dual_next)


def solution(mesh):
    placed = (
        P("chan", "facet", None),
        P("chan", None, "facet"),
        P("chan", None, None, "facet"),
        P(None, None, "facet", "chan"),
    )
    return jax.shard_map(
        shards,
        mesh=mesh,
        in_specs=placed,
        out_specs=(P(None, "facet", "chan"), P(None, None, "facet", "chan")),
        check_vma=False,
    )
```

```python
from functools import partial
import math

import jax
import jax.numpy as jnp
import ml_dtypes
import numpy as np
from jax import lax
from jax.experimental import pallas as pl
from jax.experimental.pallas import tpu as pltpu
from jax.sharding import PartitionSpec as P

GRID = 2048
RADIX = 16
LANES = 128
CHANNELS = 8

step_primal = 0.5
step_dual = 0.5
clip_radius = 4.0

PARAMS = pltpu.CompilerParams(vmem_limit_bytes=48 * 1024 * 1024)


def host_tables():
    index = np.arange(LANES)
    angle = 2.0 * np.pi * (index[:, None] * index[None, :] % LANES) / LANES
    cos, sin = np.cos(angle), np.sin(angle)
    forward = np.block([[cos, -sin], [sin, cos]])
    inverse = np.block([[cos, sin], [-sin, cos]])
    turn = 2.0 * np.pi * np.arange(RADIX)[:, None] * index[None, :] / GRID
    twiddle = np.stack([np.cos(turn), np.sin(turn)]).astype(np.float32)
    place = np.zeros((LANES, LANES))
    for at in range(LANES):
        place[at, 16 * (at % 8) + at // 8] = 1.0
    return forward, inverse, twiddle, place


def halves(table):
    high = table.astype(ml_dtypes.bfloat16)
    low = (table - high.astype(np.float64)).astype(ml_dtypes.bfloat16)
    return np.concatenate([high, high, low], axis=0)


def c_add(a, b):
    return (a[0] + b[0], b[1] if a[1] is None else a[1] if b[1] is None else a[1] + b[1])


def c_sub(a, b):
    imag = None
    if a[1] is not None and b[1] is not None:
        imag = a[1] - b[1]
    elif a[1] is not None:
        imag = a[1]
    elif b[1] is not None:
        imag = -b[1]
    return (a[0] - b[0], imag)


def add_turned(a, b, sign):
    real = a[0] if b[1] is None else (a[0] - b[1] if sign > 0 else a[0] + b[1])
    if a[1] is None:
        imag = b[0] if sign > 0 else -b[0]
    else:
        imag = a[1] + b[0] if sign > 0 else a[1] - b[0]
    return (real, imag)


def four(a, b, c, d, sign):
    sum_even, diff_even = c_add(a, c), c_sub(a, c)
    sum_odd, diff_odd = c_add(b, d), c_sub(b, d)
    return (
        c_add(sum_even, sum_odd),
        add_turned(diff_even, diff_odd, sign),
        c_sub(sum_even, sum_odd),
        add_turned(diff_even, diff_odd, -sign),
    )


def turned(a, power, sign):
    power = power % 16
    if power == 0:
        return a
    cos, sin = math.cos(2 * math.pi * power / 16), sign * math.sin(2 * math.pi * power / 16)
    real, imag = a
    if imag is None:
        if power == 4:
            return (jnp.zeros_like(real), real if sign > 0 else -real)
        return (real * cos, real * sin)
    if power == 4:
        return (-imag, real) if sign > 0 else (imag, -real)
    if abs(abs(cos) - abs(sin)) < 1e-9:
        root = math.sqrt(0.5)
        cs, ss = (1 if cos > 0 else -1), (1 if sin > 0 else -1)
        new_real = (real if cs > 0 else -real) - (imag if ss > 0 else -imag)
        new_imag = (real if ss > 0 else -real) + (imag if cs > 0 else -imag)
        return (new_real * root, new_imag * root)
    return (real * cos - imag * sin, real * sin + imag * cos)


def sixteen(values, sign):
    inner = [four(*(values[n0 + 4 * n1] for n1 in range(4)), sign) for n0 in range(4)]
    out = [None] * 16
    for k1 in range(4):
        parts = [turned(inner[n0][k1], n0 * k1, sign) for n0 in range(4)]
        for k2, value in enumerate(four(*parts, sign)):
            out[k1 + 4 * k2] = value
    return out


def split(value):
    high = value.astype(jnp.bfloat16)
    low = (value - high.astype(jnp.float32)).astype(jnp.bfloat16)
    return high, low


def dot(a, b, dims):
    return lax.dot_general(a, b, (dims, ((), ())), preferred_element_type=jnp.float32)


def fetched(source, target, semaphore):
    copy = pltpu.make_async_copy(source, target, semaphore)
    copy.start()
    return copy


def three_pass(pair, table, dims):
    high = pair[:, :256] if dims[0][0] == 1 else pair[:256, :]
    return dot(pair, table[:512, :], dims) + dot(high, table[512:, :], dims)


def store_pair(held, rows, real, imag):
    high_r, low_r = split(real)
    high_i, low_i = split(imag)
    held[rows, 0:LANES] = high_r
    held[rows, LANES : 2 * LANES] = high_i
    held[rows, 2 * LANES : 3 * LANES] = low_r
    held[rows, 3 * LANES : 4 * LANES] = low_i


def rows_forward(
    where, image, twiddle, table, out, *rest
):
    pieces, (image_v, twiddle_v, table_v, out_v, held, in_sems, out_sems) = rest[:4], rest[4:]
    chunk = 16
    steps = LANES // chunk

    def incoming(step):
        rows = pl.ds(pl.multiple_of(step * chunk, chunk), chunk)
        return pltpu.make_async_copy(image.at[rows, :], image_v.at[rows, :], in_sems.at[step])

    for step in range(steps):
        incoming(step).start()
    get_twiddle = fetched(twiddle, twiddle_v, in_sems.at[steps])
    get_table = fetched(table, table_v, in_sems.at[steps + 1])
    sent = []
    for k in range(4):
        lanes = pl.ds(pl.multiple_of((where[0] + k) % 4 * 512, 512), 512)
        sent.append(fetched(image.at[:, lanes], pieces[k], out_sems.at[8 + k]))
    get_twiddle.wait()

    def body(step, carry):
        incoming(step).wait()
        at = pl.multiple_of(step * chunk, chunk)
        values = [
            (image_v[pl.ds(at, chunk), b * LANES : (b + 1) * LANES], None) for b in range(RADIX)
        ]
        mixed = sixteen(values, -1)
        for f in range(RADIX):
            real, imag = mixed[f]
            if imag is None:
                imag = jnp.zeros_like(real)
            cos, sin = twiddle_v[0, f : f + 1, :], twiddle_v[1, f : f + 1, :]
            store_pair(
                held,
                pl.ds(f * LANES + at, chunk),
                real * cos + imag * sin,
                imag * cos - real * sin,
            )
        return carry

    lax.fori_loop(0, steps, body, 0)
    get_table.wait()
    dims = ((1,), (1,))
    for g in range(RADIX // 2):
        pair = held[256 * g : 256 * g + 256, :]
        result = dot(table_v[:, :512], pair, dims) + dot(table_v[:, 512:], pair[:, :256], dims)
        for h in range(2):
            for c in range(2):
                block = result[c * LANES : (c + 1) * LANES, h * LANES : (h + 1) * LANES]
                out_v[:, c, 2 * g + h] = block.reshape(RADIX, 8, LANES)
        both = pl.ds(2 * g, 2)
        sent.append(fetched(out_v.at[:, :, both], out.at[:, :, both], out_sems.at[g]))
    for copy in sent:
        copy.wait()


def data_prepared(weights, measured, place, out, held, out_v, sems):
    copies = []
    for n in range(3):
        source = weights[...] if n == 0 else measured[n - 1]
        held[...] = source.astype(jnp.float32)
        for f in range(RADIX):
            rows = held[pl.ds(f, LANES, stride=RADIX), :].astype(jnp.bfloat16)
            out_v[n, f] = dot(place[...], rows, ((1,), (1,))).astype(jnp.bfloat16)
        copies.append(fetched(out_v.at[n], out.at[n], sems.at[n]))
    for copy in copies:
        copy.wait()


def columns(
    cols, data, twiddle, forward, inverse, out,
    cols_v, data_v, forward_v, inverse_v, out_v, edge_v, held, in_sems, data_sems, out_sems,
):
    chunk = 32
    steps = LANES // chunk
    dims = ((1,), (0,))

    def incoming(step):
        rows = pl.ds(pl.multiple_of(step * chunk, chunk), chunk)
        return pltpu.make_async_copy(
            cols.at[:, :, rows, :], cols_v.at[:, :, rows, :], in_sems.at[step]
        )

    def incoming_data(step):
        rows = pl.ds(pl.multiple_of(step * chunk, chunk), chunk)
        return pltpu.make_async_copy(
            data.at[:, :, rows, :], data_v.at[:, :, rows, :], data_sems.at[step]
        )

    def outgoing(step, c):
        rows = pl.ds(pl.multiple_of(step * chunk, chunk), chunk)
        to_rows = pl.ds(pl.multiple_of(c * LANES + step * chunk, chunk), chunk)
        return pltpu.make_async_copy(
            out_v.at[:, c, rows, :], out.at[:, to_rows, :], out_sems.at[step, c]
        )

    for step in range(steps):
        incoming(step).start()
        incoming_data(step).start()
    get_forward = fetched(forward, forward_v, in_sems.at[steps])
    get_inverse = fetched(inverse, inverse_v, in_sems.at[steps + 1])
    edge_v[...] = jnp.zeros_like(edge_v)
    get_forward.wait()
    get_inverse.wait()
    lane_at = lax.broadcasted_iota(jnp.int32, (8, LANES), 1)

    def body(step, carry):
        incoming(step).wait()
        here = pl.ds(pl.multiple_of(step * chunk, chunk), chunk)
        mixed = sixteen([(cols_v[b, 0, here, :], cols_v[b, 1, here, :]) for b in range(RADIX)], -1)
        for f in range(RADIX):
            real, imag = mixed[f]
            cos, sin = twiddle[0, f : f + 1, :], twiddle[1, f : f + 1, :]
            rows = slice(f * chunk, (f + 1) * chunk)
            store_pair(held, rows, real * cos + imag * sin, imag * cos - real * sin)
        incoming_data(step).wait()
        spectrum = three_pass(held[...], forward_v, dims)
        for f in range(RADIX):
            rows = slice(f * chunk, (f + 1) * chunk)
            weight = data_v[0, f, here, :].astype(jnp.float32)
            real = weight * spectrum[rows, :LANES] - data_v[1, f, here, :].astype(jnp.float32)
            imag = weight * spectrum[rows, LANES:] - data_v[2, f, here, :].astype(jnp.float32)
            store_pair(held, rows, real, imag)
        back = three_pass(held[...], inverse_v, dims)
        values = []
        for f in range(RADIX):
            rows = slice(f * chunk, (f + 1) * chunk)
            real, imag = back[rows, :LANES], back[rows, LANES:]
            cos, sin = twiddle[0, f : f + 1, :], twiddle[1, f : f + 1, :]
            values.append((real * cos - imag * sin, imag * cos + real * sin))
        mixed = sixteen(values, 1)
        for b in range(RADIX):
            for c in range(2):
                out_v[b, c, here, :] = mixed[b][c]
                if b > 0:
                    edge = edge_v[b - 1]
                    for i in range(chunk // 8):
                        first = mixed[b][c][8 * i : 8 * i + 8, 0:1]
                        at_lane = lane_at == c * RADIX + step * (chunk // 8) + i
                        edge = jnp.where(at_lane, first, edge)
                    edge_v[b - 1] = edge
        outgoing(step, 0).start()
        outgoing(step, 1).start()
        return carry

    lax.fori_loop(0, steps, body, 0)
    send_edge = fetched(edge_v, out.at[:, 2 * LANES :, :], in_sems.at[0])
    for step in range(steps):
        outgoing(step, 0).wait()
        outgoing(step, 1).wait()
    send_edge.wait()


def rows_back(
    lines, twiddle, table, out, lines_v, edge_v, table_v, held, out_v, side_v, in_sems, out_sems
):
    dims = ((0,), (0,))
    get_table = fetched(table, table_v, in_sems.at[5])
    arriving = []
    for g in range(4):
        for c in range(2):
            rows = pl.ds(c * LANES + 32 * g, 32)
            arriving.append(
                fetched(
                    lines.at[:, rows, :], lines_v.at[:, pl.ds(c * LANES + 32 * g, 32), :],
                    out_sems.at[2 * g + c],
                )
            )
    get_edge = fetched(lines.at[:, 2 * LANES :, :], edge_v, in_sems.at[4])
    get_table.wait()
    for f in range(RADIX):
        if f % 4 == 0:
            arriving[f // 2].wait()
            arriving[f // 2 + 1].wait()
        real = lines_v[:, 8 * f : 8 * f + 8, :].reshape(LANES, LANES)
        imag = lines_v[:, LANES + 8 * f : LANES + 8 * f + 8, :].reshape(LANES, LANES)
        high_r, low_r = split(real)
        high_i, low_i = split(imag)
        pair = jnp.concatenate([high_r, high_i, low_r, low_i], axis=0)
        held[f] = three_pass(pair, table_v, dims)
    get_edge.wait()
    high, low = split(edge_v[...].reshape(LANES, LANES))
    edge = (
        dot(high, table_v[0:LANES, :], dims)
        + dot(low, table_v[0:LANES, :], dims)
        + dot(high, table_v[512 : 512 + LANES, :], dims)
    )
    edge_r = edge[:RADIX, :LANES] - edge[RADIX : 2 * RADIX, LANES:]
    edge_i = edge[:RADIX, LANES:] + edge[RADIX : 2 * RADIX, :LANES]
    cos, sin = twiddle[0], twiddle[1]
    edge_r, edge_i = edge_r * cos - edge_i * sin, edge_i * cos + edge_r * sin
    mixed = sixteen([(edge_r[f : f + 1], edge_i[f : f + 1]) for f in range(RADIX)], 1)
    for d in range(CHANNELS):
        out_v[d, LANES : LANES + 1, :] = jnp.concatenate(
            [mixed[2 * d][0], mixed[2 * d + 1][0]], axis=1
        )
    chunk = 16
    steps = LANES // chunk
    lane_at = lax.broadcasted_iota(jnp.int32, (chunk, LANES), 1)

    def outgoing(step):
        rows = pl.ds(pl.multiple_of(step * chunk, chunk), chunk)
        return pltpu.make_async_copy(out_v.at[:, rows, :], out.at[:, rows, :], out_sems.at[step])

    def body(step, carry):
        at = pl.multiple_of(step * chunk, chunk)
        here = pl.ds(at, chunk)
        values = []
        for f in range(RADIX):
            real, imag = held[f, here, :LANES], held[f, here, LANES:]
            cos, sin = twiddle[0, f : f + 1, :], twiddle[1, f : f + 1, :]
            values.append((real * cos - imag * sin, imag * cos + real * sin))
        mixed = sixteen(values, 1)
        side = jnp.zeros((chunk, LANES), jnp.float32)
        for b in range(RADIX):
            low_lane = (b % 2) * LANES
            out_v[b // 2, here, low_lane : low_lane + LANES] = mixed[b][0]
            if b > 0 and b % 2 == 0:
                side = jnp.where(lane_at == b // 2 - 1, mixed[b][0][:, 0:1], side)
        side_v[here, :] = side
        outgoing(step).start()
        return carry

    lax.fori_loop(0, steps, body, 0)
    beside = side_v[...].T
    for d in range(CHANNELS):
        out_v[d, LANES + 1 : LANES + 2, :LANES] = beside[d : d + 1, :]
    last = fetched(
        out_v.at[:, pl.ds(LANES, 8), :], out.at[:, pl.ds(LANES, 8), :], in_sems.at[4]
    )
    for step in range(steps):
        outgoing(step).wait()
    last.wait()


def dual_edges(dual, last_row, last_column):
    rows, cols = [], []
    for c in range(CHANNELS):
        rows.append(dual[c, 0, 112:128, :].astype(jnp.float32)[15:16, :])
        cols.append(dual[c, 1, :, LANES:].astype(jnp.float32)[:, LANES - 1 :])
    last_row[...] = jnp.concatenate(rows, axis=0)
    last_column[...] = jnp.concatenate(cols, axis=1).T


def swap_ready(where, *refs):
    pieces, out, sems = refs[:4], refs[4], refs[5]
    lanes = pl.ds(pl.multiple_of((1 - where[1]) * 256, 256), 256)
    copies = [fetched(pieces[k].at[:, lanes], out.at[k], sems.at[k]) for k in range(4)]
    for copy in copies:
        copy.wait()


def tile_ready(where, *refs):
    pieces, (swapped, dual, above, left) = refs[:4], refs[4:8]
    for_image, for_ahead, first_row, first_column = refs[8:]
    row_at = lax.broadcasted_iota(jnp.int32, (LANES, 2 * LANES), 0)
    lane_at = lax.broadcasted_iota(jnp.int32, (LANES, 2 * LANES), 1)
    for k in range(4):
        for other in range(2):
            lanes = where[1] * (1 - other) + (1 - where[1]) * other
            c = (where[0] + 4 - k) % 4 * 2 + lanes
            p = dual[c, 0].astype(jnp.float32)
            q = dual[c, 1].astype(jnp.float32)
            beside = jnp.broadcast_to(left[pl.ds(c, 1), :], (LANES, LANES)).T[:, 0:1]
            prev_p = jnp.where(row_at == 0, above[pl.ds(c, 1), :], pltpu.roll(p, 1, 0))
            prev_q = jnp.where(lane_at == 0, beside, pltpu.roll(q, 1, 1))
            adjoint = prev_p - p + prev_q - q
            if other:
                image = swapped[k]
            else:
                own = pl.ds(pl.multiple_of(where[1] * 256, 256), 256)
                image = pieces[k][:, own]
            ahead = image - adjoint
            for_image[c] = image - step_primal * adjoint
            for_ahead[c] = ahead
            first_row[pl.ds(c, 1), :] = ahead[0:1, :]
            first_column[pl.ds(c, 1), :] = ahead[:, :LANES].T[0:1, :]


def finish(
    gradient, for_image, for_ahead, dual, below, right, image_next, dual_next,
    ahead_v, side_v, image_v, dual_v, image_sems, dual_sems,
):
    sides = []
    for c in range(CHANNELS):
        sides.append(gradient[c, LANES + 1 : LANES + 2, :LANES])
    side_v[:, :CHANNELS] = (right[...] - jnp.concatenate(sides, axis=0)).T
    for c in range(CHANNELS):
        slope = gradient[c, :LANES, :]
        image_v[c] = for_image[c] - step_primal * slope
        ahead_v[c, :LANES, :] = for_ahead[c] - slope
        ahead_v[c, LANES : LANES + 1, :] = (
            below[c : c + 1, :] - gradient[c, LANES : LANES + 1, :]
        )
        pltpu.make_async_copy(image_v.at[c], image_next.at[c], image_sems.at[c]).start()
    chunk = 16
    steps = LANES // chunk
    row_at = lax.broadcasted_iota(jnp.int32, (chunk, 2 * LANES), 0)
    lane_at = lax.broadcasted_iota(jnp.int32, (chunk, 2 * LANES), 1)

    def outgoing(step):
        rows = pl.ds(pl.multiple_of(step * chunk, chunk), chunk)
        return pltpu.make_async_copy(
            dual_v.at[:, :, rows, :], dual_next.at[:, :, rows, :], dual_sems.at[step]
        )

    def body(step, carry):
        at = pl.multiple_of(step * chunk, chunk)
        here = pl.ds(at, chunk)
        after = pl.ds(pl.multiple_of(at + chunk, chunk), 8)
        firsts, seconds, total = [], [], None
        for c in range(CHANNELS):
            ahead = ahead_v[c, here, :]
            next_row = ahead_v[c, after, :][0:1, :]
            down = jnp.where(row_at == chunk - 1, next_row, pltpu.roll(ahead, chunk - 1, 0))
            beside = jnp.where(
                lane_at == 2 * LANES - 1,
                side_v[here, c : c + 1],
                pltpu.roll(ahead, 2 * LANES - 1, 1),
            )
            first = dual[c, 0, here, :].astype(jnp.float32) + step_dual * (down - ahead)
            second = dual[c, 1, here, :].astype(jnp.float32) + step_dual * (beside - ahead)
            firsts.append(first)
            seconds.append(second)
            squares = first * first + second * second
            total = squares if total is None else total + squares
        factor = 1.0 / jnp.maximum(1.0, jnp.sqrt(total) / clip_radius)
        for c in range(CHANNELS):
            dual_v[c, 0, here, :] = (firsts[c] * factor).astype(jnp.bfloat16)
            dual_v[c, 1, here, :] = (seconds[c] * factor).astype(jnp.bfloat16)
        outgoing(step).start()
        return carry

    lax.fori_loop(0, steps, body, 0)
    for c in range(CHANNELS):
        pltpu.make_async_copy(image_v.at[c], image_next.at[c], image_sems.at[c]).wait()
    for step in range(steps):
        outgoing(step).wait()


def shape(dims, dtype=jnp.float32):
    return jax.ShapeDtypeStruct(dims, dtype)


def passed_along(x, axis, by):
    devices = lax.axis_size(axis)
    pairs = [(i, i + by) for i in range(devices) if 0 <= i + by < devices]
    return lax.ppermute(x, axis, pairs)


ANY = pl.BlockSpec(memory_space=pl.ANY)
HBM = pl.BlockSpec(memory_space=pltpu.HBM)
VM = pl.BlockSpec(memory_space=pltpu.VMEM)
SM = pl.BlockSpec(memory_space=pltpu.SMEM)
DMA = pltpu.SemaphoreType.DMA


def call(kernel, out_shape, in_specs, out_specs, scratch):
    return pl.pallas_call(
        kernel,
        out_shape=out_shape,
        in_specs=in_specs,
        out_specs=out_specs,
        scratch_shapes=scratch,
        name=kernel.__name__,
        compiler_params=PARAMS,
    )


def shards(image_field, weights, measured, dual_field):
    forward, inverse, twiddle, place = host_tables()
    scale = 1.0 / GRID
    place = jnp.asarray(place, jnp.bfloat16)
    twiddle = jnp.asarray(twiddle)
    image = image_field[0]
    f32, bf16 = jnp.float32, jnp.bfloat16
    chan = lax.axis_index("chan")
    where = jnp.stack([chan // 2, chan % 2]).astype(jnp.int32)

    last_row, last_column = call(
        dual_edges,
        (shape((CHANNELS, 2 * LANES)), shape((CHANNELS, LANES))),
        [VM],
        (VM, VM),
        [],
    )(dual_field)
    above = passed_along(last_row, "facet", 1)
    left = passed_along(last_column, "chan", 1)

    spread, *pieces = call(
        rows_forward,
        (shape((RADIX, 2, RADIX, 8, LANES)),) + (shape((LANES, 512)),) * 4,
        [SM, HBM, HBM, HBM],
        (HBM,) * 5,
        [
            pltpu.VMEM((LANES, GRID), f32),
            pltpu.VMEM((2, RADIX, LANES), f32),
            pltpu.VMEM((256, 768), bf16),
            pltpu.VMEM((RADIX, 2, RADIX, 8, LANES), f32),
            pltpu.VMEM((GRID, 512), bf16),
            DMA((10,)),
            DMA((12,)),
        ],
    )(where, image, twiddle, jnp.asarray(halves(forward * scale).T))
    for k in range(1, 4):
        pairs = [(2 * x + z, (x + k) % 4 * 2 + z) for x in range(4) for z in range(2)]
        pieces[k] = lax.ppermute(pieces[k], "chan", pairs)
    cols = lax.all_to_all(
        spread.reshape(RADIX, 2 * LANES, LANES), "facet", split_axis=0, concat_axis=0, tiled=True
    )
    data = call(
        data_prepared,
        shape((3, RADIX, LANES, LANES), bf16),
        [VM] * 3,
        HBM,
        [pltpu.VMEM((GRID, LANES), f32), pltpu.VMEM((3, RADIX, LANES, LANES), bf16), DMA((3,))],
    )(weights[0], measured[0], place)
    to_swap = call(
        swap_ready, shape((4, LANES, 256)), [SM] + [HBM] * 4, HBM, [DMA((4,))]
    )(where, *pieces)
    cols, to_swap, above, left, data = lax.optimization_barrier(
        (cols, to_swap, above, left, data)
    )
    swapped = lax.ppermute(to_swap, "chan", [(i, i ^ 1) for i in range(8)])
    back = call(
        columns,
        shape((RADIX, 2 * LANES + 8, LANES)),
        [HBM, HBM, VM, HBM, HBM],
        HBM,
        [
            pltpu.VMEM((RADIX, 2, LANES, LANES), f32),
            pltpu.VMEM((3, RADIX, LANES, LANES), bf16),
            pltpu.VMEM((768, 256), bf16),
            pltpu.VMEM((768, 256), bf16),
            pltpu.VMEM((RADIX, 2, LANES, LANES), f32),
            pltpu.VMEM((RADIX, 8, LANES), f32),
            pltpu.VMEM((RADIX * 32, 512), bf16),
            DMA((6,)),
            DMA((4,)),
            DMA((4, 2)),
        ],
    )(
        cols.reshape(RADIX, 2, LANES, LANES),
        data,
        twiddle,
        jnp.asarray(halves(forward)),
        jnp.asarray(halves(inverse)),
    )
    lines = lax.all_to_all(back, "facet", split_axis=0, concat_axis=0, tiled=True)
    for_image, for_ahead, first_row, first_column = call(
        tile_ready,
        (
            shape((CHANNELS, LANES, 2 * LANES)),
            shape((CHANNELS, LANES, 2 * LANES)),
            shape((CHANNELS, 2 * LANES)),
            shape((CHANNELS, LANES)),
        ),
        [SM] + [VM] * 8,
        (VM,) * 4,
        [],
    )(where, *pieces, swapped, dual_field, above, left)
    below = passed_along(first_row, "facet", -1)
    right = passed_along(first_column, "chan", -1)
    lines, for_image, for_ahead, below, right = lax.optimization_barrier(
        (lines, for_image, for_ahead, below, right)
    )
    slopes = call(
        rows_back,
        shape((CHANNELS, LANES + 8, 2 * LANES)),
        [ANY, VM, HBM],
        ANY,
        [
            pltpu.VMEM((RADIX, 2 * LANES, LANES), f32),
            pltpu.VMEM((RADIX, 8, LANES), f32),
            pltpu.VMEM((768, 256), bf16),
            pltpu.VMEM((RADIX, LANES, 256), f32),
            pltpu.VMEM((CHANNELS, LANES + 8, 2 * LANES), f32),
            pltpu.VMEM((LANES, LANES), f32),
            DMA((6,)),
            DMA((8,)),
        ],
    )(lines, twiddle, jnp.asarray(halves(inverse * scale)))
    gradient = lax.all_to_all(slopes, "chan", split_axis=0, concat_axis=0, tiled=True)
    return call(
        finish,
        (shape((CHANNELS, LANES, 2 * LANES)), shape((CHANNELS, 2, LANES, 2 * LANES), bf16)),
        [VM] * 6,
        (ANY, ANY),
        [
            pltpu.VMEM((CHANNELS, LANES + 8, 2 * LANES), f32),
            pltpu.VMEM((LANES, LANES), f32),
            pltpu.VMEM((CHANNELS, LANES, 2 * LANES), f32),
            pltpu.VMEM((CHANNELS, 2, LANES, 2 * LANES), bf16),
            DMA((8,)),
            DMA((8,)),
        ],
    )(gradient, for_image, for_ahead, dual_field, below, right)


def solution(mesh):
    placed = (
        P("chan", "facet", None),
        P("chan", None, "facet"),
        P("chan", None, None, "facet"),
        P(None, None, "facet", "chan"),
    )
    return jax.shard_map(
        shards,
        mesh=mesh,
        in_specs=placed,
        out_specs=(P(None, "facet", "chan"), P(None, None, "facet", "chan")),
        check_vma=False,
    )
```

```python
from functools import partial
import math

import jax
import jax.numpy as jnp
import ml_dtypes
import numpy as np
from jax import lax
from jax.experimental import pallas as pl
from jax.experimental.pallas import tpu as pltpu
from jax.sharding import PartitionSpec as P

GRID = 2048
RADIX = 16
LANES = 128
CHANNELS = 8

step_primal = 0.5
step_dual = 0.5
clip_radius = 4.0

PARAMS = pltpu.CompilerParams(vmem_limit_bytes=63 * 1024 * 1024)


def host_tables():
    index = np.arange(LANES)
    angle = 2.0 * np.pi * (index[:, None] * index[None, :] % LANES) / LANES
    cos, sin = np.cos(angle), np.sin(angle)
    forward = np.block([[cos, -sin], [sin, cos]])
    inverse = np.block([[cos, sin], [-sin, cos]])
    turn = 2.0 * np.pi * np.arange(RADIX)[:, None] * index[None, :] / GRID
    twiddle = np.stack([np.cos(turn), np.sin(turn)]).astype(np.float32)
    place = np.zeros((LANES, LANES))
    for at in range(LANES):
        place[at, 16 * (at % 8) + at // 8] = 1.0
    return forward, inverse, twiddle, place


def halves(table):
    high = table.astype(ml_dtypes.bfloat16)
    low = (table - high.astype(np.float64)).astype(ml_dtypes.bfloat16)
    return np.concatenate([high, high, low], axis=0)


def c_add(a, b):
    return (a[0] + b[0], b[1] if a[1] is None else a[1] if b[1] is None else a[1] + b[1])


def c_sub(a, b):
    imag = None
    if a[1] is not None and b[1] is not None:
        imag = a[1] - b[1]
    elif a[1] is not None:
        imag = a[1]
    elif b[1] is not None:
        imag = -b[1]
    return (a[0] - b[0], imag)


def add_turned(a, b, sign):
    real = a[0] if b[1] is None else (a[0] - b[1] if sign > 0 else a[0] + b[1])
    if a[1] is None:
        imag = b[0] if sign > 0 else -b[0]
    else:
        imag = a[1] + b[0] if sign > 0 else a[1] - b[0]
    return (real, imag)


def four(a, b, c, d, sign):
    sum_even, diff_even = c_add(a, c), c_sub(a, c)
    sum_odd, diff_odd = c_add(b, d), c_sub(b, d)
    return (
        c_add(sum_even, sum_odd),
        add_turned(diff_even, diff_odd, sign),
        c_sub(sum_even, sum_odd),
        add_turned(diff_even, diff_odd, -sign),
    )


def turned(a, power, sign):
    power = power % 16
    if power == 0:
        return a
    cos, sin = math.cos(2 * math.pi * power / 16), sign * math.sin(2 * math.pi * power / 16)
    real, imag = a
    if imag is None:
        if power == 4:
            return (jnp.zeros_like(real), real if sign > 0 else -real)
        return (real * cos, real * sin)
    if power == 4:
        return (-imag, real) if sign > 0 else (imag, -real)
    if abs(abs(cos) - abs(sin)) < 1e-9:
        root = math.sqrt(0.5)
        cs, ss = (1 if cos > 0 else -1), (1 if sin > 0 else -1)
        new_real = (real if cs > 0 else -real) - (imag if ss > 0 else -imag)
        new_imag = (real if ss > 0 else -real) + (imag if cs > 0 else -imag)
        return (new_real * root, new_imag * root)
    return (real * cos - imag * sin, real * sin + imag * cos)


def sixteen(values, sign):
    inner = [four(*(values[n0 + 4 * n1] for n1 in range(4)), sign) for n0 in range(4)]
    out = [None] * 16
    for k1 in range(4):
        parts = [turned(inner[n0][k1], n0 * k1, sign) for n0 in range(4)]
        for k2, value in enumerate(four(*parts, sign)):
            out[k1 + 4 * k2] = value
    return out


def split(value):
    high = value.astype(jnp.bfloat16)
    low = (value - high.astype(jnp.float32)).astype(jnp.bfloat16)
    return high, low


def dot(a, b, dims):
    return lax.dot_general(a, b, (dims, ((), ())), preferred_element_type=jnp.float32)


def fetched(source, target, semaphore):
    copy = pltpu.make_async_copy(source, target, semaphore)
    copy.start()
    return copy


def three_pass(pair, table, dims):
    high = pair[:, :256] if dims[0][0] == 1 else pair[:256, :]
    return dot(pair, table[:512, :], dims) + dot(high, table[512:, :], dims)


def store_pair(held, rows, real, imag):
    high_r, low_r = split(real)
    high_i, low_i = split(imag)
    held[rows, 0:LANES] = high_r
    held[rows, LANES : 2 * LANES] = high_i
    held[rows, 2 * LANES : 3 * LANES] = low_r
    held[rows, 3 * LANES : 4 * LANES] = low_i


def rows_forward(
    where, image, twiddle, table, out, *rest
):
    pieces, (image_v, twiddle_v, table_v, out_v, held, in_sems, out_sems) = rest[:4], rest[4:]
    chunk = 16
    steps = LANES // chunk

    def incoming(step):
        rows = pl.ds(pl.multiple_of(step * chunk, chunk), chunk)
        return pltpu.make_async_copy(image.at[rows, :], image_v.at[rows, :], in_sems.at[step])

    for step in range(steps):
        incoming(step).start()
    get_twiddle = fetched(twiddle, twiddle_v, in_sems.at[steps])
    get_table = fetched(table, table_v, in_sems.at[steps + 1])
    sent = []
    for k in range(4):
        lanes = pl.ds(pl.multiple_of((where[0] + k) % 4 * 512, 512), 512)
        sent.append(fetched(image.at[:, lanes], pieces[k], out_sems.at[8 + k]))
    get_twiddle.wait()

    def body(step, carry):
        incoming(step).wait()
        at = pl.multiple_of(step * chunk, chunk)
        values = [
            (image_v[pl.ds(at, chunk), b * LANES : (b + 1) * LANES], None) for b in range(RADIX)
        ]
        mixed = sixteen(values, -1)
        for f in range(RADIX):
            real, imag = mixed[f]
            if imag is None:
                imag = jnp.zeros_like(real)
            cos, sin = twiddle_v[0, f : f + 1, :], twiddle_v[1, f : f + 1, :]
            store_pair(
                held,
                pl.ds(f * LANES + at, chunk),
                real * cos + imag * sin,
                imag * cos - real * sin,
            )
        return carry

    lax.fori_loop(0, steps, body, 0)
    get_table.wait()
    dims = ((1,), (1,))
    for g in range(RADIX // 2):
        pair = held[256 * g : 256 * g + 256, :]
        result = dot(table_v[:, :512], pair, dims) + dot(table_v[:, 512:], pair[:, :256], dims)
        for h in range(2):
            for c in range(2):
                block = result[c * LANES : (c + 1) * LANES, h * LANES : (h + 1) * LANES]
                out_v[:, c, 2 * g + h] = block.reshape(RADIX, 8, LANES)
        both = pl.ds(2 * g, 2)
        sent.append(fetched(out_v.at[:, :, both], out.at[:, :, both], out_sems.at[g]))
    for copy in sent:
        copy.wait()


def data_prepared(weights, measured, place, out, held, out_v, sems):
    copies = []
    for n in range(3):
        source = weights[...] if n == 0 else measured[n - 1]
        held[...] = source.astype(jnp.float32)
        for f in range(RADIX):
            rows = held[pl.ds(f, LANES, stride=RADIX), :].astype(jnp.bfloat16)
            out_v[n, f] = dot(place[...], rows, ((1,), (1,))).astype(jnp.bfloat16)
        copies.append(fetched(out_v.at[n], out.at[n], sems.at[n]))
    for copy in copies:
        copy.wait()


def columns(
    cols, data, twiddle, forward, inverse, out,
    cols_v, data_v, forward_v, inverse_v, out_v, edge_v, held, in_sems, data_sems, out_sems,
):
    chunk = 32
    steps = LANES // chunk
    dims = ((1,), (0,))

    def incoming(step):
        rows = pl.ds(pl.multiple_of(step * chunk, chunk), chunk)
        return pltpu.make_async_copy(
            cols.at[:, :, rows, :], cols_v.at[:, :, rows, :], in_sems.at[step]
        )

    def incoming_data(step):
        rows = pl.ds(pl.multiple_of(step * chunk, chunk), chunk)
        return pltpu.make_async_copy(
            data.at[:, :, rows, :], data_v.at[:, :, rows, :], data_sems.at[step]
        )

    def outgoing(step, c):
        rows = pl.ds(pl.multiple_of(step * chunk, chunk), chunk)
        to_rows = pl.ds(pl.multiple_of(c * LANES + step * chunk, chunk), chunk)
        return pltpu.make_async_copy(
            out_v.at[:, c, rows, :], out.at[:, to_rows, :], out_sems.at[step, c]
        )

    for step in range(steps):
        incoming(step).start()
        incoming_data(step).start()
    get_forward = fetched(forward, forward_v, in_sems.at[steps])
    get_inverse = fetched(inverse, inverse_v, in_sems.at[steps + 1])
    edge_v[...] = jnp.zeros_like(edge_v)
    get_forward.wait()
    get_inverse.wait()
    lane_at = lax.broadcasted_iota(jnp.int32, (8, LANES), 1)

    def body(step, carry):
        incoming(step).wait()
        here = pl.ds(pl.multiple_of(step * chunk, chunk), chunk)
        mixed = sixteen([(cols_v[b, 0, here, :], cols_v[b, 1, here, :]) for b in range(RADIX)], -1)
        for f in range(RADIX):
            real, imag = mixed[f]
            cos, sin = twiddle[0, f : f + 1, :], twiddle[1, f : f + 1, :]
            rows = slice(f * chunk, (f + 1) * chunk)
            store_pair(held, rows, real * cos + imag * sin, imag * cos - real * sin)
        incoming_data(step).wait()
        spectrum = three_pass(held[...], forward_v, dims)
        for f in range(RADIX):
            rows = slice(f * chunk, (f + 1) * chunk)
            weight = data_v[0, f, here, :].astype(jnp.float32)
            real = weight * spectrum[rows, :LANES] - data_v[1, f, here, :].astype(jnp.float32)
            imag = weight * spectrum[rows, LANES:] - data_v[2, f, here, :].astype(jnp.float32)
            store_pair(held, rows, real, imag)
        back = three_pass(held[...], inverse_v, dims)
        values = []
        for f in range(RADIX):
            rows = slice(f * chunk, (f + 1) * chunk)
            real, imag = back[rows, :LANES], back[rows, LANES:]
            cos, sin = twiddle[0, f : f + 1, :], twiddle[1, f : f + 1, :]
            values.append((real * cos - imag * sin, imag * cos + real * sin))
        mixed = sixteen(values, 1)
        for b in range(RADIX):
            for c in range(2):
                out_v[b, c, here, :] = mixed[b][c]
                if b > 0:
                    edge = edge_v[b - 1]
                    for i in range(chunk // 8):
                        first = mixed[b][c][8 * i : 8 * i + 8, 0:1]
                        at_lane = lane_at == c * RADIX + step * (chunk // 8) + i
                        edge = jnp.where(at_lane, first, edge)
                    edge_v[b - 1] = edge
        outgoing(step, 0).start()
        outgoing(step, 1).start()
        return carry

    lax.fori_loop(0, steps, body, 0)
    send_edge = fetched(edge_v, out.at[:, 2 * LANES :, :], in_sems.at[0])
    for step in range(steps):
        outgoing(step, 0).wait()
        outgoing(step, 1).wait()
    send_edge.wait()


def rows_back(
    lines, twiddle, table, out, lines_v, edge_v, table_v, held, out_v, side_v, in_sems, out_sems
):
    dims = ((0,), (0,))
    get_table = fetched(table, table_v, in_sems.at[5])
    arriving = []
    for g in range(4):
        for c in range(2):
            rows = pl.ds(c * LANES + 32 * g, 32)
            arriving.append(
                fetched(
                    lines.at[:, rows, :], lines_v.at[:, pl.ds(c * LANES + 32 * g, 32), :],
                    out_sems.at[2 * g + c],
                )
            )
    get_edge = fetched(lines.at[:, 2 * LANES :, :], edge_v, in_sems.at[4])
    get_table.wait()
    for f in range(RADIX):
        if f % 4 == 0:
            arriving[f // 2].wait()
            arriving[f // 2 + 1].wait()
        real = lines_v[:, 8 * f : 8 * f + 8, :].reshape(LANES, LANES)
        imag = lines_v[:, LANES + 8 * f : LANES + 8 * f + 8, :].reshape(LANES, LANES)
        high_r, low_r = split(real)
        high_i, low_i = split(imag)
        pair = jnp.concatenate([high_r, high_i, low_r, low_i], axis=0)
        held[f] = three_pass(pair, table_v, dims)
    get_edge.wait()
    high, low = split(edge_v[...].reshape(LANES, LANES))
    edge = (
        dot(high, table_v[0:LANES, :], dims)
        + dot(low, table_v[0:LANES, :], dims)
        + dot(high, table_v[512 : 512 + LANES, :], dims)
    )
    edge_r = edge[:RADIX, :LANES] - edge[RADIX : 2 * RADIX, LANES:]
    edge_i = edge[:RADIX, LANES:] + edge[RADIX : 2 * RADIX, :LANES]
    cos, sin = twiddle[0], twiddle[1]
    edge_r, edge_i = edge_r * cos - edge_i * sin, edge_i * cos + edge_r * sin
    mixed = sixteen([(edge_r[f : f + 1], edge_i[f : f + 1]) for f in range(RADIX)], 1)
    for d in range(CHANNELS):
        out_v[d, LANES : LANES + 1, :] = jnp.concatenate(
            [mixed[2 * d][0], mixed[2 * d + 1][0]], axis=1
        )
    chunk = 16
    steps = LANES // chunk
    lane_at = lax.broadcasted_iota(jnp.int32, (chunk, LANES), 1)

    def outgoing(step):
        rows = pl.ds(pl.multiple_of(step * chunk, chunk), chunk)
        return pltpu.make_async_copy(out_v.at[:, rows, :], out.at[:, rows, :], out_sems.at[step])

    def body(step, carry):
        at = pl.multiple_of(step * chunk, chunk)
        here = pl.ds(at, chunk)
        values = []
        for f in range(RADIX):
            real, imag = held[f, here, :LANES], held[f, here, LANES:]
            cos, sin = twiddle[0, f : f + 1, :], twiddle[1, f : f + 1, :]
            values.append((real * cos - imag * sin, imag * cos + real * sin))
        mixed = sixteen(values, 1)
        side = jnp.zeros((chunk, LANES), jnp.float32)
        for b in range(RADIX):
            low_lane = (b % 2) * LANES
            out_v[b // 2, here, low_lane : low_lane + LANES] = mixed[b][0]
            if b > 0 and b % 2 == 0:
                side = jnp.where(lane_at == b // 2 - 1, mixed[b][0][:, 0:1], side)
        side_v[here, :] = side
        outgoing(step).start()
        return carry

    lax.fori_loop(0, steps, body, 0)
    beside = side_v[...].T
    for d in range(CHANNELS):
        out_v[d, LANES + 1 : LANES + 2, :LANES] = beside[d : d + 1, :]
    last = fetched(
        out_v.at[:, pl.ds(LANES, 8), :], out.at[:, pl.ds(LANES, 8), :], in_sems.at[4]
    )
    for step in range(steps):
        outgoing(step).wait()
    last.wait()


def dual_edges(dual, last_row, last_column):
    rows, cols = [], []
    for c in range(CHANNELS):
        rows.append(dual[c, 0, 112:128, :].astype(jnp.float32)[15:16, :])
        cols.append(dual[c, 1, :, LANES:].astype(jnp.float32)[:, LANES - 1 :])
    last_row[...] = jnp.concatenate(rows, axis=0)
    last_column[...] = jnp.concatenate(cols, axis=1).T


def swap_ready(where, *refs):
    pieces, out, sems = refs[:4], refs[4], refs[5]
    lanes = pl.ds(pl.multiple_of((1 - where[1]) * 256, 256), 256)
    copies = [fetched(pieces[k].at[:, lanes], out.at[k], sems.at[k]) for k in range(4)]
    for copy in copies:
        copy.wait()


def tile_ready(where, *refs):
    pieces, (swapped, dual, above, left) = refs[:4], refs[4:8]
    for_image, for_ahead, first_row, first_column = refs[8:]
    row_at = lax.broadcasted_iota(jnp.int32, (LANES, 2 * LANES), 0)
    lane_at = lax.broadcasted_iota(jnp.int32, (LANES, 2 * LANES), 1)
    for k in range(4):
        for other in range(2):
            lanes = where[1] * (1 - other) + (1 - where[1]) * other
            c = (where[0] + 4 - k) % 4 * 2 + lanes
            p = dual[c, 0].astype(jnp.float32)
            q = dual[c, 1].astype(jnp.float32)
            beside = jnp.broadcast_to(left[pl.ds(c, 1), :], (LANES, LANES)).T[:, 0:1]
            prev_p = jnp.where(row_at == 0, above[pl.ds(c, 1), :], pltpu.roll(p, 1, 0))
            prev_q = jnp.where(lane_at == 0, beside, pltpu.roll(q, 1, 1))
            adjoint = prev_p - p + prev_q - q
            if other:
                image = swapped[k]
            else:
                own = pl.ds(pl.multiple_of(where[1] * 256, 256), 256)
                image = pieces[k][:, own]
            ahead = image - adjoint
            for_image[c] = image - step_primal * adjoint
            for_ahead[c] = ahead
            first_row[pl.ds(c, 1), :] = ahead[0:1, :]
            first_column[pl.ds(c, 1), :] = ahead[:, :LANES].T[0:1, :]


def finish(
    gradient, for_image, for_ahead, dual, below, right, image_next, dual_next,
    gradient_v, base_v, dual_in, ahead_v, side_v, image_v, dual_v,
    in_sems, dual_in_sems, image_sems, dual_sems,
):
    arriving = []
    for c in range(CHANNELS):
        arriving.append(
            [
                fetched(gradient.at[c], gradient_v.at[c], in_sems.at[c, 0]),
                fetched(for_image.at[c], base_v.at[0, c], in_sems.at[c, 1]),
                fetched(for_ahead.at[c], base_v.at[1, c], in_sems.at[c, 2]),
            ]
        )
    arriving_dual = [
        fetched(dual.at[c], dual_in.at[c], dual_in_sems.at[c]) for c in range(CHANNELS)
    ]
    sides = []
    leaving = []
    for c in range(CHANNELS):
        for copy in arriving[c]:
            copy.wait()
        slope = gradient_v[c, :LANES, :]
        image_v[c] = base_v[0, c] - step_primal * slope
        leaving.append(fetched(image_v.at[c], image_next.at[c], image_sems.at[c]))
        ahead_v[c, :LANES, :] = base_v[1, c] - slope
        ahead_v[c, LANES : LANES + 1, :] = (
            below[c : c + 1, :] - gradient_v[c, LANES : LANES + 1, :]
        )
        sides.append(gradient_v[c, LANES + 1 : LANES + 2, :LANES])
    side_v[:, :CHANNELS] = (right[...] - jnp.concatenate(sides, axis=0)).T
    for copy in arriving_dual:
        copy.wait()
    chunk = 16
    steps = LANES // chunk
    row_at = lax.broadcasted_iota(jnp.int32, (chunk, 2 * LANES), 0)
    lane_at = lax.broadcasted_iota(jnp.int32, (chunk, 2 * LANES), 1)

    def outgoing(step):
        rows = pl.ds(pl.multiple_of(step * chunk, chunk), chunk)
        return pltpu.make_async_copy(
            dual_v.at[:, :, rows, :], dual_next.at[:, :, rows, :], dual_sems.at[step]
        )

    def body(step, carry):
        at = pl.multiple_of(step * chunk, chunk)
        here = pl.ds(at, chunk)
        after = pl.ds(pl.multiple_of(at + chunk, chunk), 8)
        firsts, seconds, total = [], [], None
        for c in range(CHANNELS):
            ahead = ahead_v[c, here, :]
            next_row = ahead_v[c, after, :][0:1, :]
            down = jnp.where(row_at == chunk - 1, next_row, pltpu.roll(ahead, chunk - 1, 0))
            beside = jnp.where(
                lane_at == 2 * LANES - 1,
                side_v[here, c : c + 1],
                pltpu.roll(ahead, 2 * LANES - 1, 1),
            )
            first = dual_in[c, 0, here, :].astype(jnp.float32) + step_dual * (down - ahead)
            second = dual_in[c, 1, here, :].astype(jnp.float32) + step_dual * (beside - ahead)
            firsts.append(first)
            seconds.append(second)
            squares = first * first + second * second
            total = squares if total is None else total + squares
        factor = 1.0 / jnp.maximum(1.0, jnp.sqrt(total) / clip_radius)
        for c in range(CHANNELS):
            dual_v[c, 0, here, :] = (firsts[c] * factor).astype(jnp.bfloat16)
            dual_v[c, 1, here, :] = (seconds[c] * factor).astype(jnp.bfloat16)
        outgoing(step).start()
        return carry

    lax.fori_loop(0, steps, body, 0)
    for copy in leaving:
        copy.wait()
    for step in range(steps):
        outgoing(step).wait()


def shape(dims, dtype=jnp.float32):
    return jax.ShapeDtypeStruct(dims, dtype)


def passed_along(x, axis, by):
    devices = lax.axis_size(axis)
    pairs = [(i, i + by) for i in range(devices) if 0 <= i + by < devices]
    return lax.ppermute(x, axis, pairs)


ANY = pl.BlockSpec(memory_space=pl.ANY)
HBM = pl.BlockSpec(memory_space=pltpu.HBM)
VM = pl.BlockSpec(memory_space=pltpu.VMEM)
SM = pl.BlockSpec(memory_space=pltpu.SMEM)
DMA = pltpu.SemaphoreType.DMA


def call(kernel, out_shape, in_specs, out_specs, scratch):
    return pl.pallas_call(
        kernel,
        out_shape=out_shape,
        in_specs=in_specs,
        out_specs=out_specs,
        scratch_shapes=scratch,
        name=kernel.__name__,
        compiler_params=PARAMS,
    )


def shards(image_field, weights, measured, dual_field):
    forward, inverse, twiddle, place = host_tables()
    scale = 1.0 / GRID
    place = jnp.asarray(place, jnp.bfloat16)
    twiddle = jnp.asarray(twiddle)
    image = image_field[0]
    f32, bf16 = jnp.float32, jnp.bfloat16
    chan = lax.axis_index("chan")
    where = jnp.stack([chan // 2, chan % 2]).astype(jnp.int32)

    last_row, last_column = call(
        dual_edges,
        (shape((CHANNELS, 2 * LANES)), shape((CHANNELS, LANES))),
        [VM],
        (VM, VM),
        [],
    )(dual_field)
    above = passed_along(last_row, "facet", 1)
    left = passed_along(last_column, "chan", 1)

    spread, *pieces = call(
        rows_forward,
        (shape((RADIX, 2, RADIX, 8, LANES)),) + (shape((LANES, 512)),) * 4,
        [SM, HBM, HBM, HBM],
        (HBM,) * 5,
        [
            pltpu.VMEM((LANES, GRID), f32),
            pltpu.VMEM((2, RADIX, LANES), f32),
            pltpu.VMEM((256, 768), bf16),
            pltpu.VMEM((RADIX, 2, RADIX, 8, LANES), f32),
            pltpu.VMEM((GRID, 512), bf16),
            DMA((10,)),
            DMA((12,)),
        ],
    )(where, image, twiddle, jnp.asarray(halves(forward * scale).T))
    for k in range(1, 4):
        pairs = [(2 * x + z, (x + k) % 4 * 2 + z) for x in range(4) for z in range(2)]
        pieces[k] = lax.ppermute(pieces[k], "chan", pairs)
    cols = lax.all_to_all(
        spread.reshape(RADIX, 2 * LANES, LANES), "facet", split_axis=0, concat_axis=0, tiled=True
    )
    data = call(
        data_prepared,
        shape((3, RADIX, LANES, LANES), bf16),
        [VM] * 3,
        HBM,
        [pltpu.VMEM((GRID, LANES), f32), pltpu.VMEM((3, RADIX, LANES, LANES), bf16), DMA((3,))],
    )(weights[0], measured[0], place)
    to_swap = call(
        swap_ready, shape((4, LANES, 256)), [SM] + [HBM] * 4, HBM, [DMA((4,))]
    )(where, *pieces)
    cols, above, left, data = lax.optimization_barrier((cols, above, left, data))
    swapped = lax.ppermute(to_swap, "chan", [(i, i ^ 1) for i in range(8)])
    back = call(
        columns,
        shape((RADIX, 2 * LANES + 8, LANES)),
        [HBM, HBM, VM, HBM, HBM],
        HBM,
        [
            pltpu.VMEM((RADIX, 2, LANES, LANES), f32),
            pltpu.VMEM((3, RADIX, LANES, LANES), bf16),
            pltpu.VMEM((768, 256), bf16),
            pltpu.VMEM((768, 256), bf16),
            pltpu.VMEM((RADIX, 2, LANES, LANES), f32),
            pltpu.VMEM((RADIX, 8, LANES), f32),
            pltpu.VMEM((RADIX * 32, 512), bf16),
            DMA((6,)),
            DMA((4,)),
            DMA((4, 2)),
        ],
    )(
        cols.reshape(RADIX, 2, LANES, LANES),
        data,
        twiddle,
        jnp.asarray(halves(forward)),
        jnp.asarray(halves(inverse)),
    )
    back, swapped = lax.optimization_barrier((back, swapped))
    lines = lax.all_to_all(back, "facet", split_axis=0, concat_axis=0, tiled=True)
    for_image, for_ahead, first_row, first_column = call(
        tile_ready,
        (
            shape((CHANNELS, LANES, 2 * LANES)),
            shape((CHANNELS, LANES, 2 * LANES)),
            shape((CHANNELS, 2 * LANES)),
            shape((CHANNELS, LANES)),
        ),
        [SM] + [VM] * 8,
        (VM,) * 4,
        [],
    )(where, *pieces, swapped, dual_field, above, left)
    below = passed_along(first_row, "facet", -1)
    right = passed_along(first_column, "chan", -1)
    lines, for_image, for_ahead, below, right = lax.optimization_barrier(
        (lines, for_image, for_ahead, below, right)
    )
    slopes = call(
        rows_back,
        shape((CHANNELS, LANES + 8, 2 * LANES)),
        [ANY, VM, HBM],
        ANY,
        [
            pltpu.VMEM((RADIX, 2 * LANES, LANES), f32),
            pltpu.VMEM((RADIX, 8, LANES), f32),
            pltpu.VMEM((768, 256), bf16),
            pltpu.VMEM((RADIX, LANES, 256), f32),
            pltpu.VMEM((CHANNELS, LANES + 8, 2 * LANES), f32),
            pltpu.VMEM((LANES, LANES), f32),
            DMA((6,)),
            DMA((8,)),
        ],
    )(lines, twiddle, jnp.asarray(halves(inverse * scale)))
    gradient = lax.all_to_all(slopes, "chan", split_axis=0, concat_axis=0, tiled=True)
    return call(
        finish,
        (shape((CHANNELS, LANES, 2 * LANES)), shape((CHANNELS, 2, LANES, 2 * LANES), bf16)),
        [HBM] * 4 + [VM] * 2,
        (HBM, HBM),
        [
            pltpu.VMEM((CHANNELS, LANES + 8, 2 * LANES), f32),
            pltpu.VMEM((2, CHANNELS, LANES, 2 * LANES), f32),
            pltpu.VMEM((CHANNELS, 2, LANES, 2 * LANES), bf16),
            pltpu.VMEM((CHANNELS, LANES + 8, 2 * LANES), f32),
            pltpu.VMEM((LANES, LANES), f32),
            pltpu.VMEM((CHANNELS, LANES, 2 * LANES), f32),
            pltpu.VMEM((CHANNELS, 2, LANES, 2 * LANES), bf16),
            DMA((8, 3)),
            DMA((8,)),
            DMA((8,)),
            DMA((8,)),
        ],
    )(gradient, for_image, for_ahead, dual_field, below, right)


def solution(mesh):
    placed = (
        P("chan", "facet", None),
        P("chan", None, "facet"),
        P("chan", None, None, "facet"),
        P(None, None, "facet", "chan"),
    )
    return jax.shard_map(
        shards,
        mesh=mesh,
        in_specs=placed,
        out_specs=(P(None, "facet", "chan"), P(None, None, "facet", "chan")),
        check_vma=False,
    )
```

```python
from functools import partial
import math

import jax
import jax.numpy as jnp
import ml_dtypes
import numpy as np
from jax import lax
from jax.experimental import pallas as pl
from jax.experimental.pallas import tpu as pltpu
from jax.sharding import PartitionSpec as P

GRID = 2048
RADIX = 16
LANES = 128
CHANNELS = 8

step_primal = 0.5
step_dual = 0.5
clip_radius = 4.0

MIB = 1024 * 1024


def host_tables():
    index = np.arange(LANES)
    angle = 2.0 * np.pi * (index[:, None] * index[None, :] % LANES) / LANES
    cos, sin = np.cos(angle), np.sin(angle)
    forward = np.block([[cos, -sin], [sin, cos]])
    inverse = np.block([[cos, sin], [-sin, cos]])
    turn = 2.0 * np.pi * np.arange(RADIX)[:, None] * index[None, :] / GRID
    twiddle = np.stack([np.cos(turn), np.sin(turn)]).astype(np.float32)
    place = np.zeros((LANES, LANES))
    for at in range(LANES):
        place[at, 16 * (at % 8) + at // 8] = 1.0
    return forward, inverse, twiddle, place


def halves(table):
    high = table.astype(ml_dtypes.bfloat16)
    low = (table - high.astype(np.float64)).astype(ml_dtypes.bfloat16)
    return np.concatenate([high, high, low], axis=0)


def c_add(a, b):
    return (a[0] + b[0], b[1] if a[1] is None else a[1] if b[1] is None else a[1] + b[1])


def c_sub(a, b):
    imag = None
    if a[1] is not None and b[1] is not None:
        imag = a[1] - b[1]
    elif a[1] is not None:
        imag = a[1]
    elif b[1] is not None:
        imag = -b[1]
    return (a[0] - b[0], imag)


def add_turned(a, b, sign):
    real = a[0] if b[1] is None else (a[0] - b[1] if sign > 0 else a[0] + b[1])
    if a[1] is None:
        imag = b[0] if sign > 0 else -b[0]
    else:
        imag = a[1] + b[0] if sign > 0 else a[1] - b[0]
    return (real, imag)


def four(a, b, c, d, sign):
    sum_even, diff_even = c_add(a, c), c_sub(a, c)
    sum_odd, diff_odd = c_add(b, d), c_sub(b, d)
    return (
        c_add(sum_even, sum_odd),
        add_turned(diff_even, diff_odd, sign),
        c_sub(sum_even, sum_odd),
        add_turned(diff_even, diff_odd, -sign),
    )


def turned(a, power, sign):
    power = power % 16
    if power == 0:
        return a
    cos, sin = math.cos(2 * math.pi * power / 16), sign * math.sin(2 * math.pi * power / 16)
    real, imag = a
    if imag is None:
        if power == 4:
            return (jnp.zeros_like(real), real if sign > 0 else -real)
        return (real * cos, real * sin)
    if power == 4:
        return (-imag, real) if sign > 0 else (imag, -real)
    if abs(abs(cos) - abs(sin)) < 1e-9:
        root = math.sqrt(0.5)
        cs, ss = (1 if cos > 0 else -1), (1 if sin > 0 else -1)
        new_real = (real if cs > 0 else -real) - (imag if ss > 0 else -imag)
        new_imag = (real if ss > 0 else -real) + (imag if cs > 0 else -imag)
        return (new_real * root, new_imag * root)
    return (real * cos - imag * sin, real * sin + imag * cos)


def sixteen(values, sign):
    inner = [four(*(values[n0 + 4 * n1] for n1 in range(4)), sign) for n0 in range(4)]
    out = [None] * 16
    for k1 in range(4):
        parts = [turned(inner[n0][k1], n0 * k1, sign) for n0 in range(4)]
        for k2, value in enumerate(four(*parts, sign)):
            out[k1 + 4 * k2] = value
    return out


def split(value):
    high = value.astype(jnp.bfloat16)
    low = (value - high.astype(jnp.float32)).astype(jnp.bfloat16)
    return high, low


def dot(a, b, dims):
    return lax.dot_general(a, b, (dims, ((), ())), preferred_element_type=jnp.float32)


def fetched(source, target, semaphore):
    copy = pltpu.make_async_copy(source, target, semaphore)
    copy.start()
    return copy


def three_pass(pair, table, dims):
    high = pair[:, :256] if dims[0][0] == 1 else pair[:256, :]
    return dot(pair, table[:512, :], dims) + dot(high, table[512:, :], dims)


def store_pair(held, rows, real, imag):
    high_r, low_r = split(real)
    high_i, low_i = split(imag)
    held[rows, 0:LANES] = high_r
    held[rows, LANES : 2 * LANES] = high_i
    held[rows, 2 * LANES : 3 * LANES] = low_r
    held[rows, 3 * LANES : 4 * LANES] = low_i


def rows_forward(
    where, image, twiddle, table, out, *rest
):
    pieces, (image_v, twiddle_v, table_v, out_v, held, in_sems, out_sems) = rest[:4], rest[4:]
    chunk = 16
    steps = LANES // chunk

    def incoming(step):
        rows = pl.ds(pl.multiple_of(step * chunk, chunk), chunk)
        return pltpu.make_async_copy(image.at[rows, :], image_v.at[rows, :], in_sems.at[step])

    for step in range(steps):
        incoming(step).start()
    get_twiddle = fetched(twiddle, twiddle_v, in_sems.at[steps])
    get_table = fetched(table, table_v, in_sems.at[steps + 1])
    sent = []
    get_twiddle.wait()

    def body(step, carry):
        incoming(step).wait()
        at = pl.multiple_of(step * chunk, chunk)
        values = [
            (image_v[pl.ds(at, chunk), b * LANES : (b + 1) * LANES], None) for b in range(RADIX)
        ]
        mixed = sixteen(values, -1)
        for f in range(RADIX):
            real, imag = mixed[f]
            if imag is None:
                imag = jnp.zeros_like(real)
            cos, sin = twiddle_v[0, f : f + 1, :], twiddle_v[1, f : f + 1, :]
            store_pair(
                held,
                pl.ds(f * LANES + at, chunk),
                real * cos + imag * sin,
                imag * cos - real * sin,
            )
        return carry

    lax.fori_loop(0, steps, body, 0)
    for k in range(4):
        lanes = pl.ds(pl.multiple_of((where[0] // 2 + k) % 4 * 512, 512), 512)
        sent.append(fetched(image_v.at[:, lanes], pieces[k], out_sems.at[8 + k]))
    get_table.wait()
    dims = ((1,), (1,))
    for g in range(RADIX // 2):
        pair = held[256 * g : 256 * g + 256, :]
        result = dot(table_v[:, :512], pair, dims) + dot(table_v[:, 512:], pair[:, :256], dims)
        for h in range(2):
            for c in range(2):
                block = result[c * LANES : (c + 1) * LANES, h * LANES : (h + 1) * LANES]
                out_v[:, c, 2 * g + h] = block.reshape(RADIX, 8, LANES)
        both = pl.ds(2 * g, 2)
        sent.append(fetched(out_v.at[:, :, both], out.at[:, :, both], out_sems.at[g]))
    for copy in sent:
        copy.wait()


def data_prepared(
    weights, measured, place, forward, inverse, twiddle,
    out, forward_kept, inverse_kept, twiddle_kept, held,
):
    forward_kept[...] = forward[...]
    inverse_kept[...] = inverse[...]
    twiddle_kept[...] = twiddle[...]
    for n in range(3):
        source = weights[...] if n == 0 else measured[n - 1]
        held[...] = source.astype(jnp.float32)
        for f in range(RADIX):
            rows = held[pl.ds(f, LANES, stride=RADIX), :].astype(jnp.bfloat16)
            out[n, f] = dot(place[...], rows, ((1,), (1,))).astype(jnp.bfloat16)


def columns(cols, data, twiddle, forward, inverse, out, held):
    chunk = 32
    steps = LANES // chunk
    dims = ((1,), (0,))
    out[:, 2 * LANES :, :] = jnp.zeros((RADIX, 8, LANES), jnp.float32)
    lane_at = lax.broadcasted_iota(jnp.int32, (8, LANES), 1)

    def body(step, carry):
        at = pl.multiple_of(step * chunk, chunk)
        here = pl.ds(at, chunk)
        imag_here = pl.ds(pl.multiple_of(LANES + at, chunk), chunk)
        mixed = sixteen([(cols[b, here, :], cols[b, imag_here, :]) for b in range(RADIX)], -1)
        for f in range(RADIX):
            real, imag = mixed[f]
            cos, sin = twiddle[0, f : f + 1, :], twiddle[1, f : f + 1, :]
            rows = slice(f * chunk, (f + 1) * chunk)
            store_pair(held, rows, real * cos + imag * sin, imag * cos - real * sin)
        spectrum = three_pass(held[...], forward, dims)
        for f in range(RADIX):
            rows = slice(f * chunk, (f + 1) * chunk)
            weight = data[0, f, here, :].astype(jnp.float32)
            real = weight * spectrum[rows, :LANES] - data[1, f, here, :].astype(jnp.float32)
            imag = weight * spectrum[rows, LANES:] - data[2, f, here, :].astype(jnp.float32)
            store_pair(held, rows, real, imag)
        back = three_pass(held[...], inverse, dims)
        values = []
        for f in range(RADIX):
            rows = slice(f * chunk, (f + 1) * chunk)
            real, imag = back[rows, :LANES], back[rows, LANES:]
            cos, sin = twiddle[0, f : f + 1, :], twiddle[1, f : f + 1, :]
            values.append((real * cos - imag * sin, imag * cos + real * sin))
        mixed = sixteen(values, 1)
        for b in range(RADIX):
            for c in range(2):
                out[b, (here, imag_here)[c], :] = mixed[b][c]
                if b > 0:
                    edge = out[b - 1, 2 * LANES :, :]
                    for i in range(chunk // 8):
                        first = mixed[b][c][8 * i : 8 * i + 8, 0:1]
                        at_lane = lane_at == c * RADIX + step * (chunk // 8) + i
                        edge = jnp.where(at_lane, first, edge)
                    out[b - 1, 2 * LANES :, :] = edge
        return carry

    lax.fori_loop(0, steps, body, 0)


def rows_back(lines, twiddle, table, out, held, side_v):
    dims = ((0,), (0,))
    for f in range(RADIX):
        real = lines[:, 8 * f : 8 * f + 8, :].reshape(LANES, LANES)
        imag = lines[:, LANES + 8 * f : LANES + 8 * f + 8, :].reshape(LANES, LANES)
        high_r, low_r = split(real)
        high_i, low_i = split(imag)
        pair = jnp.concatenate([high_r, high_i, low_r, low_i], axis=0)
        held[f] = three_pass(pair, table, dims)
    high, low = split(lines[:, 2 * LANES :, :].reshape(LANES, LANES))
    edge = (
        dot(high, table[0:LANES, :], dims)
        + dot(low, table[0:LANES, :], dims)
        + dot(high, table[512 : 512 + LANES, :], dims)
    )
    edge_r = edge[:RADIX, :LANES] - edge[RADIX : 2 * RADIX, LANES:]
    edge_i = edge[:RADIX, LANES:] + edge[RADIX : 2 * RADIX, :LANES]
    scale = 1.0 / GRID
    cos, sin = twiddle[0] * scale, twiddle[1] * scale
    edge_r, edge_i = edge_r * cos - edge_i * sin, edge_i * cos + edge_r * sin
    mixed = sixteen([(edge_r[f : f + 1], edge_i[f : f + 1]) for f in range(RADIX)], 1)
    for d in range(CHANNELS):
        out[d, LANES : LANES + 1, :] = jnp.concatenate(
            [mixed[2 * d][0], mixed[2 * d + 1][0]], axis=1
        )
    chunk = 16
    steps = LANES // chunk
    lane_at = lax.broadcasted_iota(jnp.int32, (chunk, LANES), 1)

    def body(step, carry):
        at = pl.multiple_of(step * chunk, chunk)
        here = pl.ds(at, chunk)
        values = []
        for f in range(RADIX):
            real, imag = held[f, here, :LANES], held[f, here, LANES:]
            cos, sin = twiddle[0, f : f + 1, :] * scale, twiddle[1, f : f + 1, :] * scale
            values.append((real * cos - imag * sin, imag * cos + real * sin))
        mixed = sixteen(values, 1)
        side = jnp.zeros((chunk, LANES), jnp.float32)
        for b in range(RADIX):
            low_lane = (b % 2) * LANES
            out[b // 2, here, low_lane : low_lane + LANES] = mixed[b][0]
            if b > 0 and b % 2 == 0:
                side = jnp.where(lane_at == b // 2 - 1, mixed[b][0][:, 0:1], side)
        side_v[here, :] = side
        return carry

    lax.fori_loop(0, steps, body, 0)
    beside = side_v[...].T
    for d in range(CHANNELS):
        out[d, LANES + 1 : LANES + 2, :LANES] = beside[d : d + 1, :]


def dual_edges(dual, last_row, last_column):
    rows, cols = [], []
    for c in range(CHANNELS):
        rows.append(dual[c, 0, 112:128, :].astype(jnp.float32)[15:16, :])
        cols.append(dual[c, 1, :, LANES:].astype(jnp.float32)[:, LANES - 1 :])
    last_row[...] = jnp.concatenate(rows, axis=0)
    last_column[...] = jnp.concatenate(cols, axis=1).T


def swap_ready(where, *refs):
    pieces, out = refs[:4], refs[4]
    lanes = pl.ds(pl.multiple_of((1 - where[0] % 2) * 256, 256), 256)
    for k in range(4):
        out[k] = pieces[k][:, lanes]


def tile_ready(where, *refs):
    pieces, (swapped, dual, above, left) = refs[:4], refs[4:8]
    for_image, for_ahead, first_row, first_column = refs[8:]
    row_at = lax.broadcasted_iota(jnp.int32, (LANES, 2 * LANES), 0)
    lane_at = lax.broadcasted_iota(jnp.int32, (LANES, 2 * LANES), 1)
    for k in range(4):
        for other in range(2):
            half = where[0] % 2
            c = (where[0] // 2 + 4 - k) % 4 * 2 + (1 - half if other else half)
            p = dual[c, 0].astype(jnp.float32)
            q = dual[c, 1].astype(jnp.float32)
            beside = jnp.broadcast_to(left[pl.ds(c, 1), :], (LANES, LANES)).T[:, 0:1]
            prev_p = jnp.where(row_at == 0, above[pl.ds(c, 1), :], pltpu.roll(p, 1, 0))
            prev_q = jnp.where(lane_at == 0, beside, pltpu.roll(q, 1, 1))
            adjoint = prev_p - p + prev_q - q
            if other:
                image = swapped[k]
            else:
                own = pl.ds(pl.multiple_of(half * 256, 256), 256)
                image = pieces[k][:, own]
            ahead = image - adjoint
            for_image[c] = image - step_primal * adjoint
            for_ahead[c] = ahead
            first_row[pl.ds(c, 1), :] = ahead[0:1, :]
            first_column[pl.ds(c, 1), :] = ahead[:, :LANES].T[0:1, :]


def finish(
    gradient, for_image, for_ahead, dual, below, right, image_next, dual_next,
    ahead_v, side_v, image_v, dual_v, image_sems, dual_sems,
):
    sides = []
    leaving = []
    for c in range(CHANNELS):
        slope = gradient[c, :LANES, :]
        image_v[c] = for_image[c] - step_primal * slope
        leaving.append(fetched(image_v.at[c], image_next.at[c], image_sems.at[c]))
        ahead_v[c, :LANES, :] = for_ahead[c] - slope
        ahead_v[c, LANES : LANES + 1, :] = (
            below[c : c + 1, :] - gradient[c, LANES : LANES + 1, :]
        )
        sides.append(gradient[c, LANES + 1 : LANES + 2, :LANES])
    side_v[:, :CHANNELS] = (right[...] - jnp.concatenate(sides, axis=0)).T
    chunk = 16
    steps = LANES // chunk
    row_at = lax.broadcasted_iota(jnp.int32, (chunk, 2 * LANES), 0)
    lane_at = lax.broadcasted_iota(jnp.int32, (chunk, 2 * LANES), 1)

    def outgoing(step):
        rows = pl.ds(pl.multiple_of(step * chunk, chunk), chunk)
        return pltpu.make_async_copy(
            dual_v.at[:, :, rows, :], dual_next.at[:, :, rows, :], dual_sems.at[step]
        )

    def body(step, carry):
        at = pl.multiple_of(step * chunk, chunk)
        here = pl.ds(at, chunk)
        after = pl.ds(pl.multiple_of(at + chunk, chunk), 8)
        firsts, seconds, total = [], [], None
        for c in range(CHANNELS):
            ahead = ahead_v[c, here, :]
            next_row = ahead_v[c, after, :][0:1, :]
            down = jnp.where(row_at == chunk - 1, next_row, pltpu.roll(ahead, chunk - 1, 0))
            beside = jnp.where(
                lane_at == 2 * LANES - 1,
                side_v[here, c : c + 1],
                pltpu.roll(ahead, 2 * LANES - 1, 1),
            )
            first = dual[c, 0, here, :].astype(jnp.float32) + step_dual * (down - ahead)
            second = dual[c, 1, here, :].astype(jnp.float32) + step_dual * (beside - ahead)
            firsts.append(first)
            seconds.append(second)
            squares = first * first + second * second
            total = squares if total is None else total + squares
        factor = 1.0 / jnp.maximum(1.0, jnp.sqrt(total) / clip_radius)
        for c in range(CHANNELS):
            dual_v[c, 0, here, :] = (firsts[c] * factor).astype(jnp.bfloat16)
            dual_v[c, 1, here, :] = (seconds[c] * factor).astype(jnp.bfloat16)
        outgoing(step).start()
        return carry

    lax.fori_loop(0, steps, body, 0)
    for copy in leaving:
        copy.wait()
    for step in range(steps):
        outgoing(step).wait()


def shape(dims, dtype=jnp.float32):
    return jax.ShapeDtypeStruct(dims, dtype)


def passed_along(x, axis, by):
    devices = lax.axis_size(axis)
    pairs = [(i, i + by) for i in range(devices) if 0 <= i + by < devices]
    return lax.ppermute(x, axis, pairs)


ANY = pl.BlockSpec(memory_space=pl.ANY)
HBM = pl.BlockSpec(memory_space=pltpu.HBM)
VM = pl.BlockSpec(memory_space=pltpu.VMEM)
SM = pl.BlockSpec(memory_space=pltpu.SMEM)
DMA = pltpu.SemaphoreType.DMA


def call(kernel, out_shape, in_specs, out_specs, scratch, limit=16):
    return pl.pallas_call(
        kernel,
        out_shape=out_shape,
        in_specs=in_specs,
        out_specs=out_specs,
        scratch_shapes=scratch,
        name=kernel.__name__,
        compiler_params=pltpu.CompilerParams(vmem_limit_bytes=limit * MIB),
    )


def shards(image_field, weights, measured, dual_field):
    forward, inverse, twiddle, place = host_tables()
    scale = 1.0 / GRID
    place = jnp.asarray(place, jnp.bfloat16)
    twiddle = jnp.asarray(twiddle)
    image = image_field[0]
    f32, bf16 = jnp.float32, jnp.bfloat16
    chan = lax.axis_index("chan")
    where = chan.astype(jnp.int32).reshape(1)

    last_row, last_column = call(
        dual_edges,
        (shape((CHANNELS, 2 * LANES)), shape((CHANNELS, LANES))),
        [VM],
        (VM, VM),
        [],
    )(dual_field)
    above = passed_along(last_row, "facet", 1)
    left = passed_along(last_column, "chan", 1)

    spread, *pieces = call(
        rows_forward,
        (shape((RADIX, 2, RADIX, 8, LANES)),) + (shape((LANES, 512)),) * 4,
        [SM, HBM, HBM, HBM],
        (HBM,) * 5,
        [
            pltpu.VMEM((LANES, GRID), f32),
            pltpu.VMEM((2, RADIX, LANES), f32),
            pltpu.VMEM((256, 768), bf16),
            pltpu.VMEM((RADIX, 2, RADIX, 8, LANES), f32),
            pltpu.VMEM((GRID, 512), bf16),
            DMA((10,)),
            DMA((12,)),
        ],
        63,
    )(where, image, twiddle, jnp.asarray(halves(forward * scale).T))
    for k in range(1, 4):
        pairs = [(2 * x + z, (x + k) % 4 * 2 + z) for x in range(4) for z in range(2)]
        pieces[k] = lax.ppermute(pieces[k], "chan", pairs)
    cols = lax.all_to_all(
        spread.reshape(RADIX, 2 * LANES, LANES), "facet", split_axis=0, concat_axis=0, tiled=True
    )
    data, forward_kept, inverse_kept, twiddle_kept = call(
        data_prepared,
        (
            shape((3, RADIX, LANES, LANES), bf16),
            shape((768, 256), bf16),
            shape((768, 256), bf16),
            shape((2, RADIX, LANES)),
        ),
        [VM] * 6,
        (VM,) * 4,
        [pltpu.VMEM((GRID, LANES), f32)],
    )(
        weights[0],
        measured[0],
        place,
        jnp.asarray(halves(forward)),
        jnp.asarray(halves(inverse)),
        twiddle,
    )
    to_swap = call(
        swap_ready, shape((4, LANES, 256)), [SM] + [VM] * 4, VM, []
    )(where, *pieces)
    cols, above, left = lax.optimization_barrier((cols, above, left))
    swapped = lax.ppermute(to_swap, "chan", [(i, i ^ 1) for i in range(8)])
    back = call(
        columns,
        shape((RADIX, 2 * LANES + 8, LANES)),
        [VM] * 5,
        VM,
        [pltpu.VMEM((RADIX * 32, 512), bf16)],
    )(
        cols,
        data,
        twiddle_kept,
        forward_kept,
        inverse_kept,
    )
    back, swapped = lax.optimization_barrier((back, swapped))
    lines = lax.all_to_all(back, "facet", split_axis=0, concat_axis=0, tiled=True)
    for_image, for_ahead, first_row, first_column = call(
        tile_ready,
        (
            shape((CHANNELS, LANES, 2 * LANES)),
            shape((CHANNELS, LANES, 2 * LANES)),
            shape((CHANNELS, 2 * LANES)),
            shape((CHANNELS, LANES)),
        ),
        [SM] + [VM] * 8,
        (VM,) * 4,
        [],
    )(where, *pieces, swapped, dual_field, above, left)
    below = passed_along(first_row, "facet", -1)
    right = passed_along(first_column, "chan", -1)
    lines, below, right = lax.optimization_barrier((lines, below, right))
    slopes = call(
        rows_back,
        shape((CHANNELS, LANES + 8, 2 * LANES)),
        [VM] * 3,
        VM,
        [pltpu.VMEM((RADIX, LANES, 256), f32), pltpu.VMEM((LANES, LANES), f32)],
    )(lines, twiddle_kept, inverse_kept)
    gradient = lax.all_to_all(slopes, "chan", split_axis=0, concat_axis=0, tiled=True)
    return call(
        finish,
        (shape((CHANNELS, LANES, 2 * LANES)), shape((CHANNELS, 2, LANES, 2 * LANES), bf16)),
        [VM] * 6,
        (HBM, HBM),
        [
            pltpu.VMEM((CHANNELS, LANES + 8, 2 * LANES), f32),
            pltpu.VMEM((LANES, LANES), f32),
            pltpu.VMEM((CHANNELS, LANES, 2 * LANES), f32),
            pltpu.VMEM((CHANNELS, 2, LANES, 2 * LANES), bf16),
            DMA((8,)),
            DMA((8,)),
        ],
    )(gradient, for_image, for_ahead, dual_field, below, right)


def solution(mesh):
    placed = (
        P("chan", "facet", None),
        P("chan", None, "facet"),
        P("chan", None, None, "facet"),
        P(None, None, "facet", "chan"),
    )
    return jax.shard_map(
        shards,
        mesh=mesh,
        in_specs=placed,
        out_specs=(P(None, "facet", "chan"), P(None, None, "facet", "chan")),
        check_vma=False,
    )
```

```python
from functools import partial
import math

import jax
import jax.numpy as jnp
import numpy as np
from jax import lax
from jax.experimental import pallas as pl
from jax.experimental.pallas import tpu as pltpu
from jax.sharding import PartitionSpec as P

GRID = 2048
RADIX = 16
LANES = 128
CHANNELS = 8

step_primal = 0.5
step_dual = 0.5
clip_radius = 4.0

MIB = 1024 * 1024


def host_tables():
    index = np.arange(LANES)
    turn = 2.0 * np.pi * np.arange(RADIX + 8)[:, None] * index[None, :] / GRID
    twiddle = np.stack([np.cos(turn), np.sin(turn)]).astype(np.float32)
    place = np.zeros((LANES, LANES))
    for at in range(LANES):
        place[at, 16 * (at % 8) + at // 8] = 1.0
    return twiddle, place


def c_add(a, b):
    return (a[0] + b[0], b[1] if a[1] is None else a[1] if b[1] is None else a[1] + b[1])


def c_sub(a, b):
    imag = None
    if a[1] is not None and b[1] is not None:
        imag = a[1] - b[1]
    elif a[1] is not None:
        imag = a[1]
    elif b[1] is not None:
        imag = -b[1]
    return (a[0] - b[0], imag)


def add_turned(a, b, sign):
    real = a[0] if b[1] is None else (a[0] - b[1] if sign > 0 else a[0] + b[1])
    if a[1] is None:
        imag = b[0] if sign > 0 else -b[0]
    else:
        imag = a[1] + b[0] if sign > 0 else a[1] - b[0]
    return (real, imag)


def four(a, b, c, d, sign):
    sum_even, diff_even = c_add(a, c), c_sub(a, c)
    sum_odd, diff_odd = c_add(b, d), c_sub(b, d)
    return (
        c_add(sum_even, sum_odd),
        add_turned(diff_even, diff_odd, sign),
        c_sub(sum_even, sum_odd),
        add_turned(diff_even, diff_odd, -sign),
    )


def turned(a, power, sign):
    power = power % 16
    if power == 0:
        return a
    cos, sin = math.cos(2 * math.pi * power / 16), sign * math.sin(2 * math.pi * power / 16)
    real, imag = a
    if imag is None:
        if power == 4:
            return (jnp.zeros_like(real), real if sign > 0 else -real)
        return (real * cos, real * sin)
    if power == 4:
        return (-imag, real) if sign > 0 else (imag, -real)
    if abs(abs(cos) - abs(sin)) < 1e-9:
        root = math.sqrt(0.5)
        cs, ss = (1 if cos > 0 else -1), (1 if sin > 0 else -1)
        new_real = (real if cs > 0 else -real) - (imag if ss > 0 else -imag)
        new_imag = (real if ss > 0 else -real) + (imag if cs > 0 else -imag)
        return (new_real * root, new_imag * root)
    return (real * cos - imag * sin, real * sin + imag * cos)


def sixteen(values, sign):
    inner = [four(*(values[n0 + 4 * n1] for n1 in range(4)), sign) for n0 in range(4)]
    out = [None] * 16
    for k1 in range(4):
        parts = [turned(inner[n0][k1], n0 * k1, sign) for n0 in range(4)]
        for k2, value in enumerate(four(*parts, sign)):
            out[k1 + 4 * k2] = value
    return out


def split(value):
    high = value.astype(jnp.bfloat16)
    low = (value - high.astype(jnp.float32)).astype(jnp.bfloat16)
    return high, low


def dot(a, b, dims):
    return lax.dot_general(a, b, (dims, ((), ())), preferred_element_type=jnp.float32)


def fetched(source, target, semaphore):
    copy = pltpu.make_async_copy(source, target, semaphore)
    copy.start()
    return copy


def fill_table(table, twiddle, sign, transposed):
    shape = (LANES, LANES)
    row, col = (lax.broadcasted_iota(jnp.int32, shape, n) for n in range(2))
    at = jnp.bitwise_and(row * col, LANES - 1)
    cos, sin = (
        jnp.take_along_axis(
            jnp.broadcast_to(twiddle[n, RADIX : RADIX + 1, :], shape), at, axis=1
        )
        for n in range(2)
    )
    for n, value in enumerate((cos, sign * sin, -sign * sin, cos)):
        high, low = split(value)
        into, out = ((n // 2, n % 2), (n % 2, n // 2))[transposed]
        for m, half in enumerate((high, high, low)):
            if transposed:
                lane = 256 * m + LANES * out
                table[LANES * into : LANES * into + LANES, lane : lane + LANES] = half
            else:
                at_row = 256 * m + LANES * into
                table[at_row : at_row + LANES, LANES * out : LANES * out + LANES] = half


def three_pass(pair, table, dims):
    high = pair[:, :256] if dims[0][0] == 1 else pair[:256, :]
    return dot(pair, table[:512, :], dims) + dot(high, table[512:, :], dims)


def store_pair(held, rows, real, imag):
    high_r, low_r = split(real)
    high_i, low_i = split(imag)
    held[rows, 0:LANES] = high_r
    held[rows, LANES : 2 * LANES] = high_i
    held[rows, 2 * LANES : 3 * LANES] = low_r
    held[rows, 3 * LANES : 4 * LANES] = low_i


def cross_ready(where, image, *pieces):
    for k in range(4):
        to = (where[0] // 2 + k) % 4
        pieces[k][...] = image[:, pl.ds(pl.multiple_of(to * 512, 512), 512)]


def swap_ready(where, *refs):
    pieces, early, late = refs[:4], refs[4], refs[5]
    lanes = pl.ds(pl.multiple_of((1 - where[0] % 2) * 256, 256), 256)
    for k in range(4):
        early[k] = pieces[k][: LANES // 2, lanes]
        late[k] = pieces[k][LANES // 2 :, lanes]


def rows_forward(
    image_in, twiddle_in, out, image, twiddle, out_v, held, table, in_sems, sems
):
    chunk = 16
    steps = LANES // chunk

    def incoming(step):
        rows = pl.ds(pl.multiple_of(step * chunk, chunk), chunk)
        return pltpu.make_async_copy(image_in.at[rows, :], image.at[rows, :], in_sems.at[step])

    get_twiddle = fetched(twiddle_in, twiddle, in_sems.at[steps])
    for step in range(steps):
        incoming(step).start()
    get_twiddle.wait()
    fill_table(table, twiddle, -1, True)

    def body(step, carry):
        incoming(step).wait()
        at = pl.multiple_of(step * chunk, chunk)
        values = [
            (image[pl.ds(at, chunk), b * LANES : (b + 1) * LANES], None) for b in range(RADIX)
        ]
        mixed = sixteen(values, -1)
        for f in range(RADIX):
            real, imag = mixed[f]
            if imag is None:
                imag = jnp.zeros_like(real)
            cos = twiddle[0, f : f + 1, :] * (1.0 / GRID)
            sin = twiddle[1, f : f + 1, :] * (1.0 / GRID)
            store_pair(
                held,
                pl.ds(f * LANES + at, chunk),
                real * cos + imag * sin,
                imag * cos - real * sin,
            )
        return carry

    lax.fori_loop(0, steps, body, 0)
    dims = ((1,), (1,))
    sent = []
    for g in range(RADIX // 2):
        pair = held[256 * g : 256 * g + 256, :]
        result = dot(table[:, :512], pair, dims) + dot(table[:, 512:], pair[:, :256], dims)
        for h in range(2):
            for c in range(2):
                block = result[c * LANES : (c + 1) * LANES, h * LANES : (h + 1) * LANES]
                out_v[:, c, 2 * g + h] = block.reshape(RADIX, 8, LANES)
        both = pl.ds(2 * g, 2)
        sent.append(fetched(out_v.at[:, :, both], out.at[:, :, both], sems.at[g]))
    for copy in sent:
        copy.wait()


def data_prepared(weights, measured, place, twiddle, out, forward, inverse, held):
    fill_table(forward, twiddle, -1, False)
    fill_table(inverse, twiddle, 1, False)
    for n in range(3):
        source = weights[...] if n == 0 else measured[n - 1]
        held[...] = source.astype(jnp.float32)
        for f in range(RADIX):
            rows = held[pl.ds(f, LANES, stride=RADIX), :].astype(jnp.bfloat16)
            out[n, f] = dot(place[...], rows, ((1,), (1,))).astype(jnp.bfloat16)


def columns(
    cols, data_in, twiddle, forward_in, inverse_in, out_all,
    data, forward, inverse, out, held, turned_v, in_sems, out_sems,
):
    chunk = 16
    steps = LANES // chunk
    dims = ((1,), (0,))
    many = 4
    get_forward = fetched(forward_in, forward, in_sems.at[4])
    get_inverse = fetched(inverse_in, inverse, in_sems.at[5])
    get_data = []
    for g in range(RADIX // many):
        part = pl.ds(g * many, many)
        get_data.append(fetched(data_in.at[:, part], data.at[:, part], in_sems.at[g]))
    out[:, 2 * LANES :, :] = jnp.zeros((RADIX, 8, LANES), jnp.float32)
    lane_at = lax.broadcasted_iota(jnp.int32, (8, LANES), 1)

    def first(step, carry):
        at = pl.multiple_of(step * chunk, chunk)
        imag_at = pl.ds(pl.multiple_of(LANES + at, chunk), chunk)
        mixed = sixteen([(cols[b, pl.ds(at, chunk), :], cols[b, imag_at, :]) for b in range(RADIX)], -1)
        for f in range(RADIX):
            real, imag = mixed[f]
            cos, sin = twiddle[0, f : f + 1, :], twiddle[1, f : f + 1, :]
            rows = pl.ds(f * LANES + at, chunk)
            store_pair(held, rows, real * cos + imag * sin, imag * cos - real * sin)
        return carry

    lax.fori_loop(0, steps, first, 0)
    get_forward.wait()
    get_inverse.wait()
    for g in range(RADIX // many):
        get_data[g].wait()
        block = slice(g * many * LANES, (g + 1) * many * LANES)
        spectrum = three_pass(held[block, :], forward, dims)
        for i in range(many):
            f = g * many + i
            rows = slice(i * LANES, (i + 1) * LANES)
            weight = data[0, f].astype(jnp.float32)
            real = weight * spectrum[rows, :LANES] - data[1, f].astype(jnp.float32)
            imag = weight * spectrum[rows, LANES:] - data[2, f].astype(jnp.float32)
            store_pair(held, slice(f * LANES, (f + 1) * LANES), real, imag)
        turned_v[block, :] = three_pass(held[block, :], inverse, dims)

    def last(step, carry):
        at = pl.multiple_of(step * chunk, chunk)
        places = pl.ds(at, chunk), pl.ds(pl.multiple_of(LANES + at, chunk), chunk)
        values = []
        for f in range(RADIX):
            rows = pl.ds(f * LANES + at, chunk)
            real, imag = turned_v[rows, :LANES], turned_v[rows, LANES:]
            cos, sin = twiddle[0, f : f + 1, :], twiddle[1, f : f + 1, :]
            values.append((real * cos - imag * sin, imag * cos + real * sin))
        mixed = sixteen(values, 1)
        for b in range(RADIX):
            for c in range(2):
                out[b, places[c], :] = mixed[b][c]
                if b > 0:
                    edge = out[b - 1, 2 * LANES :, :]
                    for i in range(chunk // 8):
                        one = mixed[b][c][8 * i : 8 * i + 8, 0:1]
                        at_lane = lane_at == c * RADIX + step * (chunk // 8) + i
                        edge = jnp.where(at_lane, one, edge)
                    out[b - 1, 2 * LANES :, :] = edge
        for c in range(2):
            outgoing(step, c).start()
        return carry

    def outgoing(step, c):
        rows = pl.ds(pl.multiple_of(c * LANES + step * chunk, chunk), chunk)
        return pltpu.make_async_copy(
            out.at[:, rows, :], out_all.at[:, rows, :], out_sems.at[step, c]
        )

    lax.fori_loop(0, steps, last, 0)
    rows = pl.ds(2 * LANES, 8)
    edges = fetched(out.at[:, rows, :], out_all.at[:, rows, :], in_sems.at[0])
    for step in range(steps):
        for c in range(2):
            outgoing(step, c).wait()
    edges.wait()


def rows_back(lines, twiddle, out, held, side_v, table):
    fill_table(table, twiddle, 1, False)
    dims = ((0,), (0,))
    for f in range(RADIX):
        real = lines[:, 8 * f : 8 * f + 8, :].reshape(LANES, LANES)
        imag = lines[:, LANES + 8 * f : LANES + 8 * f + 8, :].reshape(LANES, LANES)
        high_r, low_r = split(real)
        high_i, low_i = split(imag)
        pair = jnp.concatenate([high_r, high_i, low_r, low_i], axis=0)
        held[f] = three_pass(pair, table, dims)
    high, low = split(lines[:, 2 * LANES :, :].reshape(LANES, LANES))
    edge = (
        dot(high, table[0:LANES, :], dims)
        + dot(low, table[0:LANES, :], dims)
        + dot(high, table[512 : 512 + LANES, :], dims)
    )
    edge_r = edge[:RADIX, :LANES] - edge[RADIX : 2 * RADIX, LANES:]
    edge_i = edge[:RADIX, LANES:] + edge[RADIX : 2 * RADIX, :LANES]
    scale = 1.0 / GRID
    cos, sin = twiddle[0, :RADIX] * scale, twiddle[1, :RADIX] * scale
    edge_r, edge_i = edge_r * cos - edge_i * sin, edge_i * cos + edge_r * sin
    mixed = sixteen([(edge_r[f : f + 1], edge_i[f : f + 1]) for f in range(RADIX)], 1)
    for d in range(CHANNELS):
        out[d, LANES : LANES + 1, :] = jnp.concatenate(
            [mixed[2 * d][0], mixed[2 * d + 1][0]], axis=1
        )
    chunk = 16
    steps = LANES // chunk
    lane_at = lax.broadcasted_iota(jnp.int32, (chunk, LANES), 1)

    def body(step, carry):
        at = pl.multiple_of(step * chunk, chunk)
        here = pl.ds(at, chunk)
        values = []
        for f in range(RADIX):
            real, imag = held[f, here, :LANES], held[f, here, LANES:]
            cos, sin = twiddle[0, f : f + 1, :] * scale, twiddle[1, f : f + 1, :] * scale
            values.append((real * cos - imag * sin, imag * cos + real * sin))
        mixed = sixteen(values, 1)
        side = jnp.zeros((chunk, LANES), jnp.float32)
        for b in range(RADIX):
            low_lane = (b % 2) * LANES
            out[b // 2, here, low_lane : low_lane + LANES] = mixed[b][0]
            if b > 0 and b % 2 == 0:
                side = jnp.where(lane_at == b // 2 - 1, mixed[b][0][:, 0:1], side)
        side_v[here, :] = side
        return carry

    lax.fori_loop(0, steps, body, 0)
    beside = side_v[...].T
    for d in range(CHANNELS):
        out[d, LANES + 1 : LANES + 2, :LANES] = beside[d : d + 1, :]


def dual_edges(dual, last_row, last_column):
    rows, cols = [], []
    for c in range(CHANNELS):
        rows.append(dual[c, 0, 112:128, :].astype(jnp.float32)[15:16, :])
        cols.append(dual[c, 1, :, LANES:].astype(jnp.float32)[:, LANES - 1 :])
    last_row[...] = jnp.concatenate(rows, axis=0)
    last_column[...] = jnp.concatenate(cols, axis=1).T


def tile_ready(where, *refs):
    pieces, (early, late, dual, above, left) = refs[:4], refs[4:9]
    for_image, for_ahead, first_row, first_column = refs[9:]
    row_at = lax.broadcasted_iota(jnp.int32, (LANES, 2 * LANES), 0)
    lane_at = lax.broadcasted_iota(jnp.int32, (LANES, 2 * LANES), 1)
    for k in range(4):
        for other in range(2):
            half = where[0] % 2
            c = (where[0] // 2 + 4 - k) % 4 * 2 + (1 - half if other else half)
            p = dual[c, 0].astype(jnp.float32)
            q = dual[c, 1].astype(jnp.float32)
            beside = jnp.broadcast_to(left[pl.ds(c, 1), :], (LANES, LANES)).T[:, 0:1]
            prev_p = jnp.where(row_at == 0, above[pl.ds(c, 1), :], pltpu.roll(p, 1, 0))
            prev_q = jnp.where(lane_at == 0, beside, pltpu.roll(q, 1, 1))
            adjoint = prev_p - p + prev_q - q
            if other:
                image = jnp.concatenate([early[k], late[k]], axis=0)
            else:
                image = pieces[k][:, pl.ds(pl.multiple_of(half * 256, 256), 256)]
            ahead = image - adjoint
            for_image[c] = image - step_primal * adjoint
            for_ahead[c] = ahead
            first_row[pl.ds(c, 1), :] = ahead[0:1, :]
            first_column[pl.ds(c, 1), :] = ahead[:, :LANES].T[0:1, :]


def finish(
    gradient, for_image, for_ahead, dual, below, right, image_next, dual_next,
    ahead_v, side_v, image_v, dual_v, image_sems, dual_sems,
):
    sides = []
    leaving = []
    for c in range(CHANNELS):
        slope = gradient[c, :LANES, :]
        image_v[c] = for_image[c] - step_primal * slope
        leaving.append(fetched(image_v.at[c], image_next.at[c], image_sems.at[c]))
        ahead_v[c, :LANES, :] = for_ahead[c] - slope
        ahead_v[c, LANES : LANES + 1, :] = (
            below[c : c + 1, :] - gradient[c, LANES : LANES + 1, :]
        )
        sides.append(gradient[c, LANES + 1 : LANES + 2, :LANES])
    side_v[:, :CHANNELS] = (right[...] - jnp.concatenate(sides, axis=0)).T
    chunk = 16
    steps = LANES // chunk
    row_at = lax.broadcasted_iota(jnp.int32, (chunk, 2 * LANES), 0)
    lane_at = lax.broadcasted_iota(jnp.int32, (chunk, 2 * LANES), 1)

    def outgoing(step):
        rows = pl.ds(pl.multiple_of(step * chunk, chunk), chunk)
        return pltpu.make_async_copy(
            dual_v.at[:, :, rows, :], dual_next.at[:, :, rows, :], dual_sems.at[step]
        )

    def body(step, carry):
        at = pl.multiple_of(step * chunk, chunk)
        here = pl.ds(at, chunk)
        after = pl.ds(pl.multiple_of(at + chunk, chunk), 8)
        firsts, seconds, total = [], [], None
        for c in range(CHANNELS):
            ahead = ahead_v[c, here, :]
            next_row = ahead_v[c, after, :][0:1, :]
            down = jnp.where(row_at == chunk - 1, next_row, pltpu.roll(ahead, chunk - 1, 0))
            beside = jnp.where(
                lane_at == 2 * LANES - 1,
                side_v[here, c : c + 1],
                pltpu.roll(ahead, 2 * LANES - 1, 1),
            )
            first = dual[c, 0, here, :].astype(jnp.float32) + step_dual * (down - ahead)
            second = dual[c, 1, here, :].astype(jnp.float32) + step_dual * (beside - ahead)
            firsts.append(first)
            seconds.append(second)
            squares = first * first + second * second
            total = squares if total is None else total + squares
        factor = 1.0 / jnp.maximum(1.0, jnp.sqrt(total) / clip_radius)
        for c in range(CHANNELS):
            dual_v[c, 0, here, :] = (firsts[c] * factor).astype(jnp.bfloat16)
            dual_v[c, 1, here, :] = (seconds[c] * factor).astype(jnp.bfloat16)
        outgoing(step).start()
        return carry

    lax.fori_loop(0, steps, body, 0)
    for copy in leaving:
        copy.wait()
    for step in range(steps):
        outgoing(step).wait()


def shape(dims, dtype=jnp.float32):
    return jax.ShapeDtypeStruct(dims, dtype)


def passed_along(x, axis, by):
    devices = lax.axis_size(axis)
    pairs = [(i, i + by) for i in range(devices) if 0 <= i + by < devices]
    return lax.ppermute(x, axis, pairs)


ANY = pl.BlockSpec(memory_space=pl.ANY)
HBM = pl.BlockSpec(memory_space=pltpu.HBM)
VM = pl.BlockSpec(memory_space=pltpu.VMEM)
SM = pl.BlockSpec(memory_space=pltpu.SMEM)
DMA = pltpu.SemaphoreType.DMA


def call(kernel, out_shape, in_specs, out_specs, scratch, limit=16):
    return pl.pallas_call(
        kernel,
        out_shape=out_shape,
        in_specs=in_specs,
        out_specs=out_specs,
        scratch_shapes=scratch,
        name=kernel.__name__,
        compiler_params=pltpu.CompilerParams(vmem_limit_bytes=limit * MIB),
    )


def shards(image_field, weights, measured, dual_field):
    twiddle, place = host_tables()
    place = jnp.asarray(place, jnp.bfloat16)
    twiddle = jnp.asarray(twiddle)
    image = image_field[0]
    f32, bf16 = jnp.float32, jnp.bfloat16
    where = lax.axis_index("chan").astype(jnp.int32).reshape(1)

    spread = call(
        rows_forward,
        shape((RADIX, 2, RADIX, 8, LANES)),
        [HBM, HBM],
        HBM,
        [
            pltpu.VMEM((LANES, GRID), f32),
            pltpu.VMEM((2, RADIX + 8, LANES), f32),
            pltpu.VMEM((RADIX, 2, RADIX, 8, LANES), f32),
            pltpu.VMEM((GRID, 512), bf16),
            pltpu.VMEM((256, 768), bf16),
            DMA((9,)),
            DMA((8,)),
        ],
        63,
    )(image, twiddle)
    cols = lax.all_to_all(
        spread.reshape(RADIX, 2 * LANES, LANES), "facet", split_axis=0, concat_axis=0, tiled=True
    )
    last_row, last_column = call(
        dual_edges,
        (shape((CHANNELS, 2 * LANES)), shape((CHANNELS, LANES))),
        [VM],
        (VM, VM),
        [],
    )(dual_field)
    above = passed_along(last_row, "facet", 1)
    left = passed_along(last_column, "chan", 1)
    pieces = list(
        call(cross_ready, (shape((LANES, 512)),) * 4, [SM, VM], (VM,) * 4, [])(where, image)
    )
    for k in range(1, 4):
        pairs = [(2 * x + z, (x + k) % 4 * 2 + z) for x in range(4) for z in range(2)]
        pieces[k] = lax.ppermute(pieces[k], "chan", pairs)
    early, late = call(
        swap_ready, (shape((4, LANES // 2, 256)),) * 2, [SM] + [VM] * 4, (VM, VM), []
    )(where, *pieces)
    other_zl = [(i, i ^ 1) for i in range(8)]
    early = lax.ppermute(early, "chan", other_zl)
    data, forward, inverse = call(
        data_prepared,
        (
            shape((3, RADIX, LANES, LANES), bf16),
            shape((768, 256), bf16),
            shape((768, 256), bf16),
        ),
        [VM] * 4,
        (VM,) * 3,
        [pltpu.VMEM((GRID, LANES), f32)],
        63,
    )(weights[0], measured[0], place, twiddle)
    cols, late, data, forward, inverse = lax.optimization_barrier(
        (cols, late, data, forward, inverse)
    )
    late = lax.ppermute(late, "chan", other_zl)
    cols = pltpu.with_memory_space_constraint(cols, pltpu.VMEM)
    data, forward, inverse = (
        pltpu.with_memory_space_constraint(x, pltpu.HBM) for x in (data, forward, inverse)
    )
    back = call(
        columns,
        shape((RADIX, 2 * LANES + 8, LANES)),
        [VM, HBM, VM, HBM, HBM],
        HBM,
        [
            pltpu.VMEM((3, RADIX, LANES, LANES), bf16),
            pltpu.VMEM((768, 256), bf16),
            pltpu.VMEM((768, 256), bf16),
            pltpu.VMEM((RADIX, 2 * LANES + 8, LANES), f32),
            pltpu.VMEM((GRID, 512), bf16),
            pltpu.VMEM((GRID, 256), f32),
            DMA((6,)),
            DMA((8, 2)),
        ],
    )(cols, data, twiddle, forward, inverse)
    back, early, late = lax.optimization_barrier((back, early, late))
    lines = lax.all_to_all(back, "facet", split_axis=0, concat_axis=0, tiled=True)
    for_image, for_ahead, first_row, first_column = call(
        tile_ready,
        (
            shape((CHANNELS, LANES, 2 * LANES)),
            shape((CHANNELS, LANES, 2 * LANES)),
            shape((CHANNELS, 2 * LANES)),
            shape((CHANNELS, LANES)),
        ),
        [SM] + [VM] * 9,
        (VM,) * 4,
        [],
    )(where, *pieces, early, late, dual_field, above, left)
    below = passed_along(first_row, "facet", -1)
    right = passed_along(first_column, "chan", -1)
    lines, below, right = lax.optimization_barrier((lines, below, right))
    lines = pltpu.with_memory_space_constraint(lines, pltpu.VMEM)
    slopes = call(
        rows_back,
        shape((CHANNELS, LANES + 8, 2 * LANES)),
        [VM] * 2,
        VM,
        [
            pltpu.VMEM((RADIX, LANES, 256), f32),
            pltpu.VMEM((LANES, LANES), f32),
            pltpu.VMEM((768, 256), bf16),
        ],
    )(lines, twiddle)
    gradient = lax.all_to_all(slopes, "chan", split_axis=0, concat_axis=0, tiled=True)
    return call(
        finish,
        (shape((CHANNELS, LANES, 2 * LANES)), shape((CHANNELS, 2, LANES, 2 * LANES), bf16)),
        [VM] * 6,
        (HBM, HBM),
        [
            pltpu.VMEM((CHANNELS, LANES + 8, 2 * LANES), f32),
            pltpu.VMEM((LANES, LANES), f32),
            pltpu.VMEM((CHANNELS, LANES, 2 * LANES), f32),
            pltpu.VMEM((CHANNELS, 2, LANES, 2 * LANES), bf16),
            DMA((8,)),
            DMA((8,)),
        ],
    )(gradient, for_image, for_ahead, dual_field, below, right)


def solution(mesh):
    placed = (
        P("chan", "facet", None),
        P("chan", None, "facet"),
        P("chan", None, None, "facet"),
        P(None, None, "facet", "chan"),
    )
    return jax.shard_map(
        shards,
        mesh=mesh,
        in_specs=placed,
        out_specs=(P(None, "facet", "chan"), P(None, None, "facet", "chan")),
        check_vma=False,
    )
```

```python
from functools import partial
import math

import jax
import jax.numpy as jnp
import numpy as np
from jax import lax
from jax.experimental import pallas as pl
from jax.experimental.pallas import tpu as pltpu
from jax.sharding import PartitionSpec as P

GRID = 2048
RADIX = 16
LANES = 128
CHANNELS = 8

step_primal = 0.5
step_dual = 0.5
clip_radius = 4.0

MIB = 1024 * 1024


def host_tables():
    index = np.arange(LANES)
    turn = 2.0 * np.pi * np.arange(RADIX + 8)[:, None] * index[None, :] / GRID
    twiddle = np.stack([np.cos(turn), np.sin(turn)]).astype(np.float32)
    place = np.zeros((LANES, LANES))
    for at in range(LANES):
        place[at, 16 * (at % 8) + at // 8] = 1.0
    return twiddle, place


def c_add(a, b):
    return (a[0] + b[0], b[1] if a[1] is None else a[1] if b[1] is None else a[1] + b[1])


def c_sub(a, b):
    imag = None
    if a[1] is not None and b[1] is not None:
        imag = a[1] - b[1]
    elif a[1] is not None:
        imag = a[1]
    elif b[1] is not None:
        imag = -b[1]
    return (a[0] - b[0], imag)


def add_turned(a, b, sign):
    real = a[0] if b[1] is None else (a[0] - b[1] if sign > 0 else a[0] + b[1])
    if a[1] is None:
        imag = b[0] if sign > 0 else -b[0]
    else:
        imag = a[1] + b[0] if sign > 0 else a[1] - b[0]
    return (real, imag)


def four(a, b, c, d, sign):
    sum_even, diff_even = c_add(a, c), c_sub(a, c)
    sum_odd, diff_odd = c_add(b, d), c_sub(b, d)
    return (
        c_add(sum_even, sum_odd),
        add_turned(diff_even, diff_odd, sign),
        c_sub(sum_even, sum_odd),
        add_turned(diff_even, diff_odd, -sign),
    )


def turned(a, power, sign):
    power = power % 16
    if power == 0:
        return a
    cos, sin = math.cos(2 * math.pi * power / 16), sign * math.sin(2 * math.pi * power / 16)
    real, imag = a
    if imag is None:
        if power == 4:
            return (jnp.zeros_like(real), real if sign > 0 else -real)
        return (real * cos, real * sin)
    if power == 4:
        return (-imag, real) if sign > 0 else (imag, -real)
    if abs(abs(cos) - abs(sin)) < 1e-9:
        root = math.sqrt(0.5)
        cs, ss = (1 if cos > 0 else -1), (1 if sin > 0 else -1)
        new_real = (real if cs > 0 else -real) - (imag if ss > 0 else -imag)
        new_imag = (real if ss > 0 else -real) + (imag if cs > 0 else -imag)
        return (new_real * root, new_imag * root)
    return (real * cos - imag * sin, real * sin + imag * cos)


def sixteen(values, sign):
    inner = [four(*(values[n0 + 4 * n1] for n1 in range(4)), sign) for n0 in range(4)]
    out = [None] * 16
    for k1 in range(4):
        parts = [turned(inner[n0][k1], n0 * k1, sign) for n0 in range(4)]
        for k2, value in enumerate(four(*parts, sign)):
            out[k1 + 4 * k2] = value
    return out


def split(value):
    high = value.astype(jnp.bfloat16)
    low = (value - high.astype(jnp.float32)).astype(jnp.bfloat16)
    return high, low


def dot(a, b, dims):
    return lax.dot_general(a, b, (dims, ((), ())), preferred_element_type=jnp.float32)


def fetched(source, target, semaphore):
    copy = pltpu.make_async_copy(source, target, semaphore)
    copy.start()
    return copy


def fill_table(table, twiddle, sign, transposed):
    shape = (LANES, LANES)
    row, col = (lax.broadcasted_iota(jnp.int32, shape, n) for n in range(2))
    at = jnp.bitwise_and(row * col, LANES - 1)
    cos, sin = (
        jnp.take_along_axis(
            jnp.broadcast_to(twiddle[n, RADIX : RADIX + 1, :], shape), at, axis=1
        )
        for n in range(2)
    )
    for n, value in enumerate((cos, sign * sin, -sign * sin, cos)):
        high, low = split(value)
        into, out = ((n // 2, n % 2), (n % 2, n // 2))[transposed]
        for m, half in enumerate((high, high, low)):
            if transposed:
                lane = 256 * m + LANES * out
                table[LANES * into : LANES * into + LANES, lane : lane + LANES] = half
            else:
                at_row = 256 * m + LANES * into
                table[at_row : at_row + LANES, LANES * out : LANES * out + LANES] = half


def three_pass(pair, table, dims):
    high = pair[:, :256] if dims[0][0] == 1 else pair[:256, :]
    return dot(pair, table[:512, :], dims) + dot(high, table[512:, :], dims)


def store_pair(held, rows, real, imag):
    high_r, low_r = split(real)
    high_i, low_i = split(imag)
    held[rows, 0:LANES] = high_r
    held[rows, LANES : 2 * LANES] = high_i
    held[rows, 2 * LANES : 3 * LANES] = low_r
    held[rows, 3 * LANES : 4 * LANES] = low_i


def cross_ready(where, image, *pieces):
    for k in range(4):
        to = (where[0] // 2 + k) % 4
        pieces[k][...] = image[:, pl.ds(pl.multiple_of(to * 512, 512), 512)]


def swap_ready(where, *refs):
    pieces, early, late = refs[:4], refs[4], refs[5]
    lanes = pl.ds(pl.multiple_of((1 - where[0] % 2) * 256, 256), 256)
    for k in range(4):
        early[k] = pieces[k][: LANES // 2, lanes]
        late[k] = pieces[k][LANES // 2 :, lanes]


def rows_forward(
    image_in, twiddle_in, out, image, twiddle, out_v, held, table, in_sems, sems
):
    chunk = 16
    steps = LANES // chunk

    def incoming(step):
        rows = pl.ds(pl.multiple_of(step * chunk, chunk), chunk)
        return pltpu.make_async_copy(image_in.at[rows, :], image.at[rows, :], in_sems.at[step])

    get_twiddle = fetched(twiddle_in, twiddle, in_sems.at[steps])
    for step in range(steps):
        incoming(step).start()
    get_twiddle.wait()
    fill_table(table, twiddle, -1, True)

    def body(step, carry):
        incoming(step).wait()
        at = pl.multiple_of(step * chunk, chunk)
        values = [
            (image[pl.ds(at, chunk), b * LANES : (b + 1) * LANES], None) for b in range(RADIX)
        ]
        mixed = sixteen(values, -1)
        for f in range(RADIX):
            real, imag = mixed[f]
            if imag is None:
                imag = jnp.zeros_like(real)
            cos = twiddle[0, f : f + 1, :] * (1.0 / GRID)
            sin = twiddle[1, f : f + 1, :] * (1.0 / GRID)
            store_pair(
                held,
                pl.ds(f * LANES + at, chunk),
                real * cos + imag * sin,
                imag * cos - real * sin,
            )
        return carry

    lax.fori_loop(0, steps, body, 0)
    dims = ((1,), (1,))
    sent = []
    for g in range(RADIX // 2):
        pair = held[256 * g : 256 * g + 256, :]
        result = dot(table[:, :512], pair, dims) + dot(table[:, 512:], pair[:, :256], dims)
        for h in range(2):
            for c in range(2):
                block = result[c * LANES : (c + 1) * LANES, h * LANES : (h + 1) * LANES]
                out_v[:, c, 2 * g + h] = block.reshape(RADIX, 8, LANES)
        both = pl.ds(2 * g, 2)
        sent.append(fetched(out_v.at[:, :, both], out.at[:, :, both], sems.at[g]))
    for copy in sent:
        copy.wait()


def data_prepared(weights, measured, place, twiddle, out, forward, inverse, held):
    fill_table(forward, twiddle, -1, False)
    fill_table(inverse, twiddle, 1, False)
    for n in range(3):
        source = weights[...] if n == 0 else measured[n - 1]
        held[...] = source.astype(jnp.float32)
        for f in range(RADIX):
            rows = held[pl.ds(f, LANES, stride=RADIX), :].astype(jnp.bfloat16)
            out[n, f] = dot(place[...], rows, ((1,), (1,))).astype(jnp.bfloat16)


def columns(
    cols_in, data_in, twiddle_in, forward_in, inverse_in, out_all,
    cols, data, twiddle, forward, inverse, out, held, in_sems, chunk_sems, out_sems,
):
    chunk = 32
    steps = LANES // chunk
    dims = ((1,), (0,))

    def incoming_cols(step):
        rows = pl.ds(pl.multiple_of(step * chunk, chunk), chunk)
        imag_rows = pl.ds(pl.multiple_of(LANES + step * chunk, chunk), chunk)
        return [
            pltpu.make_async_copy(cols_in.at[:, r, :], cols.at[:, r, :], chunk_sems.at[step, n])
            for n, r in enumerate((rows, imag_rows))
        ]

    def incoming(step):
        rows = pl.ds(pl.multiple_of(step * chunk, chunk), chunk)
        return pltpu.make_async_copy(
            data_in.at[:, :, rows, :], data.at[:, :, rows, :], chunk_sems.at[step, 2]
        )

    def outgoing(step, c):
        rows = pl.ds(pl.multiple_of(c * LANES + step * chunk, chunk), chunk)
        return pltpu.make_async_copy(
            out.at[:, rows, :], out_all.at[:, rows, :], out_sems.at[step, c]
        )

    for copy in incoming_cols(0):
        copy.start()
    get_twiddle = fetched(twiddle_in, twiddle, in_sems.at[2])
    get_forward = fetched(forward_in, forward, in_sems.at[0])
    incoming(0).start()
    get_inverse = fetched(inverse_in, inverse, in_sems.at[1])
    for step in range(1, steps):
        for copy in incoming_cols(step):
            copy.start()
        incoming(step).start()
    out[:, 2 * LANES :, :] = jnp.zeros((RADIX, 8, LANES), jnp.float32)
    lane_at = lax.broadcasted_iota(jnp.int32, (8, LANES), 1)
    get_twiddle.wait()

    def body(step, carry):
        at = pl.multiple_of(step * chunk, chunk)
        here = pl.ds(at, chunk)
        for copy in incoming_cols(step):
            copy.wait()
        imag_here = pl.ds(pl.multiple_of(LANES + at, chunk), chunk)
        mixed = sixteen([(cols[b, here, :], cols[b, imag_here, :]) for b in range(RADIX)], -1)
        for f in range(RADIX):
            real, imag = mixed[f]
            cos, sin = twiddle[0, f : f + 1, :], twiddle[1, f : f + 1, :]
            rows = slice(f * chunk, (f + 1) * chunk)
            store_pair(held, rows, real * cos + imag * sin, imag * cos - real * sin)

        @pl.when(step == 0)
        def _():
            get_forward.wait()
            get_inverse.wait()

        spectrum = three_pass(held[...], forward, dims)
        incoming(step).wait()
        for f in range(RADIX):
            rows = slice(f * chunk, (f + 1) * chunk)
            weight = data[0, f, here, :].astype(jnp.float32)
            real = weight * spectrum[rows, :LANES] - data[1, f, here, :].astype(jnp.float32)
            imag = weight * spectrum[rows, LANES:] - data[2, f, here, :].astype(jnp.float32)
            store_pair(held, rows, real, imag)
        back = three_pass(held[...], inverse, dims)
        values = []
        for f in range(RADIX):
            rows = slice(f * chunk, (f + 1) * chunk)
            real, imag = back[rows, :LANES], back[rows, LANES:]
            cos, sin = twiddle[0, f : f + 1, :], twiddle[1, f : f + 1, :]
            values.append((real * cos - imag * sin, imag * cos + real * sin))
        mixed = sixteen(values, 1)
        for b in range(RADIX):
            for c in range(2):
                out[b, (here, imag_here)[c], :] = mixed[b][c]
                if b > 0:
                    edge = out[b - 1, 2 * LANES :, :]
                    for i in range(chunk // 8):
                        first = mixed[b][c][8 * i : 8 * i + 8, 0:1]
                        at_lane = lane_at == c * RADIX + step * (chunk // 8) + i
                        edge = jnp.where(at_lane, first, edge)
                    out[b - 1, 2 * LANES :, :] = edge
        for c in range(2):
            outgoing(step, c).start()
        return carry

    lax.fori_loop(0, steps, body, 0)
    rows = pl.ds(2 * LANES, 8)
    edges = fetched(out.at[:, rows, :], out_all.at[:, rows, :], in_sems.at[0])
    for step in range(steps):
        for c in range(2):
            outgoing(step, c).wait()
    edges.wait()


def tied(value, after_one, after_two, out):
    pass


def rows_back(lines, twiddle, after_one, after_two, out, held, side_v, table):
    fill_table(table, twiddle, 1, False)
    dims = ((0,), (0,))
    for f in range(RADIX):
        real = lines[:, 8 * f : 8 * f + 8, :].reshape(LANES, LANES)
        imag = lines[:, LANES + 8 * f : LANES + 8 * f + 8, :].reshape(LANES, LANES)
        high_r, low_r = split(real)
        high_i, low_i = split(imag)
        pair = jnp.concatenate([high_r, high_i, low_r, low_i], axis=0)
        held[f] = three_pass(pair, table, dims)
    high, low = split(lines[:, 2 * LANES :, :].reshape(LANES, LANES))
    edge = (
        dot(high, table[0:LANES, :], dims)
        + dot(low, table[0:LANES, :], dims)
        + dot(high, table[512 : 512 + LANES, :], dims)
    )
    edge_r = edge[:RADIX, :LANES] - edge[RADIX : 2 * RADIX, LANES:]
    edge_i = edge[:RADIX, LANES:] + edge[RADIX : 2 * RADIX, :LANES]
    scale = 1.0 / GRID
    cos, sin = twiddle[0, :RADIX] * scale, twiddle[1, :RADIX] * scale
    edge_r, edge_i = edge_r * cos - edge_i * sin, edge_i * cos + edge_r * sin
    mixed = sixteen([(edge_r[f : f + 1], edge_i[f : f + 1]) for f in range(RADIX)], 1)
    for d in range(CHANNELS):
        out[d, LANES : LANES + 1, :] = jnp.concatenate(
            [mixed[2 * d][0], mixed[2 * d + 1][0]], axis=1
        )
    chunk = 16
    steps = LANES // chunk
    lane_at = lax.broadcasted_iota(jnp.int32, (chunk, LANES), 1)

    def body(step, carry):
        at = pl.multiple_of(step * chunk, chunk)
        here = pl.ds(at, chunk)
        values = []
        for f in range(RADIX):
            real, imag = held[f, here, :LANES], held[f, here, LANES:]
            cos, sin = twiddle[0, f : f + 1, :] * scale, twiddle[1, f : f + 1, :] * scale
            values.append((real * cos - imag * sin, imag * cos + real * sin))
        mixed = sixteen(values, 1)
        side = jnp.zeros((chunk, LANES), jnp.float32)
        for b in range(RADIX):
            low_lane = (b % 2) * LANES
            out[b // 2, here, low_lane : low_lane + LANES] = mixed[b][0]
            if b > 0 and b % 2 == 0:
                side = jnp.where(lane_at == b // 2 - 1, mixed[b][0][:, 0:1], side)
        side_v[here, :] = side
        return carry

    lax.fori_loop(0, steps, body, 0)
    beside = side_v[...].T
    for d in range(CHANNELS):
        out[d, LANES + 1 : LANES + 2, :LANES] = beside[d : d + 1, :]


def dual_edges(dual, last_row, last_column):
    rows, cols = [], []
    for c in range(CHANNELS):
        rows.append(dual[c, 0, 112:128, :].astype(jnp.float32)[15:16, :])
        cols.append(dual[c, 1, :, LANES:].astype(jnp.float32)[:, LANES - 1 :])
    last_row[...] = jnp.concatenate(rows, axis=0)
    last_column[...] = jnp.concatenate(cols, axis=1).T


def tile_ready(where, *refs):
    pieces, (early, late, dual, above, left) = refs[:4], refs[4:9]
    for_image, for_ahead, first_row, first_column = refs[9:]
    row_at = lax.broadcasted_iota(jnp.int32, (LANES, 2 * LANES), 0)
    lane_at = lax.broadcasted_iota(jnp.int32, (LANES, 2 * LANES), 1)
    for k in range(4):
        for other in range(2):
            half = where[0] % 2
            c = (where[0] // 2 + 4 - k) % 4 * 2 + (1 - half if other else half)
            p = dual[c, 0].astype(jnp.float32)
            q = dual[c, 1].astype(jnp.float32)
            beside = jnp.broadcast_to(left[pl.ds(c, 1), :], (LANES, LANES)).T[:, 0:1]
            prev_p = jnp.where(row_at == 0, above[pl.ds(c, 1), :], pltpu.roll(p, 1, 0))
            prev_q = jnp.where(lane_at == 0, beside, pltpu.roll(q, 1, 1))
            adjoint = prev_p - p + prev_q - q
            if other:
                image = jnp.concatenate([early[k], late[k]], axis=0)
            else:
                image = pieces[k][:, pl.ds(pl.multiple_of(half * 256, 256), 256)]
            ahead = image - adjoint
            for_image[c] = image - step_primal * adjoint
            for_ahead[c] = ahead
            first_row[pl.ds(c, 1), :] = ahead[0:1, :]
            first_column[pl.ds(c, 1), :] = ahead[:, :LANES].T[0:1, :]


def finish(
    gradient, for_image, for_ahead, dual, below, right, image_next, dual_next,
    ahead_v, side_v, image_v, dual_v, image_sems, dual_sems,
):
    sides = []
    leaving = []
    for c in range(CHANNELS):
        slope = gradient[c, :LANES, :]
        image_v[c] = for_image[c] - step_primal * slope
        leaving.append(fetched(image_v.at[c], image_next.at[c], image_sems.at[c]))
        ahead_v[c, :LANES, :] = for_ahead[c] - slope
        ahead_v[c, LANES : LANES + 1, :] = (
            below[c : c + 1, :] - gradient[c, LANES : LANES + 1, :]
        )
        sides.append(gradient[c, LANES + 1 : LANES + 2, :LANES])
    side_v[:, :CHANNELS] = (right[...] - jnp.concatenate(sides, axis=0)).T
    chunk = 16
    steps = LANES // chunk
    row_at = lax.broadcasted_iota(jnp.int32, (chunk, 2 * LANES), 0)
    lane_at = lax.broadcasted_iota(jnp.int32, (chunk, 2 * LANES), 1)

    def outgoing(step):
        rows = pl.ds(pl.multiple_of(step * chunk, chunk), chunk)
        return pltpu.make_async_copy(
            dual_v.at[:, :, rows, :], dual_next.at[:, :, rows, :], dual_sems.at[step]
        )

    def body(step, carry):
        at = pl.multiple_of(step * chunk, chunk)
        here = pl.ds(at, chunk)
        after = pl.ds(pl.multiple_of(at + chunk, chunk), 8)
        firsts, seconds, total = [], [], None
        for c in range(CHANNELS):
            ahead = ahead_v[c, here, :]
            next_row = ahead_v[c, after, :][0:1, :]
            down = jnp.where(row_at == chunk - 1, next_row, pltpu.roll(ahead, chunk - 1, 0))
            beside = jnp.where(
                lane_at == 2 * LANES - 1,
                side_v[here, c : c + 1],
                pltpu.roll(ahead, 2 * LANES - 1, 1),
            )
            first = dual[c, 0, here, :].astype(jnp.float32) + step_dual * (down - ahead)
            second = dual[c, 1, here, :].astype(jnp.float32) + step_dual * (beside - ahead)
            firsts.append(first)
            seconds.append(second)
            squares = first * first + second * second
            total = squares if total is None else total + squares
        factor = 1.0 / jnp.maximum(1.0, jnp.sqrt(total) / clip_radius)
        for c in range(CHANNELS):
            dual_v[c, 0, here, :] = (firsts[c] * factor).astype(jnp.bfloat16)
            dual_v[c, 1, here, :] = (seconds[c] * factor).astype(jnp.bfloat16)
        outgoing(step).start()
        return carry

    lax.fori_loop(0, steps, body, 0)
    for copy in leaving:
        copy.wait()
    for step in range(steps):
        outgoing(step).wait()


def shape(dims, dtype=jnp.float32):
    return jax.ShapeDtypeStruct(dims, dtype)


def passed_along(x, axis, by):
    devices = lax.axis_size(axis)
    pairs = [(i, i + by) for i in range(devices) if 0 <= i + by < devices]
    return lax.ppermute(x, axis, pairs)


ANY = pl.BlockSpec(memory_space=pl.ANY)
HBM = pl.BlockSpec(memory_space=pltpu.HBM)
VM = pl.BlockSpec(memory_space=pltpu.VMEM)
SM = pl.BlockSpec(memory_space=pltpu.SMEM)
DMA = pltpu.SemaphoreType.DMA


def call(kernel, out_shape, in_specs, out_specs, scratch, limit=16):
    return pl.pallas_call(
        kernel,
        out_shape=out_shape,
        in_specs=in_specs,
        out_specs=out_specs,
        scratch_shapes=scratch,
        name=kernel.__name__,
        compiler_params=pltpu.CompilerParams(vmem_limit_bytes=limit * MIB),
    )


def shards(image_field, weights, measured, dual_field):
    twiddle, place = host_tables()
    place = jnp.asarray(place, jnp.bfloat16)
    twiddle = jnp.asarray(twiddle)
    image = image_field[0]
    f32, bf16 = jnp.float32, jnp.bfloat16
    where = lax.axis_index("chan").astype(jnp.int32).reshape(1)

    spread = call(
        rows_forward,
        shape((RADIX, 2, RADIX, 8, LANES)),
        [HBM, HBM],
        HBM,
        [
            pltpu.VMEM((LANES, GRID), f32),
            pltpu.VMEM((2, RADIX + 8, LANES), f32),
            pltpu.VMEM((RADIX, 2, RADIX, 8, LANES), f32),
            pltpu.VMEM((GRID, 512), bf16),
            pltpu.VMEM((256, 768), bf16),
            DMA((9,)),
            DMA((8,)),
        ],
        63,
    )(image, twiddle)
    cols = lax.all_to_all(
        spread.reshape(RADIX, 2 * LANES, LANES), "facet", split_axis=0, concat_axis=0, tiled=True
    )
    last_row, last_column = call(
        dual_edges,
        (shape((CHANNELS, 2 * LANES)), shape((CHANNELS, LANES))),
        [VM],
        (VM, VM),
        [],
    )(dual_field)
    above = passed_along(last_row, "facet", 1)
    left = passed_along(last_column, "chan", 1)
    pieces = list(
        call(cross_ready, (shape((LANES, 512)),) * 4, [SM, VM], (VM,) * 4, [])(where, image)
    )
    for k in range(1, 4):
        pairs = [(2 * x + z, (x + k) % 4 * 2 + z) for x in range(4) for z in range(2)]
        pieces[k] = lax.ppermute(pieces[k], "chan", pairs)
    early, late = call(
        swap_ready, (shape((4, LANES // 2, 256)),) * 2, [SM] + [VM] * 4, (VM, VM), []
    )(where, *pieces)
    other_zl = [(i, i ^ 1) for i in range(8)]
    early = lax.ppermute(early, "chan", other_zl)
    data, forward, inverse = call(
        data_prepared,
        (
            shape((3, RADIX, LANES, LANES), bf16),
            shape((768, 256), bf16),
            shape((768, 256), bf16),
        ),
        [VM] * 4,
        (VM,) * 3,
        [pltpu.VMEM((GRID, LANES), f32)],
        63,
    )(weights[0], measured[0], place, twiddle)
    cols, late, above, left, data, forward, inverse = lax.optimization_barrier(
        (cols, late, above, left, data, forward, inverse)
    )
    late = lax.ppermute(late, "chan", other_zl)
    data, forward, inverse = (
        pltpu.with_memory_space_constraint(x, pltpu.HBM) for x in (data, forward, inverse)
    )
    back = call(
        columns,
        shape((RADIX, 2 * LANES + 8, LANES)),
        [HBM] * 5,
        HBM,
        [
            pltpu.VMEM((RADIX, 2 * LANES, LANES), f32),
            pltpu.VMEM((3, RADIX, LANES, LANES), bf16),
            pltpu.VMEM((2, RADIX + 8, LANES), f32),
            pltpu.VMEM((768, 256), bf16),
            pltpu.VMEM((768, 256), bf16),
            pltpu.VMEM((RADIX, 2 * LANES + 8, LANES), f32),
            pltpu.VMEM((RADIX * 32, 512), bf16),
            DMA((3,)),
            DMA((4, 3)),
            DMA((4, 2)),
        ],
        63,
    )(cols, data, twiddle, forward, inverse)
    back = pl.pallas_call(
        tied,
        out_shape=shape((RADIX, 2 * LANES + 8, LANES)),
        in_specs=[ANY] * 3,
        out_specs=ANY,
        input_output_aliases={0: 0},
        name="tied",
    )(back, early, late)
    lines = lax.all_to_all(back, "facet", split_axis=0, concat_axis=0, tiled=True)
    for_image, for_ahead, first_row, first_column = call(
        tile_ready,
        (
            shape((CHANNELS, LANES, 2 * LANES)),
            shape((CHANNELS, LANES, 2 * LANES)),
            shape((CHANNELS, 2 * LANES)),
            shape((CHANNELS, LANES)),
        ),
        [SM] + [VM] * 9,
        (VM,) * 4,
        [],
    )(where, *pieces, early, late, dual_field, above, left)
    below = passed_along(first_row, "facet", -1)
    right = passed_along(first_column, "chan", -1)
    slopes = call(
        rows_back,
        shape((CHANNELS, LANES + 8, 2 * LANES)),
        [VM] * 2 + [ANY] * 2,
        VM,
        [
            pltpu.VMEM((RADIX, LANES, 256), f32),
            pltpu.VMEM((LANES, LANES), f32),
            pltpu.VMEM((768, 256), bf16),
        ],
    )(lines, twiddle, below, right)
    gradient = lax.all_to_all(slopes, "chan", split_axis=0, concat_axis=0, tiled=True)
    return call(
        finish,
        (shape((CHANNELS, LANES, 2 * LANES)), shape((CHANNELS, 2, LANES, 2 * LANES), bf16)),
        [VM] * 6,
        (HBM, HBM),
        [
            pltpu.VMEM((CHANNELS, LANES + 8, 2 * LANES), f32),
            pltpu.VMEM((LANES, LANES), f32),
            pltpu.VMEM((CHANNELS, LANES, 2 * LANES), f32),
            pltpu.VMEM((CHANNELS, 2, LANES, 2 * LANES), bf16),
            DMA((8,)),
            DMA((8,)),
        ],
    )(gradient, for_image, for_ahead, dual_field, below, right)


def solution(mesh):
    placed = (
        P("chan", "facet", None),
        P("chan", None, "facet"),
        P("chan", None, None, "facet"),
        P(None, None, "facet", "chan"),
    )
    return jax.shard_map(
        shards,
        mesh=mesh,
        in_specs=placed,
        out_specs=(P(None, "facet", "chan"), P(None, None, "facet", "chan")),
        check_vma=False,
    )
```

```python
from functools import partial
import math

import jax
import jax.numpy as jnp
import numpy as np
from jax import lax
from jax.experimental import pallas as pl
from jax.experimental.pallas import tpu as pltpu
from jax.sharding import PartitionSpec as P

GRID = 2048
RADIX = 16
LANES = 128
CHANNELS = 8

step_primal = 0.5
step_dual = 0.5
clip_radius = 4.0

MIB = 1024 * 1024


def host_tables():
    index = np.arange(LANES)
    turn = 2.0 * np.pi * np.arange(RADIX + 8)[:, None] * index[None, :] / GRID
    twiddle = np.stack([np.cos(turn), np.sin(turn)]).astype(np.float32)
    place = np.zeros((LANES, LANES))
    for at in range(LANES):
        place[at, 16 * (at % 8) + at // 8] = 1.0
    return twiddle, place


def c_add(a, b):
    return (a[0] + b[0], b[1] if a[1] is None else a[1] if b[1] is None else a[1] + b[1])


def c_sub(a, b):
    imag = None
    if a[1] is not None and b[1] is not None:
        imag = a[1] - b[1]
    elif a[1] is not None:
        imag = a[1]
    elif b[1] is not None:
        imag = -b[1]
    return (a[0] - b[0], imag)


def add_turned(a, b, sign):
    real = a[0] if b[1] is None else (a[0] - b[1] if sign > 0 else a[0] + b[1])
    if a[1] is None:
        imag = b[0] if sign > 0 else -b[0]
    else:
        imag = a[1] + b[0] if sign > 0 else a[1] - b[0]
    return (real, imag)


def four(a, b, c, d, sign):
    sum_even, diff_even = c_add(a, c), c_sub(a, c)
    sum_odd, diff_odd = c_add(b, d), c_sub(b, d)
    return (
        c_add(sum_even, sum_odd),
        add_turned(diff_even, diff_odd, sign),
        c_sub(sum_even, sum_odd),
        add_turned(diff_even, diff_odd, -sign),
    )


def turned(a, power, sign):
    power = power % 16
    if power == 0:
        return a
    cos, sin = math.cos(2 * math.pi * power / 16), sign * math.sin(2 * math.pi * power / 16)
    real, imag = a
    if imag is None:
        if power == 4:
            return (jnp.zeros_like(real), real if sign > 0 else -real)
        return (real * cos, real * sin)
    if power == 4:
        return (-imag, real) if sign > 0 else (imag, -real)
    if abs(abs(cos) - abs(sin)) < 1e-9:
        root = math.sqrt(0.5)
        cs, ss = (1 if cos > 0 else -1), (1 if sin > 0 else -1)
        new_real = (real if cs > 0 else -real) - (imag if ss > 0 else -imag)
        new_imag = (real if ss > 0 else -real) + (imag if cs > 0 else -imag)
        return (new_real * root, new_imag * root)
    return (real * cos - imag * sin, real * sin + imag * cos)


def sixteen(values, sign):
    inner = [four(*(values[n0 + 4 * n1] for n1 in range(4)), sign) for n0 in range(4)]
    out = [None] * 16
    for k1 in range(4):
        parts = [turned(inner[n0][k1], n0 * k1, sign) for n0 in range(4)]
        for k2, value in enumerate(four(*parts, sign)):
            out[k1 + 4 * k2] = value
    return out


def split(value):
    high = value.astype(jnp.bfloat16)
    low = (value - high.astype(jnp.float32)).astype(jnp.bfloat16)
    return high, low


def dot(a, b, dims):
    return lax.dot_general(a, b, (dims, ((), ())), preferred_element_type=jnp.float32)


def fetched(source, target, semaphore):
    copy = pltpu.make_async_copy(source, target, semaphore)
    copy.start()
    return copy


def fill_table(table, twiddle, sign, transposed):
    shape = (LANES, LANES)
    row, col = (lax.broadcasted_iota(jnp.int32, shape, n) for n in range(2))
    at = jnp.bitwise_and(row * col, LANES - 1)
    cos, sin = (
        jnp.take_along_axis(
            jnp.broadcast_to(twiddle[n, RADIX : RADIX + 1, :], shape), at, axis=1
        )
        for n in range(2)
    )
    for n, value in enumerate((cos, sign * sin, -sign * sin, cos)):
        high, low = split(value)
        into, out = ((n // 2, n % 2), (n % 2, n // 2))[transposed]
        for m, half in enumerate((high, high, low)):
            if transposed:
                lane = 256 * m + LANES * out
                table[LANES * into : LANES * into + LANES, lane : lane + LANES] = half
            else:
                at_row = 256 * m + LANES * into
                table[at_row : at_row + LANES, LANES * out : LANES * out + LANES] = half


def three_pass(pair, table, dims):
    high = pair[:, :256] if dims[0][0] == 1 else pair[:256, :]
    return dot(pair, table[:512, :], dims) + dot(high, table[512:, :], dims)


def store_pair(held, rows, real, imag):
    high_r, low_r = split(real)
    high_i, low_i = split(imag)
    held[rows, 0:LANES] = high_r
    held[rows, LANES : 2 * LANES] = high_i
    held[rows, 2 * LANES : 3 * LANES] = low_r
    held[rows, 3 * LANES : 4 * LANES] = low_i


def cross_ready(where, image, *pieces):
    for k in range(4):
        to = (where[0] // 2 + k) % 4
        pieces[k][...] = image[:, pl.ds(pl.multiple_of(to * 512, 512), 512)]


def swap_ready(where, *refs):
    pieces, early, late = refs[:4], refs[4], refs[5]
    lanes = pl.ds(pl.multiple_of((1 - where[0] % 2) * 256, 256), 256)
    for k in range(4):
        early[k] = pieces[k][: LANES // 2, lanes]
        late[k] = pieces[k][LANES // 2 :, lanes]


def rows_forward(
    image_in, twiddle_in, out, image, twiddle, out_v, held, table, in_sems, sems
):
    chunk = 16
    steps = LANES // chunk

    def incoming(step):
        rows = pl.ds(pl.multiple_of(step * chunk, chunk), chunk)
        return pltpu.make_async_copy(image_in.at[rows, :], image.at[rows, :], in_sems.at[step])

    get_twiddle = fetched(twiddle_in, twiddle, in_sems.at[steps])
    for step in range(steps):
        incoming(step).start()
    get_twiddle.wait()
    fill_table(table, twiddle, -1, True)

    def body(step, carry):
        incoming(step).wait()
        at = pl.multiple_of(step * chunk, chunk)
        values = [
            (image[pl.ds(at, chunk), b * LANES : (b + 1) * LANES], None) for b in range(RADIX)
        ]
        mixed = sixteen(values, -1)
        for f in range(RADIX):
            real, imag = mixed[f]
            if imag is None:
                imag = jnp.zeros_like(real)
            cos = twiddle[0, f : f + 1, :] * (1.0 / GRID)
            sin = twiddle[1, f : f + 1, :] * (1.0 / GRID)
            store_pair(
                held,
                pl.ds(f * LANES + at, chunk),
                real * cos + imag * sin,
                imag * cos - real * sin,
            )
        return carry

    lax.fori_loop(0, steps, body, 0)
    dims = ((1,), (1,))
    sent = []
    for g in range(RADIX // 2):
        pair = held[256 * g : 256 * g + 256, :]
        result = dot(table[:, :512], pair, dims) + dot(table[:, 512:], pair[:, :256], dims)
        for h in range(2):
            for c in range(2):
                block = result[c * LANES : (c + 1) * LANES, h * LANES : (h + 1) * LANES]
                out_v[:, c, 2 * g + h] = block.reshape(RADIX, 8, LANES)
        both = pl.ds(2 * g, 2)
        sent.append(fetched(out_v.at[:, :, both], out.at[:, :, both], sems.at[g]))
    for copy in sent:
        copy.wait()


def data_prepared(weights, measured, place, twiddle, out, forward, inverse, held):
    fill_table(forward, twiddle, -1, False)
    fill_table(inverse, twiddle, 1, False)
    for n in range(3):
        source = weights[...] if n == 0 else measured[n - 1]
        held[...] = source.astype(jnp.float32)
        for f in range(RADIX):
            rows = held[pl.ds(f, LANES, stride=RADIX), :].astype(jnp.bfloat16)
            out[n, f] = dot(place[...], rows, ((1,), (1,))).astype(jnp.bfloat16)


def columns(
    cols_in, data_in, twiddle_in, forward_in, inverse_in, out_all,
    cols, data, twiddle, forward, inverse, out, held_all, in_sems, chunk_sems, out_sems,
):
    chunk = 64
    steps = LANES // chunk
    dims = ((1,), (0,))

    def incoming_cols(step):
        rows = pl.ds(step * chunk, chunk)
        imag_rows = pl.ds(LANES + step * chunk, chunk)
        return [
            pltpu.make_async_copy(cols_in.at[:, r, :], cols.at[:, r, :], chunk_sems.at[step, n])
            for n, r in enumerate((rows, imag_rows))
        ]

    def incoming(step):
        rows = pl.ds(step * chunk, chunk)
        return pltpu.make_async_copy(
            data_in.at[:, :, rows, :], data.at[:, :, rows, :], chunk_sems.at[step, 2]
        )

    def outgoing(step, c):
        rows = pl.ds(c * LANES + step * chunk, chunk)
        return pltpu.make_async_copy(
            out.at[:, rows, :], out_all.at[:, rows, :], out_sems.at[step, c]
        )

    for copy in incoming_cols(0):
        copy.start()
    get_twiddle = fetched(twiddle_in, twiddle, in_sems.at[2])
    get_forward = fetched(forward_in, forward, in_sems.at[0])
    incoming(0).start()
    get_inverse = fetched(inverse_in, inverse, in_sems.at[1])
    for step in range(1, steps):
        for copy in incoming_cols(step):
            copy.start()
        incoming(step).start()
    out[:, 2 * LANES :, :] = jnp.zeros((RADIX, 8, LANES), jnp.float32)
    lane_at = lax.broadcasted_iota(jnp.int32, (8, LANES), 1)
    get_twiddle.wait()

    for step in range(steps):
        held = held_all.at[step % 2]
        at = step * chunk
        here = pl.ds(at, chunk)
        for copy in incoming_cols(step):
            copy.wait()
        imag_here = pl.ds(LANES + at, chunk)
        mixed = sixteen([(cols[b, here, :], cols[b, imag_here, :]) for b in range(RADIX)], -1)
        for f in range(RADIX):
            real, imag = mixed[f]
            cos, sin = twiddle[0, f : f + 1, :], twiddle[1, f : f + 1, :]
            rows = slice(f * chunk, (f + 1) * chunk)
            store_pair(held, rows, real * cos + imag * sin, imag * cos - real * sin)
        if step == 0:
            get_forward.wait()
            get_inverse.wait()
        spectrum = three_pass(held[...], forward, dims)
        incoming(step).wait()
        for f in range(RADIX):
            rows = slice(f * chunk, (f + 1) * chunk)
            weight = data[0, f, here, :].astype(jnp.float32)
            real = weight * spectrum[rows, :LANES] - data[1, f, here, :].astype(jnp.float32)
            imag = weight * spectrum[rows, LANES:] - data[2, f, here, :].astype(jnp.float32)
            store_pair(held, rows, real, imag)
        back = three_pass(held[...], inverse, dims)
        values = []
        for f in range(RADIX):
            rows = slice(f * chunk, (f + 1) * chunk)
            real, imag = back[rows, :LANES], back[rows, LANES:]
            cos, sin = twiddle[0, f : f + 1, :], twiddle[1, f : f + 1, :]
            values.append((real * cos - imag * sin, imag * cos + real * sin))
        mixed = sixteen(values, 1)
        for b in range(RADIX):
            for c in range(2):
                out[b, (here, imag_here)[c], :] = mixed[b][c]
                if b > 0:
                    edge = out[b - 1, 2 * LANES :, :]
                    for i in range(chunk // 8):
                        first = mixed[b][c][8 * i : 8 * i + 8, 0:1]
                        at_lane = lane_at == c * RADIX + step * (chunk // 8) + i
                        edge = jnp.where(at_lane, first, edge)
                    out[b - 1, 2 * LANES :, :] = edge
        for c in range(2):
            outgoing(step, c).start()
    rows = pl.ds(2 * LANES, 8)
    edges = fetched(out.at[:, rows, :], out_all.at[:, rows, :], in_sems.at[0])
    for step in range(steps):
        for c in range(2):
            outgoing(step, c).wait()
    edges.wait()


def tied(value, after_one, after_two, out):
    pass


def rows_back(lines, twiddle, after_one, after_two, out, held, side_v, table):
    fill_table(table, twiddle, 1, False)
    dims = ((0,), (0,))
    for f in range(RADIX):
        real = lines[:, 8 * f : 8 * f + 8, :].reshape(LANES, LANES)
        imag = lines[:, LANES + 8 * f : LANES + 8 * f + 8, :].reshape(LANES, LANES)
        high_r, low_r = split(real)
        high_i, low_i = split(imag)
        pair = jnp.concatenate([high_r, high_i, low_r, low_i], axis=0)
        held[f] = three_pass(pair, table, dims)
    high, low = split(lines[:, 2 * LANES :, :].reshape(LANES, LANES))
    edge = (
        dot(high, table[0:LANES, :], dims)
        + dot(low, table[0:LANES, :], dims)
        + dot(high, table[512 : 512 + LANES, :], dims)
    )
    edge_r = edge[:RADIX, :LANES] - edge[RADIX : 2 * RADIX, LANES:]
    edge_i = edge[:RADIX, LANES:] + edge[RADIX : 2 * RADIX, :LANES]
    scale = 1.0 / GRID
    cos, sin = twiddle[0, :RADIX] * scale, twiddle[1, :RADIX] * scale
    edge_r, edge_i = edge_r * cos - edge_i * sin, edge_i * cos + edge_r * sin
    mixed = sixteen([(edge_r[f : f + 1], edge_i[f : f + 1]) for f in range(RADIX)], 1)
    for d in range(CHANNELS):
        out[d, LANES : LANES + 1, :] = jnp.concatenate(
            [mixed[2 * d][0], mixed[2 * d + 1][0]], axis=1
        )
    chunk = 16
    steps = LANES // chunk
    lane_at = lax.broadcasted_iota(jnp.int32, (chunk, LANES), 1)

    def body(step, carry):
        at = pl.multiple_of(step * chunk, chunk)
        here = pl.ds(at, chunk)
        values = []
        for f in range(RADIX):
            real, imag = held[f, here, :LANES], held[f, here, LANES:]
            cos, sin = twiddle[0, f : f + 1, :] * scale, twiddle[1, f : f + 1, :] * scale
            values.append((real * cos - imag * sin, imag * cos + real * sin))
        mixed = sixteen(values, 1)
        side = jnp.zeros((chunk, LANES), jnp.float32)
        for b in range(RADIX):
            low_lane = (b % 2) * LANES
            out[b // 2, here, low_lane : low_lane + LANES] = mixed[b][0]
            if b > 0 and b % 2 == 0:
                side = jnp.where(lane_at == b // 2 - 1, mixed[b][0][:, 0:1], side)
        side_v[here, :] = side
        return carry

    lax.fori_loop(0, steps, body, 0)
    beside = side_v[...].T
    for d in range(CHANNELS):
        out[d, LANES + 1 : LANES + 2, :LANES] = beside[d : d + 1, :]


def dual_edges(dual, last_row, last_column):
    rows, cols = [], []
    for c in range(CHANNELS):
        rows.append(dual[c, 0, 112:128, :].astype(jnp.float32)[15:16, :])
        cols.append(dual[c, 1, :, LANES:].astype(jnp.float32)[:, LANES - 1 :])
    last_row[...] = jnp.concatenate(rows, axis=0)
    last_column[...] = jnp.concatenate(cols, axis=1).T


def tile_ready(where, *refs):
    pieces, (early, late, dual, above, left) = refs[:4], refs[4:9]
    for_image, for_ahead, first_row, first_column = refs[9:]
    row_at = lax.broadcasted_iota(jnp.int32, (LANES, 2 * LANES), 0)
    lane_at = lax.broadcasted_iota(jnp.int32, (LANES, 2 * LANES), 1)
    for k in range(4):
        for other in range(2):
            half = where[0] % 2
            c = (where[0] // 2 + 4 - k) % 4 * 2 + (1 - half if other else half)
            p = dual[c, 0].astype(jnp.float32)
            q = dual[c, 1].astype(jnp.float32)
            beside = jnp.broadcast_to(left[pl.ds(c, 1), :], (LANES, LANES)).T[:, 0:1]
            prev_p = jnp.where(row_at == 0, above[pl.ds(c, 1), :], pltpu.roll(p, 1, 0))
            prev_q = jnp.where(lane_at == 0, beside, pltpu.roll(q, 1, 1))
            adjoint = prev_p - p + prev_q - q
            if other:
                image = jnp.concatenate([early[k], late[k]], axis=0)
            else:
                image = pieces[k][:, pl.ds(pl.multiple_of(half * 256, 256), 256)]
            ahead = image - adjoint
            for_image[c] = image - step_primal * adjoint
            for_ahead[c] = ahead
            first_row[pl.ds(c, 1), :] = ahead[0:1, :]
            first_column[pl.ds(c, 1), :] = ahead[:, :LANES].T[0:1, :]


def finish(
    gradient, for_image, for_ahead, dual, below, right, image_next, dual_next,
    ahead_v, side_v, image_v, dual_v, image_sems, dual_sems,
):
    sides = []
    leaving = []
    for c in range(CHANNELS):
        slope = gradient[c, :LANES, :]
        image_v[c] = for_image[c] - step_primal * slope
        leaving.append(fetched(image_v.at[c], image_next.at[c], image_sems.at[c]))
        ahead_v[c, :LANES, :] = for_ahead[c] - slope
        ahead_v[c, LANES : LANES + 1, :] = (
            below[c : c + 1, :] - gradient[c, LANES : LANES + 1, :]
        )
        sides.append(gradient[c, LANES + 1 : LANES + 2, :LANES])
    side_v[:, :CHANNELS] = (right[...] - jnp.concatenate(sides, axis=0)).T
    chunk = 16
    steps = LANES // chunk
    row_at = lax.broadcasted_iota(jnp.int32, (chunk, 2 * LANES), 0)
    lane_at = lax.broadcasted_iota(jnp.int32, (chunk, 2 * LANES), 1)

    def outgoing(step):
        rows = pl.ds(pl.multiple_of(step * chunk, chunk), chunk)
        return pltpu.make_async_copy(
            dual_v.at[:, :, rows, :], dual_next.at[:, :, rows, :], dual_sems.at[step]
        )

    def body(step, carry):
        at = pl.multiple_of(step * chunk, chunk)
        here = pl.ds(at, chunk)
        after = pl.ds(pl.multiple_of(at + chunk, chunk), 8)
        firsts, seconds, total = [], [], None
        for c in range(CHANNELS):
            ahead = ahead_v[c, here, :]
            next_row = ahead_v[c, after, :][0:1, :]
            down = jnp.where(row_at == chunk - 1, next_row, pltpu.roll(ahead, chunk - 1, 0))
            beside = jnp.where(
                lane_at == 2 * LANES - 1,
                side_v[here, c : c + 1],
                pltpu.roll(ahead, 2 * LANES - 1, 1),
            )
            first = dual[c, 0, here, :].astype(jnp.float32) + step_dual * (down - ahead)
            second = dual[c, 1, here, :].astype(jnp.float32) + step_dual * (beside - ahead)
            firsts.append(first)
            seconds.append(second)
            squares = first * first + second * second
            total = squares if total is None else total + squares
        factor = 1.0 / jnp.maximum(1.0, jnp.sqrt(total) / clip_radius)
        for c in range(CHANNELS):
            dual_v[c, 0, here, :] = (firsts[c] * factor).astype(jnp.bfloat16)
            dual_v[c, 1, here, :] = (seconds[c] * factor).astype(jnp.bfloat16)
        outgoing(step).start()
        return carry

    lax.fori_loop(0, steps, body, 0)
    for copy in leaving:
        copy.wait()
    for step in range(steps):
        outgoing(step).wait()


def shape(dims, dtype=jnp.float32):
    return jax.ShapeDtypeStruct(dims, dtype)


def passed_along(x, axis, by):
    devices = lax.axis_size(axis)
    pairs = [(i, i + by) for i in range(devices) if 0 <= i + by < devices]
    return lax.ppermute(x, axis, pairs)


ANY = pl.BlockSpec(memory_space=pl.ANY)
HBM = pl.BlockSpec(memory_space=pltpu.HBM)
VM = pl.BlockSpec(memory_space=pltpu.VMEM)
SM = pl.BlockSpec(memory_space=pltpu.SMEM)
DMA = pltpu.SemaphoreType.DMA


def call(kernel, out_shape, in_specs, out_specs, scratch, limit=16):
    return pl.pallas_call(
        kernel,
        out_shape=out_shape,
        in_specs=in_specs,
        out_specs=out_specs,
        scratch_shapes=scratch,
        name=kernel.__name__,
        compiler_params=pltpu.CompilerParams(vmem_limit_bytes=limit * MIB),
    )


def shards(image_field, weights, measured, dual_field):
    twiddle, place = host_tables()
    place = jnp.asarray(place, jnp.bfloat16)
    twiddle = jnp.asarray(twiddle)
    image = image_field[0]
    f32, bf16 = jnp.float32, jnp.bfloat16
    where = lax.axis_index("chan").astype(jnp.int32).reshape(1)

    spread = call(
        rows_forward,
        shape((RADIX, 2, RADIX, 8, LANES)),
        [HBM, HBM],
        HBM,
        [
            pltpu.VMEM((LANES, GRID), f32),
            pltpu.VMEM((2, RADIX + 8, LANES), f32),
            pltpu.VMEM((RADIX, 2, RADIX, 8, LANES), f32),
            pltpu.VMEM((GRID, 512), bf16),
            pltpu.VMEM((256, 768), bf16),
            DMA((9,)),
            DMA((8,)),
        ],
        63,
    )(image, twiddle)
    cols = lax.all_to_all(
        spread.reshape(RADIX, 2 * LANES, LANES), "facet", split_axis=0, concat_axis=0, tiled=True
    )
    last_row, last_column = call(
        dual_edges,
        (shape((CHANNELS, 2 * LANES)), shape((CHANNELS, LANES))),
        [VM],
        (VM, VM),
        [],
    )(dual_field)
    above = passed_along(last_row, "facet", 1)
    left = passed_along(last_column, "chan", 1)
    pieces = list(
        call(cross_ready, (shape((LANES, 512)),) * 4, [SM, VM], (VM,) * 4, [])(where, image)
    )
    for k in range(1, 4):
        pairs = [(2 * x + z, (x + k) % 4 * 2 + z) for x in range(4) for z in range(2)]
        pieces[k] = lax.ppermute(pieces[k], "chan", pairs)
    early, late = call(
        swap_ready, (shape((4, LANES // 2, 256)),) * 2, [SM] + [VM] * 4, (VM, VM), []
    )(where, *pieces)
    other_zl = [(i, i ^ 1) for i in range(8)]
    early = lax.ppermute(early, "chan", other_zl)
    data, forward, inverse = call(
        data_prepared,
        (
            shape((3, RADIX, LANES, LANES), bf16),
            shape((768, 256), bf16),
            shape((768, 256), bf16),
        ),
        [VM] * 4,
        (VM,) * 3,
        [pltpu.VMEM((GRID, LANES), f32)],
        63,
    )(weights[0], measured[0], place, twiddle)
    cols, late, above, left, data, forward, inverse = lax.optimization_barrier(
        (cols, late, above, left, data, forward, inverse)
    )
    late = lax.ppermute(late, "chan", other_zl)
    data, forward, inverse = (
        pltpu.with_memory_space_constraint(x, pltpu.HBM) for x in (data, forward, inverse)
    )
    back = call(
        columns,
        shape((RADIX, 2 * LANES + 8, LANES)),
        [HBM] * 5,
        HBM,
        [
            pltpu.VMEM((RADIX, 2 * LANES, LANES), f32),
            pltpu.VMEM((3, RADIX, LANES, LANES), bf16),
            pltpu.VMEM((2, RADIX + 8, LANES), f32),
            pltpu.VMEM((768, 256), bf16),
            pltpu.VMEM((768, 256), bf16),
            pltpu.VMEM((RADIX, 2 * LANES + 8, LANES), f32),
            pltpu.VMEM((2, RADIX * 64, 512), bf16),
            DMA((3,)),
            DMA((2, 3)),
            DMA((2, 2)),
        ],
        63,
    )(cols, data, twiddle, forward, inverse)
    back = pl.pallas_call(
        tied,
        out_shape=shape((RADIX, 2 * LANES + 8, LANES)),
        in_specs=[ANY] * 3,
        out_specs=ANY,
        input_output_aliases={0: 0},
        name="tied",
    )(back, early[0, :8, :LANES], late[0, :8, :LANES])
    lines = lax.all_to_all(back, "facet", split_axis=0, concat_axis=0, tiled=True)
    for_image, for_ahead, first_row, first_column = call(
        tile_ready,
        (
            shape((CHANNELS, LANES, 2 * LANES)),
            shape((CHANNELS, LANES, 2 * LANES)),
            shape((CHANNELS, 2 * LANES)),
            shape((CHANNELS, LANES)),
        ),
        [SM] + [VM] * 9,
        (VM,) * 4,
        [],
    )(where, *pieces, early, late, dual_field, above, left)
    below = passed_along(first_row, "facet", -1)
    right = passed_along(first_column, "chan", -1)
    slopes = call(
        rows_back,
        shape((CHANNELS, LANES + 8, 2 * LANES)),
        [VM] * 2 + [ANY] * 2,
        VM,
        [
            pltpu.VMEM((RADIX, LANES, 256), f32),
            pltpu.VMEM((LANES, LANES), f32),
            pltpu.VMEM((768, 256), bf16),
        ],
    )(lines, twiddle, below, right)
    gradient = lax.all_to_all(slopes, "chan", split_axis=0, concat_axis=0, tiled=True)
    return call(
        finish,
        (shape((CHANNELS, LANES, 2 * LANES)), shape((CHANNELS, 2, LANES, 2 * LANES), bf16)),
        [VM] * 6,
        (HBM, HBM),
        [
            pltpu.VMEM((CHANNELS, LANES + 8, 2 * LANES), f32),
            pltpu.VMEM((LANES, LANES), f32),
            pltpu.VMEM((CHANNELS, LANES, 2 * LANES), f32),
            pltpu.VMEM((CHANNELS, 2, LANES, 2 * LANES), bf16),
            DMA((8,)),
            DMA((8,)),
        ],
    )(gradient, for_image, for_ahead, dual_field, below, right)


def solution(mesh):
    placed = (
        P("chan", "facet", None),
        P("chan", None, "facet"),
        P("chan", None, None, "facet"),
        P(None, None, "facet", "chan"),
    )
    return jax.shard_map(
        shards,
        mesh=mesh,
        in_specs=placed,
        out_specs=(P(None, "facet", "chan"), P(None, None, "facet", "chan")),
        check_vma=False,
    )
```

```python
from functools import partial
import math

import jax
import jax.numpy as jnp
import numpy as np
from jax import lax
from jax.experimental import pallas as pl
from jax.experimental.pallas import tpu as pltpu
from jax.sharding import PartitionSpec as P

GRID = 2048
RADIX = 16
LANES = 128
CHANNELS = 8

step_primal = 0.5
step_dual = 0.5
clip_radius = 4.0

MIB = 1024 * 1024


def host_tables():
    index = np.arange(LANES)
    turn = 2.0 * np.pi * np.arange(RADIX + 8)[:, None] * index[None, :] / GRID
    twiddle = np.stack([np.cos(turn), np.sin(turn)]).astype(np.float32)
    place = np.zeros((LANES, LANES))
    for at in range(LANES):
        place[at, 16 * (at % 8) + at // 8] = 1.0
    return twiddle, place


def c_add(a, b):
    return (a[0] + b[0], b[1] if a[1] is None else a[1] if b[1] is None else a[1] + b[1])


def c_sub(a, b):
    imag = None
    if a[1] is not None and b[1] is not None:
        imag = a[1] - b[1]
    elif a[1] is not None:
        imag = a[1]
    elif b[1] is not None:
        imag = -b[1]
    return (a[0] - b[0], imag)


def add_turned(a, b, sign):
    real = a[0] if b[1] is None else (a[0] - b[1] if sign > 0 else a[0] + b[1])
    if a[1] is None:
        imag = b[0] if sign > 0 else -b[0]
    else:
        imag = a[1] + b[0] if sign > 0 else a[1] - b[0]
    return (real, imag)


def four(a, b, c, d, sign):
    sum_even, diff_even = c_add(a, c), c_sub(a, c)
    sum_odd, diff_odd = c_add(b, d), c_sub(b, d)
    return (
        c_add(sum_even, sum_odd),
        add_turned(diff_even, diff_odd, sign),
        c_sub(sum_even, sum_odd),
        add_turned(diff_even, diff_odd, -sign),
    )


def turned(a, power, sign):
    power = power % 16
    if power == 0:
        return a
    cos, sin = math.cos(2 * math.pi * power / 16), sign * math.sin(2 * math.pi * power / 16)
    real, imag = a
    if imag is None:
        if power == 4:
            return (jnp.zeros_like(real), real if sign > 0 else -real)
        return (real * cos, real * sin)
    if power == 4:
        return (-imag, real) if sign > 0 else (imag, -real)
    if abs(abs(cos) - abs(sin)) < 1e-9:
        root = math.sqrt(0.5)
        cs, ss = (1 if cos > 0 else -1), (1 if sin > 0 else -1)
        new_real = (real if cs > 0 else -real) - (imag if ss > 0 else -imag)
        new_imag = (real if ss > 0 else -real) + (imag if cs > 0 else -imag)
        return (new_real * root, new_imag * root)
    return (real * cos - imag * sin, real * sin + imag * cos)


def sixteen(values, sign):
    inner = [four(*(values[n0 + 4 * n1] for n1 in range(4)), sign) for n0 in range(4)]
    out = [None] * 16
    for k1 in range(4):
        parts = [turned(inner[n0][k1], n0 * k1, sign) for n0 in range(4)]
        for k2, value in enumerate(four(*parts, sign)):
            out[k1 + 4 * k2] = value
    return out


def split(value):
    high = value.astype(jnp.bfloat16)
    low = (value - high.astype(jnp.float32)).astype(jnp.bfloat16)
    return high, low


def dot(a, b, dims):
    return lax.dot_general(a, b, (dims, ((), ())), preferred_element_type=jnp.float32)


def fetched(source, target, semaphore):
    copy = pltpu.make_async_copy(source, target, semaphore)
    copy.start()
    return copy


def fill_table(table, twiddle, sign, transposed):
    shape = (LANES, LANES)
    row, col = (lax.broadcasted_iota(jnp.int32, shape, n) for n in range(2))
    at = jnp.bitwise_and(row * col, LANES - 1)
    cos, sin = (
        jnp.take_along_axis(
            jnp.broadcast_to(twiddle[n, RADIX : RADIX + 1, :], shape), at, axis=1
        )
        for n in range(2)
    )
    for n, value in enumerate((cos, sign * sin, -sign * sin, cos)):
        high, low = split(value)
        into, out = ((n // 2, n % 2), (n % 2, n // 2))[transposed]
        for m, half in enumerate((high, high, low)):
            if transposed:
                lane = 256 * m + LANES * out
                table[LANES * into : LANES * into + LANES, lane : lane + LANES] = half
            else:
                at_row = 256 * m + LANES * into
                table[at_row : at_row + LANES, LANES * out : LANES * out + LANES] = half


def three_pass(pair, table, dims):
    high = pair[:, :256] if dims[0][0] == 1 else pair[:256, :]
    return dot(pair, table[:512, :], dims) + dot(high, table[512:, :], dims)


def store_pair(held, rows, real, imag):
    high_r, low_r = split(real)
    high_i, low_i = split(imag)
    held[rows, 0:LANES] = high_r
    held[rows, LANES : 2 * LANES] = high_i
    held[rows, 2 * LANES : 3 * LANES] = low_r
    held[rows, 3 * LANES : 4 * LANES] = low_i


def cross_ready(where, image, *pieces):
    for k in range(4):
        to = (where[0] // 2 + k) % 4
        pieces[k][...] = image[:, pl.ds(pl.multiple_of(to * 512, 512), 512)]


def swap_ready(where, *refs):
    pieces, early, late = refs[:4], refs[-2], refs[-1]
    lanes = pl.ds(pl.multiple_of((1 - where[0] % 2) * 256, 256), 256)
    for k in range(4):
        early[k] = pieces[k][: LANES // 2, lanes]
        late[k] = pieces[k][LANES // 2 :, lanes]


def rows_forward(
    image_in, twiddle_in, out, image, twiddle, out_v, held, table, in_sems, sems
):
    chunk = 16
    steps = LANES // chunk

    def incoming(step):
        rows = pl.ds(pl.multiple_of(step * chunk, chunk), chunk)
        return pltpu.make_async_copy(image_in.at[rows, :], image.at[rows, :], in_sems.at[step])

    get_twiddle = fetched(twiddle_in, twiddle, in_sems.at[steps])
    for step in range(steps):
        incoming(step).start()
    get_twiddle.wait()
    fill_table(table, twiddle, -1, True)

    def body(step, carry):
        incoming(step).wait()
        at = pl.multiple_of(step * chunk, chunk)
        values = [
            (image[pl.ds(at, chunk), b * LANES : (b + 1) * LANES], None) for b in range(RADIX)
        ]
        mixed = sixteen(values, -1)
        for f in range(RADIX):
            real, imag = mixed[f]
            if imag is None:
                imag = jnp.zeros_like(real)
            cos = twiddle[0, f : f + 1, :] * (1.0 / GRID)
            sin = twiddle[1, f : f + 1, :] * (1.0 / GRID)
            store_pair(
                held,
                pl.ds(f * LANES + at, chunk),
                real * cos + imag * sin,
                imag * cos - real * sin,
            )
        return carry

    lax.fori_loop(0, steps, body, 0)
    dims = ((1,), (1,))
    sent = []
    for g in range(RADIX // 2):
        pair = held[256 * g : 256 * g + 256, :]
        result = dot(table[:, :512], pair, dims) + dot(table[:, 512:], pair[:, :256], dims)
        for h in range(2):
            for c in range(2):
                block = result[c * LANES : (c + 1) * LANES, h * LANES : (h + 1) * LANES]
                out_v[:, c, 2 * g + h] = block.reshape(RADIX, 8, LANES)
        both = pl.ds(2 * g, 2)
        sent.append(fetched(out_v.at[:, :, both], out.at[:, :, both], sems.at[g]))
    for copy in sent:
        copy.wait()


def data_prepared(weights, measured, place, twiddle, out, forward, inverse, held):
    fill_table(forward, twiddle, -1, False)
    fill_table(inverse, twiddle, 1, False)
    for n in range(3):
        source = weights[...] if n == 0 else measured[n - 1]
        held[...] = source.astype(jnp.float32)
        for f in range(RADIX):
            rows = held[pl.ds(f, LANES, stride=RADIX), :].astype(jnp.bfloat16)
            out[n, f] = dot(place[...], rows, ((1,), (1,))).astype(jnp.bfloat16)


def columns(
    cols_in, data_in, twiddle_in, forward_in, inverse_in, out_all,
    cols, data, twiddle, forward, inverse, out, held_all, in_sems, chunk_sems, out_sems,
):
    chunk = 64
    steps = LANES // chunk
    dims = ((1,), (0,))

    def incoming_cols(step):
        rows = pl.ds(step * chunk, chunk)
        imag_rows = pl.ds(LANES + step * chunk, chunk)
        return [
            pltpu.make_async_copy(cols_in.at[:, r, :], cols.at[:, r, :], chunk_sems.at[step, n])
            for n, r in enumerate((rows, imag_rows))
        ]

    def incoming(step):
        rows = pl.ds(step * chunk, chunk)
        return pltpu.make_async_copy(
            data_in.at[:, :, rows, :], data.at[:, :, rows, :], chunk_sems.at[step, 2]
        )

    def outgoing(step, c):
        rows = pl.ds(c * LANES + step * chunk, chunk)
        return pltpu.make_async_copy(
            out.at[:, rows, :], out_all.at[:, rows, :], out_sems.at[step, c]
        )

    for copy in incoming_cols(0):
        copy.start()
    get_twiddle = fetched(twiddle_in, twiddle, in_sems.at[2])
    get_forward = fetched(forward_in, forward, in_sems.at[0])
    incoming(0).start()
    get_inverse = fetched(inverse_in, inverse, in_sems.at[1])
    for step in range(1, steps):
        for copy in incoming_cols(step):
            copy.start()
        incoming(step).start()
    out[:, 2 * LANES :, :] = jnp.zeros((RADIX, 8, LANES), jnp.float32)
    lane_at = lax.broadcasted_iota(jnp.int32, (8, LANES), 1)
    get_twiddle.wait()

    for step in range(steps):
        held = held_all.at[step % 2]
        at = step * chunk
        here = pl.ds(at, chunk)
        for copy in incoming_cols(step):
            copy.wait()
        imag_here = pl.ds(LANES + at, chunk)
        mixed = sixteen([(cols[b, here, :], cols[b, imag_here, :]) for b in range(RADIX)], -1)
        for f in range(RADIX):
            real, imag = mixed[f]
            cos, sin = twiddle[0, f : f + 1, :], twiddle[1, f : f + 1, :]
            rows = slice(f * chunk, (f + 1) * chunk)
            store_pair(held, rows, real * cos + imag * sin, imag * cos - real * sin)
        if step == 0:
            get_forward.wait()
            get_inverse.wait()
        spectrum = three_pass(held[...], forward, dims)
        incoming(step).wait()
        for f in range(RADIX):
            rows = slice(f * chunk, (f + 1) * chunk)
            weight = data[0, f, here, :].astype(jnp.float32)
            real = weight * spectrum[rows, :LANES] - data[1, f, here, :].astype(jnp.float32)
            imag = weight * spectrum[rows, LANES:] - data[2, f, here, :].astype(jnp.float32)
            store_pair(held, rows, real, imag)
        back = three_pass(held[...], inverse, dims)
        values = []
        for f in range(RADIX):
            rows = slice(f * chunk, (f + 1) * chunk)
            real, imag = back[rows, :LANES], back[rows, LANES:]
            cos, sin = twiddle[0, f : f + 1, :], twiddle[1, f : f + 1, :]
            values.append((real * cos - imag * sin, imag * cos + real * sin))
        mixed = sixteen(values, 1)
        for b in range(RADIX):
            for c in range(2):
                out[b, (here, imag_here)[c], :] = mixed[b][c]
                if b > 0:
                    edge = out[b - 1, 2 * LANES :, :]
                    for i in range(chunk // 8):
                        first = mixed[b][c][8 * i : 8 * i + 8, 0:1]
                        at_lane = lane_at == c * RADIX + step * (chunk // 8) + i
                        edge = jnp.where(at_lane, first, edge)
                    out[b - 1, 2 * LANES :, :] = edge
        for c in range(2):
            outgoing(step, c).start()
    rows = pl.ds(2 * LANES, 8)
    edges = fetched(out.at[:, rows, :], out_all.at[:, rows, :], in_sems.at[0])
    for step in range(steps):
        for c in range(2):
            outgoing(step, c).wait()
    edges.wait()


def tied(value, after, out):
    pass


def rows_back(lines, twiddle, after_one, after_two, out, held, side_v, table):
    fill_table(table, twiddle, 1, False)
    dims = ((0,), (0,))
    for f in range(RADIX):
        real = lines[:, 8 * f : 8 * f + 8, :].reshape(LANES, LANES)
        imag = lines[:, LANES + 8 * f : LANES + 8 * f + 8, :].reshape(LANES, LANES)
        high_r, low_r = split(real)
        high_i, low_i = split(imag)
        pair = jnp.concatenate([high_r, high_i, low_r, low_i], axis=0)
        held[f] = three_pass(pair, table, dims)
    high, low = split(lines[:, 2 * LANES :, :].reshape(LANES, LANES))
    edge = (
        dot(high, table[0:LANES, :], dims)
        + dot(low, table[0:LANES, :], dims)
        + dot(high, table[512 : 512 + LANES, :], dims)
    )
    edge_r = edge[:RADIX, :LANES] - edge[RADIX : 2 * RADIX, LANES:]
    edge_i = edge[:RADIX, LANES:] + edge[RADIX : 2 * RADIX, :LANES]
    scale = 1.0 / GRID
    cos, sin = twiddle[0, :RADIX] * scale, twiddle[1, :RADIX] * scale
    edge_r, edge_i = edge_r * cos - edge_i * sin, edge_i * cos + edge_r * sin
    mixed = sixteen([(edge_r[f : f + 1], edge_i[f : f + 1]) for f in range(RADIX)], 1)
    for d in range(CHANNELS):
        out[d, LANES : LANES + 1, :] = jnp.concatenate(
            [mixed[2 * d][0], mixed[2 * d + 1][0]], axis=1
        )
    chunk = 16
    steps = LANES // chunk
    lane_at = lax.broadcasted_iota(jnp.int32, (chunk, LANES), 1)

    def body(step, carry):
        at = pl.multiple_of(step * chunk, chunk)
        here = pl.ds(at, chunk)
        values = []
        for f in range(RADIX):
            real, imag = held[f, here, :LANES], held[f, here, LANES:]
            cos, sin = twiddle[0, f : f + 1, :] * scale, twiddle[1, f : f + 1, :] * scale
            values.append((real * cos - imag * sin, imag * cos + real * sin))
        mixed = sixteen(values, 1)
        side = jnp.zeros((chunk, LANES), jnp.float32)
        for b in range(RADIX):
            low_lane = (b % 2) * LANES
            out[b // 2, here, low_lane : low_lane + LANES] = mixed[b][0]
            if b > 0 and b % 2 == 0:
                side = jnp.where(lane_at == b // 2 - 1, mixed[b][0][:, 0:1], side)
        side_v[here, :] = side
        return carry

    lax.fori_loop(0, steps, body, 0)
    beside = side_v[...].T
    for d in range(CHANNELS):
        out[d, LANES + 1 : LANES + 2, :LANES] = beside[d : d + 1, :]


def dual_edges(dual, last_row, last_column):
    rows, cols = [], []
    for c in range(CHANNELS):
        rows.append(dual[c, 0, 112:128, :].astype(jnp.float32)[15:16, :])
        cols.append(dual[c, 1, :, LANES:].astype(jnp.float32)[:, LANES - 1 :])
    last_row[...] = jnp.concatenate(rows, axis=0)
    last_column[...] = jnp.concatenate(cols, axis=1).T


def tile_ready(where, *refs):
    pieces, (early, late, dual, above, left) = refs[:4], refs[4:9]
    for_image, for_ahead, first_row, first_column = refs[9:]
    row_at = lax.broadcasted_iota(jnp.int32, (LANES, 2 * LANES), 0)
    lane_at = lax.broadcasted_iota(jnp.int32, (LANES, 2 * LANES), 1)
    for k in range(4):
        for other in range(2):
            half = where[0] % 2
            c = (where[0] // 2 + 4 - k) % 4 * 2 + (1 - half if other else half)
            p = dual[c, 0].astype(jnp.float32)
            q = dual[c, 1].astype(jnp.float32)
            beside = jnp.broadcast_to(left[pl.ds(c, 1), :], (LANES, LANES)).T[:, 0:1]
            prev_p = jnp.where(row_at == 0, above[pl.ds(c, 1), :], pltpu.roll(p, 1, 0))
            prev_q = jnp.where(lane_at == 0, beside, pltpu.roll(q, 1, 1))
            adjoint = prev_p - p + prev_q - q
            if other:
                image = jnp.concatenate([early[k], late[k]], axis=0)
            else:
                image = pieces[k][:, pl.ds(pl.multiple_of(half * 256, 256), 256)]
            ahead = image - adjoint
            for_image[c] = image - step_primal * adjoint
            for_ahead[c] = ahead
            first_row[pl.ds(c, 1), :] = ahead[0:1, :]
            first_column[pl.ds(c, 1), :] = ahead[:, :LANES].T[0:1, :]


def finish(
    gradient, for_image, for_ahead, dual, below, right, image_next, dual_next,
    ahead_v, side_v, image_v, dual_v, image_sems, dual_sems,
):
    sides = []
    leaving = []
    for c in range(CHANNELS):
        slope = gradient[c, :LANES, :]
        image_v[c] = for_image[c] - step_primal * slope
        leaving.append(fetched(image_v.at[c], image_next.at[c], image_sems.at[c]))
        ahead_v[c, :LANES, :] = for_ahead[c] - slope
        ahead_v[c, LANES : LANES + 1, :] = (
            below[c : c + 1, :] - gradient[c, LANES : LANES + 1, :]
        )
        sides.append(gradient[c, LANES + 1 : LANES + 2, :LANES])
    side_v[:, :CHANNELS] = (right[...] - jnp.concatenate(sides, axis=0)).T
    chunk = 16
    steps = LANES // chunk
    row_at = lax.broadcasted_iota(jnp.int32, (chunk, 2 * LANES), 0)
    lane_at = lax.broadcasted_iota(jnp.int32, (chunk, 2 * LANES), 1)

    def outgoing(step):
        rows = pl.ds(pl.multiple_of(step * chunk, chunk), chunk)
        return pltpu.make_async_copy(
            dual_v.at[:, :, rows, :], dual_next.at[:, :, rows, :], dual_sems.at[step]
        )

    def body(step, carry):
        at = pl.multiple_of(step * chunk, chunk)
        here = pl.ds(at, chunk)
        after = pl.ds(pl.multiple_of(at + chunk, chunk), 8)
        firsts, seconds, total = [], [], None
        for c in range(CHANNELS):
            ahead = ahead_v[c, here, :]
            next_row = ahead_v[c, after, :][0:1, :]
            down = jnp.where(row_at == chunk - 1, next_row, pltpu.roll(ahead, chunk - 1, 0))
            beside = jnp.where(
                lane_at == 2 * LANES - 1,
                side_v[here, c : c + 1],
                pltpu.roll(ahead, 2 * LANES - 1, 1),
            )
            first = dual[c, 0, here, :].astype(jnp.float32) + step_dual * (down - ahead)
            second = dual[c, 1, here, :].astype(jnp.float32) + step_dual * (beside - ahead)
            firsts.append(first)
            seconds.append(second)
            squares = first * first + second * second
            total = squares if total is None else total + squares
        factor = 1.0 / jnp.maximum(1.0, jnp.sqrt(total) / clip_radius)
        for c in range(CHANNELS):
            dual_v[c, 0, here, :] = (firsts[c] * factor).astype(jnp.bfloat16)
            dual_v[c, 1, here, :] = (seconds[c] * factor).astype(jnp.bfloat16)
        outgoing(step).start()
        return carry

    lax.fori_loop(0, steps, body, 0)
    for copy in leaving:
        copy.wait()
    for step in range(steps):
        outgoing(step).wait()


def shape(dims, dtype=jnp.float32):
    return jax.ShapeDtypeStruct(dims, dtype)


def passed_along(x, axis, by):
    devices = lax.axis_size(axis)
    pairs = [(i, i + by) for i in range(devices) if 0 <= i + by < devices]
    return lax.ppermute(x, axis, pairs)


ANY = pl.BlockSpec(memory_space=pl.ANY)
HBM = pl.BlockSpec(memory_space=pltpu.HBM)
VM = pl.BlockSpec(memory_space=pltpu.VMEM)
SM = pl.BlockSpec(memory_space=pltpu.SMEM)
DMA = pltpu.SemaphoreType.DMA


def call(kernel, out_shape, in_specs, out_specs, scratch, limit=16):
    return pl.pallas_call(
        kernel,
        out_shape=out_shape,
        in_specs=in_specs,
        out_specs=out_specs,
        scratch_shapes=scratch,
        name=kernel.__name__,
        compiler_params=pltpu.CompilerParams(vmem_limit_bytes=limit * MIB),
    )


def shards(image_field, weights, measured, dual_field):
    twiddle, place = host_tables()
    place = jnp.asarray(place, jnp.bfloat16)
    twiddle = jnp.asarray(twiddle)
    image = image_field[0]
    f32, bf16 = jnp.float32, jnp.bfloat16
    where = lax.axis_index("chan").astype(jnp.int32).reshape(1)

    spread = call(
        rows_forward,
        shape((RADIX, 2, RADIX, 8, LANES)),
        [HBM, HBM],
        HBM,
        [
            pltpu.VMEM((LANES, GRID), f32),
            pltpu.VMEM((2, RADIX + 8, LANES), f32),
            pltpu.VMEM((RADIX, 2, RADIX, 8, LANES), f32),
            pltpu.VMEM((GRID, 512), bf16),
            pltpu.VMEM((256, 768), bf16),
            DMA((9,)),
            DMA((8,)),
        ],
        63,
    )(image, twiddle)
    cols = lax.all_to_all(
        spread.reshape(RADIX, 2 * LANES, LANES), "facet", split_axis=0, concat_axis=0, tiled=True
    )
    last_row, last_column = call(
        dual_edges,
        (shape((CHANNELS, 2 * LANES)), shape((CHANNELS, LANES))),
        [VM],
        (VM, VM),
        [],
    )(dual_field)
    above = passed_along(last_row, "facet", 1)
    left = passed_along(last_column, "chan", 1)
    pieces = list(
        call(cross_ready, (shape((LANES, 512)),) * 4, [SM, VM], (VM,) * 4, [])(where, image)
    )
    for k in range(1, 4):
        pairs = [(2 * x + z, (x + k) % 4 * 2 + z) for x in range(4) for z in range(2)]
        pieces[k] = lax.ppermute(pieces[k], "chan", pairs)
    data, forward, inverse = call(
        data_prepared,
        (
            shape((3, RADIX, LANES, LANES), bf16),
            shape((768, 256), bf16),
            shape((768, 256), bf16),
        ),
        [VM] * 4,
        (VM,) * 3,
        [pltpu.VMEM((GRID, LANES), f32)],
        63,
    )(weights[0], measured[0], place, twiddle)
    early, late = call(
        swap_ready,
        (shape((4, LANES // 2, 256)),) * 2,
        [SM] + [VM] * 4 + [ANY] * 2,
        (VM, VM),
        [],
    )(where, *pieces, data, last_row)
    other_zl = [(i, i ^ 1) for i in range(8)]
    early = lax.ppermute(early, "chan", other_zl)
    cols, late, above, left, data, forward, inverse = lax.optimization_barrier(
        (cols, late, above, left, data, forward, inverse)
    )
    late = lax.ppermute(late, "chan", other_zl)
    data, forward, inverse = (
        pltpu.with_memory_space_constraint(x, pltpu.HBM) for x in (data, forward, inverse)
    )
    back = call(
        columns,
        shape((RADIX, 2 * LANES + 8, LANES)),
        [HBM] * 5,
        HBM,
        [
            pltpu.VMEM((RADIX, 2 * LANES, LANES), f32),
            pltpu.VMEM((3, RADIX, LANES, LANES), bf16),
            pltpu.VMEM((2, RADIX + 8, LANES), f32),
            pltpu.VMEM((768, 256), bf16),
            pltpu.VMEM((768, 256), bf16),
            pltpu.VMEM((RADIX, 2 * LANES + 8, LANES), f32),
            pltpu.VMEM((2, RADIX * 64, 512), bf16),
            DMA((3,)),
            DMA((2, 3)),
            DMA((2, 2)),
        ],
        63,
    )(cols, data, twiddle, forward, inverse)
    back = pl.pallas_call(
        tied,
        out_shape=shape((RADIX, 2 * LANES + 8, LANES)),
        in_specs=[ANY] * 2,
        out_specs=ANY,
        input_output_aliases={0: 0},
        name="tied",
    )(back, early[0, :8, :LANES] + late[0, :8, :LANES])
    lines = lax.all_to_all(back, "facet", split_axis=0, concat_axis=0, tiled=True)
    for_image, for_ahead, first_row, first_column = call(
        tile_ready,
        (
            shape((CHANNELS, LANES, 2 * LANES)),
            shape((CHANNELS, LANES, 2 * LANES)),
            shape((CHANNELS, 2 * LANES)),
            shape((CHANNELS, LANES)),
        ),
        [SM] + [VM] * 9,
        (VM,) * 4,
        [],
    )(where, *pieces, early, late, dual_field, above, left)
    below = passed_along(first_row, "facet", -1)
    right = passed_along(first_column, "chan", -1)
    slopes = call(
        rows_back,
        shape((CHANNELS, LANES + 8, 2 * LANES)),
        [VM] * 2 + [ANY] * 2,
        VM,
        [
            pltpu.VMEM((RADIX, LANES, 256), f32),
            pltpu.VMEM((LANES, LANES), f32),
            pltpu.VMEM((768, 256), bf16),
        ],
    )(lines, twiddle, below, right)
    gradient = lax.all_to_all(slopes, "chan", split_axis=0, concat_axis=0, tiled=True)
    return call(
        finish,
        (shape((CHANNELS, LANES, 2 * LANES)), shape((CHANNELS, 2, LANES, 2 * LANES), bf16)),
        [VM] * 6,
        (HBM, HBM),
        [
            pltpu.VMEM((CHANNELS, LANES + 8, 2 * LANES), f32),
            pltpu.VMEM((LANES, LANES), f32),
            pltpu.VMEM((CHANNELS, LANES, 2 * LANES), f32),
            pltpu.VMEM((CHANNELS, 2, LANES, 2 * LANES), bf16),
            DMA((8,)),
            DMA((8,)),
        ],
    )(gradient, for_image, for_ahead, dual_field, below, right)


def solution(mesh):
    placed = (
        P("chan", "facet", None),
        P("chan", None, "facet"),
        P("chan", None, None, "facet"),
        P(None, None, "facet", "chan"),
    )
    return jax.shard_map(
        shards,
        mesh=mesh,
        in_specs=placed,
        out_specs=(P(None, "facet", "chan"), P(None, None, "facet", "chan")),
        check_vma=False,
    )
```

```python
from functools import partial
import math

import jax
import jax.numpy as jnp
import numpy as np
from jax import lax
from jax.experimental import pallas as pl
from jax.experimental.pallas import tpu as pltpu
from jax.sharding import PartitionSpec as P

GRID = 2048
RADIX = 16
LANES = 128
CHANNELS = 8
EARLY = 80

step_primal = 0.5
step_dual = 0.5
clip_radius = 4.0

MIB = 1024 * 1024


def host_tables():
    index = np.arange(LANES)
    turn = 2.0 * np.pi * np.arange(RADIX + 8)[:, None] * index[None, :] / GRID
    twiddle = np.stack([np.cos(turn), np.sin(turn)]).astype(np.float32)
    place = np.zeros((LANES, LANES))
    for at in range(LANES):
        place[at, 16 * (at % 8) + at // 8] = 1.0
    return twiddle, place


def c_add(a, b):
    return (a[0] + b[0], b[1] if a[1] is None else a[1] if b[1] is None else a[1] + b[1])


def c_sub(a, b):
    imag = None
    if a[1] is not None and b[1] is not None:
        imag = a[1] - b[1]
    elif a[1] is not None:
        imag = a[1]
    elif b[1] is not None:
        imag = -b[1]
    return (a[0] - b[0], imag)


def add_turned(a, b, sign):
    real = a[0] if b[1] is None else (a[0] - b[1] if sign > 0 else a[0] + b[1])
    if a[1] is None:
        imag = b[0] if sign > 0 else -b[0]
    else:
        imag = a[1] + b[0] if sign > 0 else a[1] - b[0]
    return (real, imag)


def four(a, b, c, d, sign):
    sum_even, diff_even = c_add(a, c), c_sub(a, c)
    sum_odd, diff_odd = c_add(b, d), c_sub(b, d)
    return (
        c_add(sum_even, sum_odd),
        add_turned(diff_even, diff_odd, sign),
        c_sub(sum_even, sum_odd),
        add_turned(diff_even, diff_odd, -sign),
    )


def turned(a, power, sign):
    power = power % 16
    if power == 0:
        return a
    cos, sin = math.cos(2 * math.pi * power / 16), sign * math.sin(2 * math.pi * power / 16)
    real, imag = a
    if imag is None:
        if power == 4:
            return (jnp.zeros_like(real), real if sign > 0 else -real)
        return (real * cos, real * sin)
    if power == 4:
        return (-imag, real) if sign > 0 else (imag, -real)
    if abs(abs(cos) - abs(sin)) < 1e-9:
        root = math.sqrt(0.5)
        cs, ss = (1 if cos > 0 else -1), (1 if sin > 0 else -1)
        new_real = (real if cs > 0 else -real) - (imag if ss > 0 else -imag)
        new_imag = (real if ss > 0 else -real) + (imag if cs > 0 else -imag)
        return (new_real * root, new_imag * root)
    return (real * cos - imag * sin, real * sin + imag * cos)


def sixteen(values, sign):
    inner = [four(*(values[n0 + 4 * n1] for n1 in range(4)), sign) for n0 in range(4)]
    out = [None] * 16
    for k1 in range(4):
        parts = [turned(inner[n0][k1], n0 * k1, sign) for n0 in range(4)]
        for k2, value in enumerate(four(*parts, sign)):
            out[k1 + 4 * k2] = value
    return out


def split(value):
    high = value.astype(jnp.bfloat16)
    low = (value - high.astype(jnp.float32)).astype(jnp.bfloat16)
    return high, low


def dot(a, b, dims):
    return lax.dot_general(a, b, (dims, ((), ())), preferred_element_type=jnp.float32)


def fetched(source, target, semaphore):
    copy = pltpu.make_async_copy(source, target, semaphore)
    copy.start()
    return copy


def fill_table(table, twiddle, sign, transposed):
    shape = (LANES, LANES)
    row, col = (lax.broadcasted_iota(jnp.int32, shape, n) for n in range(2))
    at = jnp.bitwise_and(row * col, LANES - 1)
    cos, sin = (
        jnp.take_along_axis(
            jnp.broadcast_to(twiddle[n, RADIX : RADIX + 1, :], shape), at, axis=1
        )
        for n in range(2)
    )
    for n, value in enumerate((cos, sign * sin, -sign * sin, cos)):
        high, low = split(value)
        into, out = ((n // 2, n % 2), (n % 2, n // 2))[transposed]
        for m, half in enumerate((high, high, low)):
            if transposed:
                lane = 256 * m + LANES * out
                table[LANES * into : LANES * into + LANES, lane : lane + LANES] = half
            else:
                at_row = 256 * m + LANES * into
                table[at_row : at_row + LANES, LANES * out : LANES * out + LANES] = half


def three_pass(pair, table, dims):
    high = pair[:, :256] if dims[0][0] == 1 else pair[:256, :]
    return dot(pair, table[:512, :], dims) + dot(high, table[512:, :], dims)


def store_pair(held, rows, real, imag):
    high_r, low_r = split(real)
    high_i, low_i = split(imag)
    held[rows, 0:LANES] = high_r
    held[rows, LANES : 2 * LANES] = high_i
    held[rows, 2 * LANES : 3 * LANES] = low_r
    held[rows, 3 * LANES : 4 * LANES] = low_i


def cross_ready(where, image, *pieces):
    for k in range(4):
        to = (where[0] // 2 + k) % 4
        pieces[k][...] = image[:, pl.ds(pl.multiple_of(to * 512, 512), 512)]


def swap_ready(where, *refs):
    pieces, early, late = refs[:4], refs[-2], refs[-1]
    lanes = pl.ds(pl.multiple_of((1 - where[0] % 2) * 256, 256), 256)
    for k in range(4):
        early[k] = pieces[k][:EARLY, lanes]
        late[k] = pieces[k][EARLY:, lanes]


def rows_forward(
    image_in, twiddle_in, out, image, twiddle, out_v, held, table, in_sems, sems
):
    chunk = 16
    steps = LANES // chunk

    def incoming(step):
        rows = pl.ds(step * chunk, chunk)
        return pltpu.make_async_copy(image_in.at[rows, :], image.at[rows, :], in_sems.at[step])

    get_twiddle = fetched(twiddle_in, twiddle, in_sems.at[steps])
    for step in range(steps):
        incoming(step).start()
    get_twiddle.wait()
    fill_table(table, twiddle, -1, True)

    def body(step):
        incoming(step).wait()
        at = step * chunk
        values = [
            (image[pl.ds(at, chunk), b * LANES : (b + 1) * LANES], None) for b in range(RADIX)
        ]
        mixed = sixteen(values, -1)
        for f in range(RADIX):
            real, imag = mixed[f]
            if imag is None:
                imag = jnp.zeros_like(real)
            cos = twiddle[0, f : f + 1, :] * (1.0 / GRID)
            sin = twiddle[1, f : f + 1, :] * (1.0 / GRID)
            store_pair(
                held,
                pl.ds(f * LANES + at, chunk),
                real * cos + imag * sin,
                imag * cos - real * sin,
            )

    for step in range(steps):
        body(step)
    dims = ((1,), (1,))
    sent = []
    for g in range(RADIX // 2):
        pair = held[256 * g : 256 * g + 256, :]
        result = dot(table[:, :512], pair, dims) + dot(table[:, 512:], pair[:, :256], dims)
        for h in range(2):
            for c in range(2):
                block = result[c * LANES : (c + 1) * LANES, h * LANES : (h + 1) * LANES]
                out_v[:, c, 2 * g + h] = block.reshape(RADIX, 8, LANES)
        both = pl.ds(2 * g, 2)
        sent.append(fetched(out_v.at[:, :, both], out.at[:, :, both], sems.at[g]))
    for copy in sent:
        copy.wait()


def data_prepared(weights, measured, place, twiddle, out, forward, inverse, held):
    fill_table(forward, twiddle, -1, False)
    fill_table(inverse, twiddle, 1, False)
    for n in range(3):
        source = weights[...] if n == 0 else measured[n - 1]
        held[...] = source.astype(jnp.float32)
        for f in range(RADIX):
            rows = held[pl.ds(f, LANES, stride=RADIX), :].astype(jnp.bfloat16)
            out[n, f] = dot(place[...], rows, ((1,), (1,))).astype(jnp.bfloat16)


def columns(
    cols_in, data_in, twiddle_in, forward_in, inverse_in, out_all,
    cols, data, twiddle, forward, inverse, out, held_all, in_sems, chunk_sems, out_sems,
):
    chunk = 64
    steps = LANES // chunk
    dims = ((1,), (0,))

    def incoming_cols(step):
        rows = pl.ds(step * chunk, chunk)
        imag_rows = pl.ds(LANES + step * chunk, chunk)
        return [
            pltpu.make_async_copy(cols_in.at[:, r, :], cols.at[:, r, :], chunk_sems.at[step, n])
            for n, r in enumerate((rows, imag_rows))
        ]

    def incoming(step):
        rows = pl.ds(step * chunk, chunk)
        return pltpu.make_async_copy(
            data_in.at[:, :, rows, :], data.at[:, :, rows, :], chunk_sems.at[step, 2]
        )

    def outgoing(step, c):
        rows = pl.ds(c * LANES + step * chunk, chunk)
        return pltpu.make_async_copy(
            out.at[:, rows, :], out_all.at[:, rows, :], out_sems.at[step, c]
        )

    for copy in incoming_cols(0):
        copy.start()
    get_twiddle = fetched(twiddle_in, twiddle, in_sems.at[2])
    get_forward = fetched(forward_in, forward, in_sems.at[0])
    incoming(0).start()
    get_inverse = fetched(inverse_in, inverse, in_sems.at[1])
    for step in range(1, steps):
        for copy in incoming_cols(step):
            copy.start()
        incoming(step).start()
    out[:, 2 * LANES :, :] = jnp.zeros((RADIX, 8, LANES), jnp.float32)
    lane_at = lax.broadcasted_iota(jnp.int32, (8, LANES), 1)
    get_twiddle.wait()

    for step in range(steps):
        held = held_all.at[step % 2]
        at = step * chunk
        here = pl.ds(at, chunk)
        for copy in incoming_cols(step):
            copy.wait()
        imag_here = pl.ds(LANES + at, chunk)
        mixed = sixteen([(cols[b, here, :], cols[b, imag_here, :]) for b in range(RADIX)], -1)
        for f in range(RADIX):
            real, imag = mixed[f]
            cos, sin = twiddle[0, f : f + 1, :], twiddle[1, f : f + 1, :]
            rows = slice(f * chunk, (f + 1) * chunk)
            store_pair(held, rows, real * cos + imag * sin, imag * cos - real * sin)
        if step == 0:
            get_forward.wait()
            get_inverse.wait()
        spectrum = three_pass(held[...], forward, dims)
        incoming(step).wait()
        for f in range(RADIX):
            rows = slice(f * chunk, (f + 1) * chunk)
            weight = data[0, f, here, :].astype(jnp.float32)
            real = weight * spectrum[rows, :LANES] - data[1, f, here, :].astype(jnp.float32)
            imag = weight * spectrum[rows, LANES:] - data[2, f, here, :].astype(jnp.float32)
            store_pair(held, rows, real, imag)
        back = three_pass(held[...], inverse, dims)
        values = []
        for f in range(RADIX):
            rows = slice(f * chunk, (f + 1) * chunk)
            real, imag = back[rows, :LANES], back[rows, LANES:]
            cos, sin = twiddle[0, f : f + 1, :], twiddle[1, f : f + 1, :]
            values.append((real * cos - imag * sin, imag * cos + real * sin))
        mixed = sixteen(values, 1)
        for b in range(RADIX):
            for c in range(2):
                out[b, (here, imag_here)[c], :] = mixed[b][c]
                if b > 0:
                    edge = out[b - 1, 2 * LANES :, :]
                    for i in range(chunk // 8):
                        first = mixed[b][c][8 * i : 8 * i + 8, 0:1]
                        at_lane = lane_at == c * RADIX + step * (chunk // 8) + i
                        edge = jnp.where(at_lane, first, edge)
                    out[b - 1, 2 * LANES :, :] = edge
        for c in range(2):
            outgoing(step, c).start()
    rows = pl.ds(2 * LANES, 8)
    edges = fetched(out.at[:, rows, :], out_all.at[:, rows, :], in_sems.at[0])
    for step in range(steps):
        for c in range(2):
            outgoing(step, c).wait()
    edges.wait()


def tied(value, after, out):
    pass


def rows_back(lines, twiddle, after_one, after_two, out, held, side_v, table):
    fill_table(table, twiddle, 1, False)
    dims = ((0,), (0,))
    for f in range(RADIX):
        real = lines[:, 8 * f : 8 * f + 8, :].reshape(LANES, LANES)
        imag = lines[:, LANES + 8 * f : LANES + 8 * f + 8, :].reshape(LANES, LANES)
        high_r, low_r = split(real)
        high_i, low_i = split(imag)
        pair = jnp.concatenate([high_r, high_i, low_r, low_i], axis=0)
        held[f] = three_pass(pair, table, dims)
    high, low = split(lines[:, 2 * LANES :, :].reshape(LANES, LANES))
    edge = (
        dot(high, table[0:LANES, :], dims)
        + dot(low, table[0:LANES, :], dims)
        + dot(high, table[512 : 512 + LANES, :], dims)
    )
    edge_r = edge[:RADIX, :LANES] - edge[RADIX : 2 * RADIX, LANES:]
    edge_i = edge[:RADIX, LANES:] + edge[RADIX : 2 * RADIX, :LANES]
    scale = 1.0 / GRID
    cos, sin = twiddle[0, :RADIX] * scale, twiddle[1, :RADIX] * scale
    edge_r, edge_i = edge_r * cos - edge_i * sin, edge_i * cos + edge_r * sin
    mixed = sixteen([(edge_r[f : f + 1], edge_i[f : f + 1]) for f in range(RADIX)], 1)
    for d in range(CHANNELS):
        out[d, LANES : LANES + 1, :] = jnp.concatenate(
            [mixed[2 * d][0], mixed[2 * d + 1][0]], axis=1
        )
    chunk = 16
    steps = LANES // chunk
    lane_at = lax.broadcasted_iota(jnp.int32, (chunk, LANES), 1)

    def body(step):
        at = step * chunk
        here = pl.ds(at, chunk)
        values = []
        for f in range(RADIX):
            real, imag = held[f, here, :LANES], held[f, here, LANES:]
            cos, sin = twiddle[0, f : f + 1, :] * scale, twiddle[1, f : f + 1, :] * scale
            values.append((real * cos - imag * sin, imag * cos + real * sin))
        mixed = sixteen(values, 1)
        side = jnp.zeros((chunk, LANES), jnp.float32)
        for b in range(RADIX):
            low_lane = (b % 2) * LANES
            out[b // 2, here, low_lane : low_lane + LANES] = mixed[b][0]
            if b > 0 and b % 2 == 0:
                side = jnp.where(lane_at == b // 2 - 1, mixed[b][0][:, 0:1], side)
        side_v[here, :] = side

    for step in range(steps):
        body(step)
    beside = side_v[...].T
    for d in range(CHANNELS):
        out[d, LANES + 1 : LANES + 2, :LANES] = beside[d : d + 1, :]


def dual_edges(dual, last_row, last_column):
    rows, cols = [], []
    for c in range(CHANNELS):
        rows.append(dual[c, 0, 112:128, :].astype(jnp.float32)[15:16, :])
        cols.append(dual[c, 1, :, LANES:].astype(jnp.float32)[:, LANES - 1 :])
    last_row[...] = jnp.concatenate(rows, axis=0)
    last_column[...] = jnp.concatenate(cols, axis=1).T


def tile_ready(where, *refs):
    pieces, (early, late, dual, above, left) = refs[:4], refs[4:9]
    for_image, for_ahead, first_row, first_column = refs[9:]
    row_at = lax.broadcasted_iota(jnp.int32, (LANES, 2 * LANES), 0)
    lane_at = lax.broadcasted_iota(jnp.int32, (LANES, 2 * LANES), 1)
    for k in range(4):
        for other in range(2):
            half = where[0] % 2
            c = (where[0] // 2 + 4 - k) % 4 * 2 + (1 - half if other else half)
            p = dual[c, 0].astype(jnp.float32)
            q = dual[c, 1].astype(jnp.float32)
            beside = jnp.broadcast_to(left[pl.ds(c, 1), :], (LANES, LANES)).T[:, 0:1]
            prev_p = jnp.where(row_at == 0, above[pl.ds(c, 1), :], pltpu.roll(p, 1, 0))
            prev_q = jnp.where(lane_at == 0, beside, pltpu.roll(q, 1, 1))
            adjoint = prev_p - p + prev_q - q
            if other:
                image = jnp.concatenate([early[k], late[k]], axis=0)
            else:
                image = pieces[k][:, pl.ds(pl.multiple_of(half * 256, 256), 256)]
            ahead = image - adjoint
            for_image[c] = image - step_primal * adjoint
            for_ahead[c] = ahead
            first_row[pl.ds(c, 1), :] = ahead[0:1, :]
            first_column[pl.ds(c, 1), :] = ahead[:, :LANES].T[0:1, :]


def finish(
    gradient, for_image, for_ahead, dual, below, right, image_next, dual_next,
    ahead_v, side_v, image_v, dual_v, image_sems, dual_sems,
):
    sides = []
    leaving = []
    for c in range(CHANNELS):
        slope = gradient[c, :LANES, :]
        image_v[c] = for_image[c] - step_primal * slope
        leaving.append(fetched(image_v.at[c], image_next.at[c], image_sems.at[c]))
        ahead_v[c, :LANES, :] = for_ahead[c] - slope
        ahead_v[c, LANES : LANES + 1, :] = (
            below[c : c + 1, :] - gradient[c, LANES : LANES + 1, :]
        )
        sides.append(gradient[c, LANES + 1 : LANES + 2, :LANES])
    side_v[:, :CHANNELS] = (right[...] - jnp.concatenate(sides, axis=0)).T
    chunk = 16
    steps = LANES // chunk
    row_at = lax.broadcasted_iota(jnp.int32, (chunk, 2 * LANES), 0)
    lane_at = lax.broadcasted_iota(jnp.int32, (chunk, 2 * LANES), 1)

    def outgoing(step):
        rows = pl.ds(step * chunk, chunk)
        return pltpu.make_async_copy(
            dual_v.at[:, :, rows, :], dual_next.at[:, :, rows, :], dual_sems.at[step]
        )

    def body(step):
        at = step * chunk
        here = pl.ds(at, chunk)
        after = pl.ds(at + chunk, 8)
        firsts, seconds, total = [], [], None
        for c in range(CHANNELS):
            ahead = ahead_v[c, here, :]
            next_row = ahead_v[c, after, :][0:1, :]
            down = jnp.where(row_at == chunk - 1, next_row, pltpu.roll(ahead, chunk - 1, 0))
            beside = jnp.where(
                lane_at == 2 * LANES - 1,
                side_v[here, c : c + 1],
                pltpu.roll(ahead, 2 * LANES - 1, 1),
            )
            first = dual[c, 0, here, :].astype(jnp.float32) + step_dual * (down - ahead)
            second = dual[c, 1, here, :].astype(jnp.float32) + step_dual * (beside - ahead)
            firsts.append(first)
            seconds.append(second)
            squares = first * first + second * second
            total = squares if total is None else total + squares
        factor = 1.0 / jnp.maximum(1.0, jnp.sqrt(total) / clip_radius)
        for c in range(CHANNELS):
            dual_v[c, 0, here, :] = (firsts[c] * factor).astype(jnp.bfloat16)
            dual_v[c, 1, here, :] = (seconds[c] * factor).astype(jnp.bfloat16)
        outgoing(step).start()

    for step in range(steps):
        body(step)
    for copy in leaving:
        copy.wait()
    for step in range(steps):
        outgoing(step).wait()


def shape(dims, dtype=jnp.float32):
    return jax.ShapeDtypeStruct(dims, dtype)


def passed_along(x, axis, by):
    devices = lax.axis_size(axis)
    pairs = [(i, i + by) for i in range(devices) if 0 <= i + by < devices]
    return lax.ppermute(x, axis, pairs)


ANY = pl.BlockSpec(memory_space=pl.ANY)
HBM = pl.BlockSpec(memory_space=pltpu.HBM)
VM = pl.BlockSpec(memory_space=pltpu.VMEM)
SM = pl.BlockSpec(memory_space=pltpu.SMEM)
DMA = pltpu.SemaphoreType.DMA


def call(kernel, out_shape, in_specs, out_specs, scratch, limit=16):
    return pl.pallas_call(
        kernel,
        out_shape=out_shape,
        in_specs=in_specs,
        out_specs=out_specs,
        scratch_shapes=scratch,
        name=kernel.__name__,
        compiler_params=pltpu.CompilerParams(vmem_limit_bytes=limit * MIB),
    )


def shards(image_field, weights, measured, dual_field):
    twiddle, place = host_tables()
    place = jnp.asarray(place, jnp.bfloat16)
    twiddle = jnp.asarray(twiddle)
    image = image_field[0]
    f32, bf16 = jnp.float32, jnp.bfloat16
    where = lax.axis_index("chan").astype(jnp.int32).reshape(1)

    spread = call(
        rows_forward,
        shape((RADIX, 2, RADIX, 8, LANES)),
        [HBM, HBM],
        HBM,
        [
            pltpu.VMEM((LANES, GRID), f32),
            pltpu.VMEM((2, RADIX + 8, LANES), f32),
            pltpu.VMEM((RADIX, 2, RADIX, 8, LANES), f32),
            pltpu.VMEM((GRID, 512), bf16),
            pltpu.VMEM((256, 768), bf16),
            DMA((9,)),
            DMA((8,)),
        ],
        63,
    )(image, twiddle)
    cols = lax.all_to_all(
        spread.reshape(RADIX, 2 * LANES, LANES), "facet", split_axis=0, concat_axis=0, tiled=True
    )
    last_row, last_column = call(
        dual_edges,
        (shape((CHANNELS, 2 * LANES)), shape((CHANNELS, LANES))),
        [VM],
        (VM, VM),
        [],
    )(dual_field)
    above = passed_along(last_row, "facet", 1)
    left = passed_along(last_column, "chan", 1)
    pieces = list(
        call(cross_ready, (shape((LANES, 512)),) * 4, [SM, VM], (VM,) * 4, [])(where, image)
    )
    for k in range(1, 4):
        pairs = [(2 * x + z, (x + k) % 4 * 2 + z) for x in range(4) for z in range(2)]
        pieces[k] = lax.ppermute(pieces[k], "chan", pairs)
    data, forward, inverse = call(
        data_prepared,
        (
            shape((3, RADIX, LANES, LANES), bf16),
            shape((768, 256), bf16),
            shape((768, 256), bf16),
        ),
        [VM] * 4,
        (VM,) * 3,
        [pltpu.VMEM((GRID, LANES), f32)],
        63,
    )(weights[0], measured[0], place, twiddle)
    early, late = call(
        swap_ready,
        (shape((4, EARLY, 256)), shape((4, LANES - EARLY, 256))),
        [SM] + [VM] * 4 + [ANY],
        (VM, VM),
        [],
    )(where, *pieces, last_row)
    other_zl = [(i, i ^ 1) for i in range(8)]
    early = lax.ppermute(early, "chan", other_zl)
    cols, late, above, left, data, forward, inverse = lax.optimization_barrier(
        (cols, late, above, left, data, forward, inverse)
    )
    late = lax.ppermute(late, "chan", other_zl)
    data, forward, inverse = (
        pltpu.with_memory_space_constraint(x, pltpu.HBM) for x in (data, forward, inverse)
    )
    back = call(
        columns,
        shape((RADIX, 2 * LANES + 8, LANES)),
        [HBM] * 5,
        HBM,
        [
            pltpu.VMEM((RADIX, 2 * LANES, LANES), f32),
            pltpu.VMEM((3, RADIX, LANES, LANES), bf16),
            pltpu.VMEM((2, RADIX + 8, LANES), f32),
            pltpu.VMEM((768, 256), bf16),
            pltpu.VMEM((768, 256), bf16),
            pltpu.VMEM((RADIX, 2 * LANES + 8, LANES), f32),
            pltpu.VMEM((2, RADIX * 64, 512), bf16),
            DMA((3,)),
            DMA((2, 3)),
            DMA((2, 2)),
        ],
        63,
    )(cols, data, twiddle, forward, inverse)
    back = pl.pallas_call(
        tied,
        out_shape=shape((RADIX, 2 * LANES + 8, LANES)),
        in_specs=[ANY] * 2,
        out_specs=ANY,
        input_output_aliases={0: 0},
        name="tied",
    )(back, early[0, :8, :LANES] + late[0, :8, :LANES])
    lines = lax.all_to_all(back, "facet", split_axis=0, concat_axis=0, tiled=True)
    for_image, for_ahead, first_row, first_column = call(
        tile_ready,
        (
            shape((CHANNELS, LANES, 2 * LANES)),
            shape((CHANNELS, LANES, 2 * LANES)),
            shape((CHANNELS, 2 * LANES)),
            shape((CHANNELS, LANES)),
        ),
        [SM] + [VM] * 9,
        (VM,) * 4,
        [],
    )(where, *pieces, early, late, dual_field, above, left)
    below = passed_along(first_row, "facet", -1)
    right = passed_along(first_column, "chan", -1)
    slopes = call(
        rows_back,
        shape((CHANNELS, LANES + 8, 2 * LANES)),
        [VM] * 2 + [ANY] * 2,
        VM,
        [
            pltpu.VMEM((RADIX, LANES, 256), f32),
            pltpu.VMEM((LANES, LANES), f32),
            pltpu.VMEM((768, 256), bf16),
        ],
    )(lines, twiddle, below, right)
    gradient = lax.all_to_all(slopes, "chan", split_axis=0, concat_axis=0, tiled=True)
    return call(
        finish,
        (shape((CHANNELS, LANES, 2 * LANES)), shape((CHANNELS, 2, LANES, 2 * LANES), bf16)),
        [VM] * 6,
        (HBM, HBM),
        [
            pltpu.VMEM((CHANNELS, LANES + 8, 2 * LANES), f32),
            pltpu.VMEM((LANES, LANES), f32),
            pltpu.VMEM((CHANNELS, LANES, 2 * LANES), f32),
            pltpu.VMEM((CHANNELS, 2, LANES, 2 * LANES), bf16),
            DMA((8,)),
            DMA((8,)),
        ],
    )(gradient, for_image, for_ahead, dual_field, below, right)


def solution(mesh):
    placed = (
        P("chan", "facet", None),
        P("chan", None, "facet"),
        P("chan", None, None, "facet"),
        P(None, None, "facet", "chan"),
    )
    return jax.shard_map(
        shards,
        mesh=mesh,
        in_specs=placed,
        out_specs=(P(None, "facet", "chan"), P(None, None, "facet", "chan")),
        check_vma=False,
    )
```

```python
from functools import partial
import math

import jax
import jax.numpy as jnp
import numpy as np
from jax import lax
from jax.experimental import pallas as pl
from jax.experimental.pallas import tpu as pltpu
from jax.sharding import PartitionSpec as P

GRID = 2048
RADIX = 16
LANES = 128
CHANNELS = 8
EARLY = 64

step_primal = 0.5
step_dual = 0.5
clip_radius = 4.0

MIB = 1024 * 1024


def host_tables():
    index = np.arange(LANES)
    turn = 2.0 * np.pi * np.arange(RADIX + 8)[:, None] * index[None, :] / GRID
    twiddle = np.stack([np.cos(turn), np.sin(turn)]).astype(np.float32)
    place = np.zeros((LANES, LANES))
    for at in range(LANES):
        place[at, 16 * (at % 8) + at // 8] = 1.0
    return twiddle, place


def c_add(a, b):
    return (a[0] + b[0], b[1] if a[1] is None else a[1] if b[1] is None else a[1] + b[1])


def c_sub(a, b):
    imag = None
    if a[1] is not None and b[1] is not None:
        imag = a[1] - b[1]
    elif a[1] is not None:
        imag = a[1]
    elif b[1] is not None:
        imag = -b[1]
    return (a[0] - b[0], imag)


def add_turned(a, b, sign):
    real = a[0] if b[1] is None else (a[0] - b[1] if sign > 0 else a[0] + b[1])
    if a[1] is None:
        imag = b[0] if sign > 0 else -b[0]
    else:
        imag = a[1] + b[0] if sign > 0 else a[1] - b[0]
    return (real, imag)


def four(a, b, c, d, sign):
    sum_even, diff_even = c_add(a, c), c_sub(a, c)
    sum_odd, diff_odd = c_add(b, d), c_sub(b, d)
    return (
        c_add(sum_even, sum_odd),
        add_turned(diff_even, diff_odd, sign),
        c_sub(sum_even, sum_odd),
        add_turned(diff_even, diff_odd, -sign),
    )


def turned(a, power, sign):
    power = power % 16
    if power == 0:
        return a
    cos, sin = math.cos(2 * math.pi * power / 16), sign * math.sin(2 * math.pi * power / 16)
    real, imag = a
    if imag is None:
        if power == 4:
            return (jnp.zeros_like(real), real if sign > 0 else -real)
        return (real * cos, real * sin)
    if power == 4:
        return (-imag, real) if sign > 0 else (imag, -real)
    if abs(abs(cos) - abs(sin)) < 1e-9:
        root = math.sqrt(0.5)
        cs, ss = (1 if cos > 0 else -1), (1 if sin > 0 else -1)
        new_real = (real if cs > 0 else -real) - (imag if ss > 0 else -imag)
        new_imag = (real if ss > 0 else -real) + (imag if cs > 0 else -imag)
        return (new_real * root, new_imag * root)
    return (real * cos - imag * sin, real * sin + imag * cos)


def sixteen(values, sign):
    inner = [four(*(values[n0 + 4 * n1] for n1 in range(4)), sign) for n0 in range(4)]
    out = [None] * 16
    for k1 in range(4):
        parts = [turned(inner[n0][k1], n0 * k1, sign) for n0 in range(4)]
        for k2, value in enumerate(four(*parts, sign)):
            out[k1 + 4 * k2] = value
    return out


def split(value):
    high = value.astype(jnp.bfloat16)
    low = (value - high.astype(jnp.float32)).astype(jnp.bfloat16)
    return high, low


def dot(a, b, dims):
    return lax.dot_general(a, b, (dims, ((), ())), preferred_element_type=jnp.float32)


def fetched(source, target, semaphore):
    copy = pltpu.make_async_copy(source, target, semaphore)
    copy.start()
    return copy


def fill_table(table, twiddle, sign, transposed):
    shape = (LANES, LANES)
    row, col = (lax.broadcasted_iota(jnp.int32, shape, n) for n in range(2))
    at = jnp.bitwise_and(row * col, LANES - 1)
    cos, sin = (
        jnp.take_along_axis(
            jnp.broadcast_to(twiddle[n, RADIX : RADIX + 1, :], shape), at, axis=1
        )
        for n in range(2)
    )
    for n, value in enumerate((cos, sign * sin, -sign * sin, cos)):
        high, low = split(value)
        into, out = ((n // 2, n % 2), (n % 2, n // 2))[transposed]
        for m, half in enumerate((high, high, low)):
            if transposed:
                lane = 256 * m + LANES * out
                table[LANES * into : LANES * into + LANES, lane : lane + LANES] = half
            else:
                at_row = 256 * m + LANES * into
                table[at_row : at_row + LANES, LANES * out : LANES * out + LANES] = half


def three_pass(pair, table, dims):
    high = pair[:, :256] if dims[0][0] == 1 else pair[:256, :]
    return dot(pair, table[:512, :], dims) + dot(high, table[512:, :], dims)


def store_pair(held, rows, real, imag):
    high_r, low_r = split(real)
    high_i, low_i = split(imag)
    held[rows, 0:LANES] = high_r
    held[rows, LANES : 2 * LANES] = high_i
    held[rows, 2 * LANES : 3 * LANES] = low_r
    held[rows, 3 * LANES : 4 * LANES] = low_i


def cross_ready(where, image, *pieces):
    for k in range(4):
        to = (where[0] // 2 + k) % 4
        pieces[k][...] = image[:, pl.ds(pl.multiple_of(to * 512, 512), 512)]


def swap_ready(where, *refs):
    pieces, early, late = refs[:4], refs[-2], refs[-1]
    lanes = pl.ds(pl.multiple_of((1 - where[0] % 2) * 256, 256), 256)
    for k in range(4):
        early[k] = pieces[k][:EARLY, lanes]
        late[k] = pieces[k][EARLY:, lanes]


def rows_forward(
    image_in, twiddle_in, out, image, twiddle, out_v, held, table, in_sems, sems
):
    chunk = 16
    steps = LANES // chunk

    def incoming(step):
        rows = pl.ds(step * chunk, chunk)
        return pltpu.make_async_copy(image_in.at[rows, :], image.at[rows, :], in_sems.at[step])

    get_twiddle = fetched(twiddle_in, twiddle, in_sems.at[steps])
    for step in range(steps):
        incoming(step).start()
    get_twiddle.wait()
    fill_table(table, twiddle, -1, True)

    def body(step):
        incoming(step).wait()
        at = step * chunk
        values = [
            (image[pl.ds(at, chunk), b * LANES : (b + 1) * LANES], None) for b in range(RADIX)
        ]
        mixed = sixteen(values, -1)
        for f in range(RADIX):
            real, imag = mixed[f]
            if imag is None:
                imag = jnp.zeros_like(real)
            cos = twiddle[0, f : f + 1, :] * (1.0 / GRID)
            sin = twiddle[1, f : f + 1, :] * (1.0 / GRID)
            store_pair(
                held,
                pl.ds(f * LANES + at, chunk),
                real * cos + imag * sin,
                imag * cos - real * sin,
            )

    for step in range(steps):
        body(step)
    dims = ((1,), (1,))
    sent = []
    for g in range(RADIX // 2):
        pair = held[256 * g : 256 * g + 256, :]
        result = dot(table[:, :512], pair, dims) + dot(table[:, 512:], pair[:, :256], dims)
        for h in range(2):
            for c in range(2):
                block = result[c * LANES : (c + 1) * LANES, h * LANES : (h + 1) * LANES]
                out_v[:, c, 2 * g + h] = block.reshape(RADIX, 8, LANES)
        both = pl.ds(2 * g, 2)
        sent.append(fetched(out_v.at[:, :, both], out.at[:, :, both], sems.at[g]))
    for copy in sent:
        copy.wait()


def data_prepared(weights, measured, place, twiddle, out, forward, inverse, held):
    fill_table(forward, twiddle, -1, False)
    fill_table(inverse, twiddle, 1, False)
    for n in range(3):
        source = weights[...] if n == 0 else measured[n - 1]
        held[...] = source.astype(jnp.float32)
        for f in range(RADIX):
            rows = held[pl.ds(f, LANES, stride=RADIX), :].astype(jnp.bfloat16)
            out[n, f] = dot(place[...], rows, ((1,), (1,))).astype(jnp.bfloat16)


def columns(
    cols_in, data_in, twiddle_in, forward_in, inverse_in, out_all,
    cols, data, twiddle, forward, inverse, out, held_all, in_sems, chunk_sems, out_sems,
):
    chunk = 64
    steps = LANES // chunk
    dims = ((1,), (0,))

    def incoming_cols(step):
        rows = pl.ds(step * chunk, chunk)
        imag_rows = pl.ds(LANES + step * chunk, chunk)
        return [
            pltpu.make_async_copy(cols_in.at[:, r, :], cols.at[:, r, :], chunk_sems.at[step, n])
            for n, r in enumerate((rows, imag_rows))
        ]

    def incoming(step):
        rows = pl.ds(step * chunk, chunk)
        return pltpu.make_async_copy(
            data_in.at[:, :, rows, :], data.at[:, :, rows, :], chunk_sems.at[step, 2]
        )

    def outgoing(step, c):
        rows = pl.ds(c * LANES + step * chunk, chunk)
        return pltpu.make_async_copy(
            out.at[:, rows, :], out_all.at[:, rows, :], out_sems.at[step, c]
        )

    for copy in incoming_cols(0):
        copy.start()
    get_twiddle = fetched(twiddle_in, twiddle, in_sems.at[2])
    get_forward = fetched(forward_in, forward, in_sems.at[0])
    incoming(0).start()
    get_inverse = fetched(inverse_in, inverse, in_sems.at[1])
    for step in range(1, steps):
        for copy in incoming_cols(step):
            copy.start()
        incoming(step).start()
    out[:, 2 * LANES :, :] = jnp.zeros((RADIX, 8, LANES), jnp.float32)
    lane_at = lax.broadcasted_iota(jnp.int32, (8, LANES), 1)
    get_twiddle.wait()

    for step in range(steps):
        held = held_all.at[step % 2]
        at = step * chunk
        here = pl.ds(at, chunk)
        for copy in incoming_cols(step):
            copy.wait()
        imag_here = pl.ds(LANES + at, chunk)
        mixed = sixteen([(cols[b, here, :], cols[b, imag_here, :]) for b in range(RADIX)], -1)
        for f in range(RADIX):
            real, imag = mixed[f]
            cos, sin = twiddle[0, f : f + 1, :], twiddle[1, f : f + 1, :]
            rows = slice(f * chunk, (f + 1) * chunk)
            store_pair(held, rows, real * cos + imag * sin, imag * cos - real * sin)
        if step == 0:
            get_forward.wait()
            get_inverse.wait()
        spectrum = three_pass(held[...], forward, dims)
        incoming(step).wait()
        for f in range(RADIX):
            rows = slice(f * chunk, (f + 1) * chunk)
            weight = data[0, f, here, :].astype(jnp.float32)
            real = weight * spectrum[rows, :LANES] - data[1, f, here, :].astype(jnp.float32)
            imag = weight * spectrum[rows, LANES:] - data[2, f, here, :].astype(jnp.float32)
            store_pair(held, rows, real, imag)
        back = three_pass(held[...], inverse, dims)
        values = []
        for f in range(RADIX):
            rows = slice(f * chunk, (f + 1) * chunk)
            real, imag = back[rows, :LANES], back[rows, LANES:]
            cos, sin = twiddle[0, f : f + 1, :], twiddle[1, f : f + 1, :]
            values.append((real * cos - imag * sin, imag * cos + real * sin))
        mixed = sixteen(values, 1)
        for b in range(RADIX):
            for c in range(2):
                out[b, (here, imag_here)[c], :] = mixed[b][c]
                if b > 0:
                    edge = out[b - 1, 2 * LANES :, :]
                    for i in range(chunk // 8):
                        first = mixed[b][c][8 * i : 8 * i + 8, 0:1]
                        at_lane = lane_at == c * RADIX + step * (chunk // 8) + i
                        edge = jnp.where(at_lane, first, edge)
                    out[b - 1, 2 * LANES :, :] = edge
        for c in range(2):
            outgoing(step, c).start()
    rows = pl.ds(2 * LANES, 8)
    edges = fetched(out.at[:, rows, :], out_all.at[:, rows, :], in_sems.at[0])
    for step in range(steps):
        for c in range(2):
            outgoing(step, c).wait()
    edges.wait()


def tied(value, after, out):
    pass


def rows_back(lines, twiddle, after_one, after_two, out, held, side_v, table):
    fill_table(table, twiddle, 1, False)
    dims = ((0,), (0,))
    for f in range(RADIX):
        real = lines[:, 8 * f : 8 * f + 8, :].reshape(LANES, LANES)
        imag = lines[:, LANES + 8 * f : LANES + 8 * f + 8, :].reshape(LANES, LANES)
        high_r, low_r = split(real)
        high_i, low_i = split(imag)
        pair = jnp.concatenate([high_r, high_i, low_r, low_i], axis=0)
        held[f] = three_pass(pair, table, dims)
    high, low = split(lines[:, 2 * LANES :, :].reshape(LANES, LANES))
    edge = (
        dot(high, table[0:LANES, :], dims)
        + dot(low, table[0:LANES, :], dims)
        + dot(high, table[512 : 512 + LANES, :], dims)
    )
    edge_r = edge[:RADIX, :LANES] - edge[RADIX : 2 * RADIX, LANES:]
    edge_i = edge[:RADIX, LANES:] + edge[RADIX : 2 * RADIX, :LANES]
    scale = 1.0 / GRID
    cos, sin = twiddle[0, :RADIX] * scale, twiddle[1, :RADIX] * scale
    edge_r, edge_i = edge_r * cos - edge_i * sin, edge_i * cos + edge_r * sin
    mixed = sixteen([(edge_r[f : f + 1], edge_i[f : f + 1]) for f in range(RADIX)], 1)
    for d in range(CHANNELS):
        out[d, LANES : LANES + 1, :] = jnp.concatenate(
            [mixed[2 * d][0], mixed[2 * d + 1][0]], axis=1
        )
    chunk = 16
    steps = LANES // chunk
    lane_at = lax.broadcasted_iota(jnp.int32, (chunk, LANES), 1)

    def body(step):
        at = step * chunk
        here = pl.ds(at, chunk)
        values = []
        for f in range(RADIX):
            real, imag = held[f, here, :LANES], held[f, here, LANES:]
            cos, sin = twiddle[0, f : f + 1, :] * scale, twiddle[1, f : f + 1, :] * scale
            values.append((real * cos - imag * sin, imag * cos + real * sin))
        mixed = sixteen(values, 1)
        side = jnp.zeros((chunk, LANES), jnp.float32)
        for b in range(RADIX):
            low_lane = (b % 2) * LANES
            out[b // 2, here, low_lane : low_lane + LANES] = mixed[b][0]
            if b > 0 and b % 2 == 0:
                side = jnp.where(lane_at == b // 2 - 1, mixed[b][0][:, 0:1], side)
        side_v[here, :] = side

    for step in range(steps):
        body(step)
    beside = side_v[...].T
    for d in range(CHANNELS):
        out[d, LANES + 1 : LANES + 2, :LANES] = beside[d : d + 1, :]


def dual_edges(dual, last_row, last_column):
    rows, cols = [], []
    for c in range(CHANNELS):
        rows.append(dual[c, 0, 112:128, :].astype(jnp.float32)[15:16, :])
        cols.append(dual[c, 1, :, LANES:].astype(jnp.float32)[:, LANES - 1 :])
    last_row[...] = jnp.concatenate(rows, axis=0)
    last_column[...] = jnp.concatenate(cols, axis=1).T


def tile_ready(where, *refs):
    pieces, (early, late, dual, above, left) = refs[:4], refs[4:9]
    for_image, for_ahead, first_row, first_column = refs[9:]
    row_at = lax.broadcasted_iota(jnp.int32, (LANES, 2 * LANES), 0)
    lane_at = lax.broadcasted_iota(jnp.int32, (LANES, 2 * LANES), 1)
    for k in range(4):
        for other in range(2):
            half = where[0] % 2
            c = (where[0] // 2 + 4 - k) % 4 * 2 + (1 - half if other else half)
            p = dual[c, 0].astype(jnp.float32)
            q = dual[c, 1].astype(jnp.float32)
            beside = jnp.broadcast_to(left[pl.ds(c, 1), :], (LANES, LANES)).T[:, 0:1]
            prev_p = jnp.where(row_at == 0, above[pl.ds(c, 1), :], pltpu.roll(p, 1, 0))
            prev_q = jnp.where(lane_at == 0, beside, pltpu.roll(q, 1, 1))
            adjoint = prev_p - p + prev_q - q
            if other:
                image = jnp.concatenate([early[k], late[k]], axis=0)
            else:
                image = pieces[k][:, pl.ds(pl.multiple_of(half * 256, 256), 256)]
            ahead = image - adjoint
            for_image[c] = image - step_primal * adjoint
            for_ahead[c] = ahead
            first_row[pl.ds(c, 1), :] = ahead[0:1, :]
            first_column[pl.ds(c, 1), :] = ahead[:, :LANES].T[0:1, :]


def finish(
    gradient, for_image, for_ahead, dual, below, right, image_next, dual_next,
    ahead_v, side_v, image_v, dual_v, image_sems, dual_sems,
):
    sides = []
    leaving = []
    for c in range(CHANNELS):
        slope = gradient[c, :LANES, :]
        image_v[c] = for_image[c] - step_primal * slope
        leaving.append(fetched(image_v.at[c], image_next.at[c], image_sems.at[c]))
        ahead_v[c, :LANES, :] = for_ahead[c] - slope
        ahead_v[c, LANES : LANES + 1, :] = (
            below[c : c + 1, :] - gradient[c, LANES : LANES + 1, :]
        )
        sides.append(gradient[c, LANES + 1 : LANES + 2, :LANES])
    side_v[:, :CHANNELS] = (right[...] - jnp.concatenate(sides, axis=0)).T
    chunk = 16
    steps = LANES // chunk
    row_at = lax.broadcasted_iota(jnp.int32, (chunk, 2 * LANES), 0)
    lane_at = lax.broadcasted_iota(jnp.int32, (chunk, 2 * LANES), 1)

    def outgoing(step):
        rows = pl.ds(step * chunk, chunk)
        return pltpu.make_async_copy(
            dual_v.at[:, :, rows, :], dual_next.at[:, :, rows, :], dual_sems.at[step]
        )

    def body(step):
        at = step * chunk
        here = pl.ds(at, chunk)
        after = pl.ds(at + chunk, 8)
        firsts, seconds, total = [], [], None
        for c in range(CHANNELS):
            ahead = ahead_v[c, here, :]
            next_row = ahead_v[c, after, :][0:1, :]
            down = jnp.where(row_at == chunk - 1, next_row, pltpu.roll(ahead, chunk - 1, 0))
            beside = jnp.where(
                lane_at == 2 * LANES - 1,
                side_v[here, c : c + 1],
                pltpu.roll(ahead, 2 * LANES - 1, 1),
            )
            first = dual[c, 0, here, :].astype(jnp.float32) + step_dual * (down - ahead)
            second = dual[c, 1, here, :].astype(jnp.float32) + step_dual * (beside - ahead)
            firsts.append(first)
            seconds.append(second)
            squares = first * first + second * second
            total = squares if total is None else total + squares
        factor = 1.0 / jnp.maximum(1.0, jnp.sqrt(total) / clip_radius)
        for c in range(CHANNELS):
            dual_v[c, 0, here, :] = (firsts[c] * factor).astype(jnp.bfloat16)
            dual_v[c, 1, here, :] = (seconds[c] * factor).astype(jnp.bfloat16)
        outgoing(step).start()

    for step in range(steps):
        body(step)
    for copy in leaving:
        copy.wait()
    for step in range(steps):
        outgoing(step).wait()


def shape(dims, dtype=jnp.float32):
    return jax.ShapeDtypeStruct(dims, dtype)


def passed_along(x, axis, by):
    devices = lax.axis_size(axis)
    pairs = [(i, i + by) for i in range(devices) if 0 <= i + by < devices]
    return lax.ppermute(x, axis, pairs)


ANY = pl.BlockSpec(memory_space=pl.ANY)
HBM = pl.BlockSpec(memory_space=pltpu.HBM)
VM = pl.BlockSpec(memory_space=pltpu.VMEM)
SM = pl.BlockSpec(memory_space=pltpu.SMEM)
DMA = pltpu.SemaphoreType.DMA


def call(kernel, out_shape, in_specs, out_specs, scratch, limit=16):
    return pl.pallas_call(
        kernel,
        out_shape=out_shape,
        in_specs=in_specs,
        out_specs=out_specs,
        scratch_shapes=scratch,
        name=kernel.__name__,
        compiler_params=pltpu.CompilerParams(vmem_limit_bytes=limit * MIB),
    )


def shards(image_field, weights, measured, dual_field):
    twiddle, place = host_tables()
    place = jnp.asarray(place, jnp.bfloat16)
    twiddle = jnp.asarray(twiddle)
    image = image_field[0]
    f32, bf16 = jnp.float32, jnp.bfloat16
    where = lax.axis_index("chan").astype(jnp.int32).reshape(1)

    spread = call(
        rows_forward,
        shape((RADIX, 2, RADIX, 8, LANES)),
        [HBM, HBM],
        HBM,
        [
            pltpu.VMEM((LANES, GRID), f32),
            pltpu.VMEM((2, RADIX + 8, LANES), f32),
            pltpu.VMEM((RADIX, 2, RADIX, 8, LANES), f32),
            pltpu.VMEM((GRID, 512), bf16),
            pltpu.VMEM((256, 768), bf16),
            DMA((9,)),
            DMA((8,)),
        ],
        63,
    )(image, twiddle)
    cols = lax.all_to_all(
        spread.reshape(RADIX, 2 * LANES, LANES), "facet", split_axis=0, concat_axis=0, tiled=True
    )
    last_row, last_column = call(
        dual_edges,
        (shape((CHANNELS, 2 * LANES)), shape((CHANNELS, LANES))),
        [VM],
        (VM, VM),
        [],
    )(dual_field)
    above = passed_along(last_row, "facet", 1)
    left = passed_along(last_column, "chan", 1)
    pieces = list(
        call(cross_ready, (shape((LANES, 512)),) * 4, [SM, VM], (VM,) * 4, [])(where, image)
    )
    for k in range(1, 4):
        pairs = [(2 * x + z, (x + k) % 4 * 2 + z) for x in range(4) for z in range(2)]
        pieces[k] = lax.ppermute(pieces[k], "chan", pairs)
    data, forward, inverse = call(
        data_prepared,
        (
            shape((3, RADIX, LANES, LANES), bf16),
            shape((768, 256), bf16),
            shape((768, 256), bf16),
        ),
        [VM] * 4,
        (VM,) * 3,
        [pltpu.VMEM((GRID, LANES), f32)],
        63,
    )(weights[0], measured[0], place, twiddle)
    early, late = call(
        swap_ready,
        (shape((4, EARLY, 256)), shape((4, LANES - EARLY, 256))),
        [SM] + [VM] * 4 + [ANY] * 2,
        (VM, VM),
        [],
    )(where, *pieces, data, last_row)
    other_zl = [(i, i ^ 1) for i in range(8)]
    early = lax.ppermute(early, "chan", other_zl)
    cols, late, above, left, data, forward, inverse = lax.optimization_barrier(
        (cols, late, above, left, data, forward, inverse)
    )
    late = lax.ppermute(late, "chan", other_zl)
    data, forward, inverse = (
        pltpu.with_memory_space_constraint(x, pltpu.HBM) for x in (data, forward, inverse)
    )
    back = call(
        columns,
        shape((RADIX, 2 * LANES + 8, LANES)),
        [HBM] * 5,
        HBM,
        [
            pltpu.VMEM((RADIX, 2 * LANES, LANES), f32),
            pltpu.VMEM((3, RADIX, LANES, LANES), bf16),
            pltpu.VMEM((2, RADIX + 8, LANES), f32),
            pltpu.VMEM((768, 256), bf16),
            pltpu.VMEM((768, 256), bf16),
            pltpu.VMEM((RADIX, 2 * LANES + 8, LANES), f32),
            pltpu.VMEM((2, RADIX * 64, 512), bf16),
            DMA((3,)),
            DMA((2, 3)),
            DMA((2, 2)),
        ],
        63,
    )(cols, data, twiddle, forward, inverse)
    back = pl.pallas_call(
        tied,
        out_shape=shape((RADIX, 2 * LANES + 8, LANES)),
        in_specs=[ANY] * 2,
        out_specs=ANY,
        input_output_aliases={0: 0},
        name="tied",
    )(back, early[0, :8, :LANES] + late[0, :8, :LANES])
    lines = lax.all_to_all(back, "facet", split_axis=0, concat_axis=0, tiled=True)
    for_image, for_ahead, first_row, first_column = call(
        tile_ready,
        (
            shape((CHANNELS, LANES, 2 * LANES)),
            shape((CHANNELS, LANES, 2 * LANES)),
            shape((CHANNELS, 2 * LANES)),
            shape((CHANNELS, LANES)),
        ),
        [SM] + [VM] * 9,
        (VM,) * 4,
        [],
    )(where, *pieces, early, late, dual_field, above, left)
    below = passed_along(first_row, "facet", -1)
    right = passed_along(first_column, "chan", -1)
    slopes = call(
        rows_back,
        shape((CHANNELS, LANES + 8, 2 * LANES)),
        [VM] * 2 + [ANY] * 2,
        VM,
        [
            pltpu.VMEM((RADIX, LANES, 256), f32),
            pltpu.VMEM((LANES, LANES), f32),
            pltpu.VMEM((768, 256), bf16),
        ],
    )(lines, twiddle, below, right)
    gradient = lax.all_to_all(slopes, "chan", split_axis=0, concat_axis=0, tiled=True)
    return call(
        finish,
        (shape((CHANNELS, LANES, 2 * LANES)), shape((CHANNELS, 2, LANES, 2 * LANES), bf16)),
        [VM] * 6,
        (HBM, HBM),
        [
            pltpu.VMEM((CHANNELS, LANES + 8, 2 * LANES), f32),
            pltpu.VMEM((LANES, LANES), f32),
            pltpu.VMEM((CHANNELS, LANES, 2 * LANES), f32),
            pltpu.VMEM((CHANNELS, 2, LANES, 2 * LANES), bf16),
            DMA((8,)),
            DMA((8,)),
        ],
    )(gradient, for_image, for_ahead, dual_field, below, right)


def solution(mesh):
    placed = (
        P("chan", "facet", None),
        P("chan", None, "facet"),
        P("chan", None, None, "facet"),
        P(None, None, "facet", "chan"),
    )
    return jax.shard_map(
        shards,
        mesh=mesh,
        in_specs=placed,
        out_specs=(P(None, "facet", "chan"), P(None, None, "facet", "chan")),
        check_vma=False,
    )
```

```python
from functools import partial
import math

import jax
import jax.numpy as jnp
import numpy as np
from jax import lax
from jax.experimental import pallas as pl
from jax.experimental.pallas import tpu as pltpu
from jax.sharding import PartitionSpec as P

GRID = 2048
RADIX = 16
LANES = 128
CHANNELS = 8
EARLY = 64

step_primal = 0.5
step_dual = 0.5
clip_radius = 4.0

MIB = 1024 * 1024


def host_tables():
    index = np.arange(LANES)
    turn = 2.0 * np.pi * np.arange(RADIX + 8)[:, None] * index[None, :] / GRID
    twiddle = np.stack([np.cos(turn), np.sin(turn)]).astype(np.float32)
    place = np.zeros((LANES, LANES))
    for at in range(LANES):
        place[at, 16 * (at % 8) + at // 8] = 1.0
    return twiddle, place


def c_add(a, b):
    return (a[0] + b[0], b[1] if a[1] is None else a[1] if b[1] is None else a[1] + b[1])


def c_sub(a, b):
    imag = None
    if a[1] is not None and b[1] is not None:
        imag = a[1] - b[1]
    elif a[1] is not None:
        imag = a[1]
    elif b[1] is not None:
        imag = -b[1]
    return (a[0] - b[0], imag)


def add_turned(a, b, sign):
    real = a[0] if b[1] is None else (a[0] - b[1] if sign > 0 else a[0] + b[1])
    if a[1] is None:
        imag = b[0] if sign > 0 else -b[0]
    else:
        imag = a[1] + b[0] if sign > 0 else a[1] - b[0]
    return (real, imag)


def four(a, b, c, d, sign):
    sum_even, diff_even = c_add(a, c), c_sub(a, c)
    sum_odd, diff_odd = c_add(b, d), c_sub(b, d)
    return (
        c_add(sum_even, sum_odd),
        add_turned(diff_even, diff_odd, sign),
        c_sub(sum_even, sum_odd),
        add_turned(diff_even, diff_odd, -sign),
    )


def turned(a, power, sign):
    power = power % 16
    if power == 0:
        return a
    cos, sin = math.cos(2 * math.pi * power / 16), sign * math.sin(2 * math.pi * power / 16)
    real, imag = a
    if imag is None:
        if power == 4:
            return (jnp.zeros_like(real), real if sign > 0 else -real)
        return (real * cos, real * sin)
    if power == 4:
        return (-imag, real) if sign > 0 else (imag, -real)
    if abs(abs(cos) - abs(sin)) < 1e-9:
        root = math.sqrt(0.5)
        cs, ss = (1 if cos > 0 else -1), (1 if sin > 0 else -1)
        new_real = (real if cs > 0 else -real) - (imag if ss > 0 else -imag)
        new_imag = (real if ss > 0 else -real) + (imag if cs > 0 else -imag)
        return (new_real * root, new_imag * root)
    return (real * cos - imag * sin, real * sin + imag * cos)


def sixteen(values, sign):
    inner = [four(*(values[n0 + 4 * n1] for n1 in range(4)), sign) for n0 in range(4)]
    out = [None] * 16
    for k1 in range(4):
        parts = [turned(inner[n0][k1], n0 * k1, sign) for n0 in range(4)]
        for k2, value in enumerate(four(*parts, sign)):
            out[k1 + 4 * k2] = value
    return out


def split(value):
    high = value.astype(jnp.bfloat16)
    low = (value - high.astype(jnp.float32)).astype(jnp.bfloat16)
    return high, low


def dot(a, b, dims):
    return lax.dot_general(a, b, (dims, ((), ())), preferred_element_type=jnp.float32)


def fetched(source, target, semaphore):
    copy = pltpu.make_async_copy(source, target, semaphore)
    copy.start()
    return copy


def fill_table(table, twiddle, sign, transposed):
    shape = (LANES, LANES)
    row, col = (lax.broadcasted_iota(jnp.int32, shape, n) for n in range(2))
    at = jnp.bitwise_and(row * col, LANES - 1)
    cos, sin = (
        jnp.take_along_axis(
            jnp.broadcast_to(twiddle[n, RADIX : RADIX + 1, :], shape), at, axis=1
        )
        for n in range(2)
    )
    for n, value in enumerate((cos, sign * sin, -sign * sin, cos)):
        high, low = split(value)
        into, out = ((n // 2, n % 2), (n % 2, n // 2))[transposed]
        for m, half in enumerate((high, high, low)):
            if transposed:
                lane = 256 * m + LANES * out
                table[LANES * into : LANES * into + LANES, lane : lane + LANES] = half
            else:
                at_row = 256 * m + LANES * into
                table[at_row : at_row + LANES, LANES * out : LANES * out + LANES] = half


def three_pass(pair, table, dims):
    high = pair[:, :256] if dims[0][0] == 1 else pair[:256, :]
    return dot(pair, table[:512, :], dims) + dot(high, table[512:, :], dims)


def store_pair(held, rows, real, imag):
    high_r, low_r = split(real)
    high_i, low_i = split(imag)
    held[rows, 0:LANES] = high_r
    held[rows, LANES : 2 * LANES] = high_i
    held[rows, 2 * LANES : 3 * LANES] = low_r
    held[rows, 3 * LANES : 4 * LANES] = low_i


def cross_ready(where, image, *pieces):
    for k in range(4):
        to = (where[0] // 2 + k) % 4
        pieces[k][...] = image[:, pl.ds(pl.multiple_of(to * 512, 512), 512)]


def swap_ready(where, *refs):
    pieces, early, late = refs[:4], refs[-2], refs[-1]
    lanes = pl.ds(pl.multiple_of((1 - where[0] % 2) * 256, 256), 256)
    for k in range(4):
        early[k] = pieces[k][:EARLY, lanes]
        late[k] = pieces[k][EARLY:, lanes]


def rows_forward(
    image_in, twiddle_in, out, image, twiddle, out_v, held, table, in_sems, sems
):
    chunk = 16
    steps = LANES // chunk

    def incoming(step):
        rows = pl.ds(step * chunk, chunk)
        return pltpu.make_async_copy(image_in.at[rows, :], image.at[rows, :], in_sems.at[step])

    get_twiddle = fetched(twiddle_in, twiddle, in_sems.at[steps])
    for step in range(steps):
        incoming(step).start()
    get_twiddle.wait()
    fill_table(table, twiddle, -1, True)

    def body(step):
        incoming(step).wait()
        at = step * chunk
        values = [
            (image[pl.ds(at, chunk), b * LANES : (b + 1) * LANES], None) for b in range(RADIX)
        ]
        mixed = sixteen(values, -1)
        for f in range(RADIX):
            real, imag = mixed[f]
            if imag is None:
                imag = jnp.zeros_like(real)
            cos = twiddle[0, f : f + 1, :] * (1.0 / GRID)
            sin = twiddle[1, f : f + 1, :] * (1.0 / GRID)
            store_pair(
                held,
                pl.ds(f * LANES + at, chunk),
                real * cos + imag * sin,
                imag * cos - real * sin,
            )

    for step in range(steps):
        body(step)
    dims = ((1,), (1,))
    sent = []
    for g in range(RADIX // 2):
        pair = held[256 * g : 256 * g + 256, :]
        result = dot(table[:, :512], pair, dims) + dot(table[:, 512:], pair[:, :256], dims)
        for h in range(2):
            for c in range(2):
                block = result[c * LANES : (c + 1) * LANES, h * LANES : (h + 1) * LANES]
                out_v[:, c, 2 * g + h] = block.reshape(RADIX, 8, LANES)
        both = pl.ds(2 * g, 2)
        sent.append(fetched(out_v.at[:, :, both], out.at[:, :, both], sems.at[g]))
    for copy in sent:
        copy.wait()


def data_prepared(weights, measured, place, twiddle, out, forward, inverse, mark, held):
    mark[...] = jnp.zeros_like(mark)
    fill_table(forward, twiddle, -1, False)
    fill_table(inverse, twiddle, 1, False)
    for n in range(3):
        source = weights[...] if n == 0 else measured[n - 1]
        held[...] = source.astype(jnp.float32)
        for f in range(RADIX):
            rows = held[pl.ds(f, LANES, stride=RADIX), :].astype(jnp.bfloat16)
            out[n, f] = dot(place[...], rows, ((1,), (1,))).astype(jnp.bfloat16)


def columns(
    cols_in, data_in, twiddle_in, forward_in, inverse_in, out_all,
    cols, data, twiddle, forward, inverse, out, held_all, in_sems, chunk_sems, out_sems,
):
    chunk = 64
    steps = LANES // chunk
    dims = ((1,), (0,))

    def incoming_cols(step):
        rows = pl.ds(step * chunk, chunk)
        imag_rows = pl.ds(LANES + step * chunk, chunk)
        return [
            pltpu.make_async_copy(cols_in.at[:, r, :], cols.at[:, r, :], chunk_sems.at[step, n])
            for n, r in enumerate((rows, imag_rows))
        ]

    def incoming(step):
        rows = pl.ds(step * chunk, chunk)
        return pltpu.make_async_copy(
            data_in.at[:, :, rows, :], data.at[:, :, rows, :], chunk_sems.at[step, 2]
        )

    def outgoing(step, c):
        rows = pl.ds(c * LANES + step * chunk, chunk)
        return pltpu.make_async_copy(
            out.at[:, rows, :], out_all.at[:, rows, :], out_sems.at[step, c]
        )

    for copy in incoming_cols(0):
        copy.start()
    get_twiddle = fetched(twiddle_in, twiddle, in_sems.at[2])
    get_forward = fetched(forward_in, forward, in_sems.at[0])
    incoming(0).start()
    get_inverse = fetched(inverse_in, inverse, in_sems.at[1])
    for step in range(1, steps):
        for copy in incoming_cols(step):
            copy.start()
        incoming(step).start()
    out[:, 2 * LANES :, :] = jnp.zeros((RADIX, 8, LANES), jnp.float32)
    lane_at = lax.broadcasted_iota(jnp.int32, (8, LANES), 1)
    get_twiddle.wait()

    for step in range(steps):
        held = held_all.at[step % 2]
        at = step * chunk
        here = pl.ds(at, chunk)
        for copy in incoming_cols(step):
            copy.wait()
        imag_here = pl.ds(LANES + at, chunk)
        mixed = sixteen([(cols[b, here, :], cols[b, imag_here, :]) for b in range(RADIX)], -1)
        for f in range(RADIX):
            real, imag = mixed[f]
            cos, sin = twiddle[0, f : f + 1, :], twiddle[1, f : f + 1, :]
            rows = slice(f * chunk, (f + 1) * chunk)
            store_pair(held, rows, real * cos + imag * sin, imag * cos - real * sin)
        if step == 0:
            get_forward.wait()
            get_inverse.wait()
        spectrum = three_pass(held[...], forward, dims)
        incoming(step).wait()
        for f in range(RADIX):
            rows = slice(f * chunk, (f + 1) * chunk)
            weight = data[0, f, here, :].astype(jnp.float32)
            real = weight * spectrum[rows, :LANES] - data[1, f, here, :].astype(jnp.float32)
            imag = weight * spectrum[rows, LANES:] - data[2, f, here, :].astype(jnp.float32)
            store_pair(held, rows, real, imag)
        back = three_pass(held[...], inverse, dims)
        values = []
        for f in range(RADIX):
            rows = slice(f * chunk, (f + 1) * chunk)
            real, imag = back[rows, :LANES], back[rows, LANES:]
            cos, sin = twiddle[0, f : f + 1, :], twiddle[1, f : f + 1, :]
            values.append((real * cos - imag * sin, imag * cos + real * sin))
        mixed = sixteen(values, 1)
        for b in range(RADIX):
            for c in range(2):
                out[b, (here, imag_here)[c], :] = mixed[b][c]
                if b > 0:
                    edge = out[b - 1, 2 * LANES :, :]
                    for i in range(chunk // 8):
                        first = mixed[b][c][8 * i : 8 * i + 8, 0:1]
                        at_lane = lane_at == c * RADIX + step * (chunk // 8) + i
                        edge = jnp.where(at_lane, first, edge)
                    out[b - 1, 2 * LANES :, :] = edge
        for c in range(2):
            outgoing(step, c).start()
    rows = pl.ds(2 * LANES, 8)
    edges = fetched(out.at[:, rows, :], out_all.at[:, rows, :], in_sems.at[0])
    for step in range(steps):
        for c in range(2):
            outgoing(step, c).wait()
    edges.wait()


def tied(value, after, out):
    pass


def rows_back(lines, twiddle, after_one, after_two, out, held, side_v, table):
    fill_table(table, twiddle, 1, False)
    dims = ((0,), (0,))
    for f in range(RADIX):
        real = lines[:, 8 * f : 8 * f + 8, :].reshape(LANES, LANES)
        imag = lines[:, LANES + 8 * f : LANES + 8 * f + 8, :].reshape(LANES, LANES)
        high_r, low_r = split(real)
        high_i, low_i = split(imag)
        pair = jnp.concatenate([high_r, high_i, low_r, low_i], axis=0)
        held[f] = three_pass(pair, table, dims)
    high, low = split(lines[:, 2 * LANES :, :].reshape(LANES, LANES))
    edge = (
        dot(high, table[0:LANES, :], dims)
        + dot(low, table[0:LANES, :], dims)
        + dot(high, table[512 : 512 + LANES, :], dims)
    )
    edge_r = edge[:RADIX, :LANES] - edge[RADIX : 2 * RADIX, LANES:]
    edge_i = edge[:RADIX, LANES:] + edge[RADIX : 2 * RADIX, :LANES]
    scale = 1.0 / GRID
    cos, sin = twiddle[0, :RADIX] * scale, twiddle[1, :RADIX] * scale
    edge_r, edge_i = edge_r * cos - edge_i * sin, edge_i * cos + edge_r * sin
    mixed = sixteen([(edge_r[f : f + 1], edge_i[f : f + 1]) for f in range(RADIX)], 1)
    for d in range(CHANNELS):
        out[d, LANES : LANES + 1, :] = jnp.concatenate(
            [mixed[2 * d][0], mixed[2 * d + 1][0]], axis=1
        )
    chunk = 16
    steps = LANES // chunk
    lane_at = lax.broadcasted_iota(jnp.int32, (chunk, LANES), 1)

    def body(step):
        at = step * chunk
        here = pl.ds(at, chunk)
        values = []
        for f in range(RADIX):
            real, imag = held[f, here, :LANES], held[f, here, LANES:]
            cos, sin = twiddle[0, f : f + 1, :] * scale, twiddle[1, f : f + 1, :] * scale
            values.append((real * cos - imag * sin, imag * cos + real * sin))
        mixed = sixteen(values, 1)
        side = jnp.zeros((chunk, LANES), jnp.float32)
        for b in range(RADIX):
            low_lane = (b % 2) * LANES
            out[b // 2, here, low_lane : low_lane + LANES] = mixed[b][0]
            if b > 0 and b % 2 == 0:
                side = jnp.where(lane_at == b // 2 - 1, mixed[b][0][:, 0:1], side)
        side_v[here, :] = side

    for step in range(steps):
        body(step)
    beside = side_v[...].T
    for d in range(CHANNELS):
        out[d, LANES + 1 : LANES + 2, :LANES] = beside[d : d + 1, :]


def dual_edges(dual, last_row, last_column):
    rows, cols = [], []
    for c in range(CHANNELS):
        rows.append(dual[c, 0, 112:128, :].astype(jnp.float32)[15:16, :])
        cols.append(dual[c, 1, :, LANES:].astype(jnp.float32)[:, LANES - 1 :])
    last_row[...] = jnp.concatenate(rows, axis=0)
    last_column[...] = jnp.concatenate(cols, axis=1).T


def tile_ready(where, *refs):
    pieces, (early, late, dual, above, left) = refs[:4], refs[4:9]
    for_image, for_ahead, first_row, first_column = refs[9:]
    row_at = lax.broadcasted_iota(jnp.int32, (LANES, 2 * LANES), 0)
    lane_at = lax.broadcasted_iota(jnp.int32, (LANES, 2 * LANES), 1)
    for k in range(4):
        for other in range(2):
            half = where[0] % 2
            c = (where[0] // 2 + 4 - k) % 4 * 2 + (1 - half if other else half)
            p = dual[c, 0].astype(jnp.float32)
            q = dual[c, 1].astype(jnp.float32)
            beside = jnp.broadcast_to(left[pl.ds(c, 1), :], (LANES, LANES)).T[:, 0:1]
            prev_p = jnp.where(row_at == 0, above[pl.ds(c, 1), :], pltpu.roll(p, 1, 0))
            prev_q = jnp.where(lane_at == 0, beside, pltpu.roll(q, 1, 1))
            adjoint = prev_p - p + prev_q - q
            if other:
                image = jnp.concatenate([early[k], late[k]], axis=0)
            else:
                image = pieces[k][:, pl.ds(pl.multiple_of(half * 256, 256), 256)]
            ahead = image - adjoint
            for_image[c] = image - step_primal * adjoint
            for_ahead[c] = ahead
            first_row[pl.ds(c, 1), :] = ahead[0:1, :]
            first_column[pl.ds(c, 1), :] = ahead[:, :LANES].T[0:1, :]


def finish(
    gradient, for_image, for_ahead, dual, below, right, image_next, dual_next,
    ahead_v, side_v, image_v, dual_v, image_sems, dual_sems,
):
    sides = []
    leaving = []
    for c in range(CHANNELS):
        slope = gradient[c, :LANES, :]
        image_v[c] = for_image[c] - step_primal * slope
        leaving.append(fetched(image_v.at[c], image_next.at[c], image_sems.at[c]))
        ahead_v[c, :LANES, :] = for_ahead[c] - slope
        ahead_v[c, LANES : LANES + 1, :] = (
            below[c : c + 1, :] - gradient[c, LANES : LANES + 1, :]
        )
        sides.append(gradient[c, LANES + 1 : LANES + 2, :LANES])
    side_v[:, :CHANNELS] = (right[...] - jnp.concatenate(sides, axis=0)).T
    chunk = 16
    steps = LANES // chunk
    row_at = lax.broadcasted_iota(jnp.int32, (chunk, 2 * LANES), 0)
    lane_at = lax.broadcasted_iota(jnp.int32, (chunk, 2 * LANES), 1)

    def outgoing(step):
        rows = pl.ds(step * chunk, chunk)
        return pltpu.make_async_copy(
            dual_v.at[:, :, rows, :], dual_next.at[:, :, rows, :], dual_sems.at[step]
        )

    def body(step):
        at = step * chunk
        here = pl.ds(at, chunk)
        after = pl.ds(at + chunk, 8)
        firsts, seconds, total = [], [], None
        for c in range(CHANNELS):
            ahead = ahead_v[c, here, :]
            next_row = ahead_v[c, after, :][0:1, :]
            down = jnp.where(row_at == chunk - 1, next_row, pltpu.roll(ahead, chunk - 1, 0))
            beside = jnp.where(
                lane_at == 2 * LANES - 1,
                side_v[here, c : c + 1],
                pltpu.roll(ahead, 2 * LANES - 1, 1),
            )
            first = dual[c, 0, here, :].astype(jnp.float32) + step_dual * (down - ahead)
            second = dual[c, 1, here, :].astype(jnp.float32) + step_dual * (beside - ahead)
            firsts.append(first)
            seconds.append(second)
            squares = first * first + second * second
            total = squares if total is None else total + squares
        factor = 1.0 / jnp.maximum(1.0, jnp.sqrt(total) / clip_radius)
        for c in range(CHANNELS):
            dual_v[c, 0, here, :] = (firsts[c] * factor).astype(jnp.bfloat16)
            dual_v[c, 1, here, :] = (seconds[c] * factor).astype(jnp.bfloat16)
        outgoing(step).start()

    for step in range(steps):
        body(step)
    for copy in leaving:
        copy.wait()
    for step in range(steps):
        outgoing(step).wait()


def shape(dims, dtype=jnp.float32):
    return jax.ShapeDtypeStruct(dims, dtype)


def passed_along(x, axis, by):
    devices = lax.axis_size(axis)
    pairs = [(i, i + by) for i in range(devices) if 0 <= i + by < devices]
    return lax.ppermute(x, axis, pairs)


ANY = pl.BlockSpec(memory_space=pl.ANY)
HBM = pl.BlockSpec(memory_space=pltpu.HBM)
VM = pl.BlockSpec(memory_space=pltpu.VMEM)
SM = pl.BlockSpec(memory_space=pltpu.SMEM)
DMA = pltpu.SemaphoreType.DMA


def call(kernel, out_shape, in_specs, out_specs, scratch, limit=16):
    return pl.pallas_call(
        kernel,
        out_shape=out_shape,
        in_specs=in_specs,
        out_specs=out_specs,
        scratch_shapes=scratch,
        name=kernel.__name__,
        compiler_params=pltpu.CompilerParams(vmem_limit_bytes=limit * MIB),
    )


def shards(image_field, weights, measured, dual_field):
    twiddle, place = host_tables()
    place = jnp.asarray(place, jnp.bfloat16)
    twiddle = jnp.asarray(twiddle)
    image = image_field[0]
    f32, bf16 = jnp.float32, jnp.bfloat16
    where = lax.axis_index("chan").astype(jnp.int32).reshape(1)

    spread = call(
        rows_forward,
        shape((RADIX, 2, RADIX, 8, LANES)),
        [HBM, HBM],
        HBM,
        [
            pltpu.VMEM((LANES, GRID), f32),
            pltpu.VMEM((2, RADIX + 8, LANES), f32),
            pltpu.VMEM((RADIX, 2, RADIX, 8, LANES), f32),
            pltpu.VMEM((GRID, 512), bf16),
            pltpu.VMEM((256, 768), bf16),
            DMA((9,)),
            DMA((8,)),
        ],
        63,
    )(image, twiddle)
    cols = lax.all_to_all(
        spread.reshape(RADIX, 2 * LANES, LANES), "facet", split_axis=0, concat_axis=0, tiled=True
    )
    last_row, last_column = call(
        dual_edges,
        (shape((CHANNELS, 2 * LANES)), shape((CHANNELS, LANES))),
        [VM],
        (VM, VM),
        [],
    )(dual_field)
    above = passed_along(last_row, "facet", 1)
    left = passed_along(last_column, "chan", 1)
    pieces = list(
        call(cross_ready, (shape((LANES, 512)),) * 4, [SM, VM], (VM,) * 4, [])(where, image)
    )
    for k in range(1, 4):
        pairs = [(2 * x + z, (x + k) % 4 * 2 + z) for x in range(4) for z in range(2)]
        pieces[k] = lax.ppermute(pieces[k], "chan", pairs)
    data, forward, inverse, mark = call(
        data_prepared,
        (
            shape((3, RADIX, LANES, LANES), bf16),
            shape((768, 256), bf16),
            shape((768, 256), bf16),
            shape((8, LANES)),
        ),
        [VM] * 4,
        (VM,) * 4,
        [pltpu.VMEM((GRID, LANES), f32)],
        63,
    )(weights[0], measured[0], place, twiddle)
    early, late = call(
        swap_ready,
        (shape((4, EARLY, 256)), shape((4, LANES - EARLY, 256))),
        [SM] + [VM] * 4 + [ANY] * 2,
        (VM, VM),
        [],
    )(where, *pieces, mark, last_row)
    other_zl = [(i, i ^ 1) for i in range(8)]
    early = lax.ppermute(early, "chan", other_zl)
    cols, late, above, left, data, forward, inverse = lax.optimization_barrier(
        (cols, late, above, left, data, forward, inverse)
    )
    late = lax.ppermute(late, "chan", other_zl)
    data, forward, inverse = (
        pltpu.with_memory_space_constraint(x, pltpu.HBM) for x in (data, forward, inverse)
    )
    back = call(
        columns,
        shape((RADIX, 2 * LANES + 8, LANES)),
        [HBM] * 5,
        HBM,
        [
            pltpu.VMEM((RADIX, 2 * LANES, LANES), f32),
            pltpu.VMEM((3, RADIX, LANES, LANES), bf16),
            pltpu.VMEM((2, RADIX + 8, LANES), f32),
            pltpu.VMEM((768, 256), bf16),
            pltpu.VMEM((768, 256), bf16),
            pltpu.VMEM((RADIX, 2 * LANES + 8, LANES), f32),
            pltpu.VMEM((2, RADIX * 64, 512), bf16),
            DMA((3,)),
            DMA((2, 3)),
            DMA((2, 2)),
        ],
        63,
    )(cols, data, twiddle, forward, inverse)
    back = pl.pallas_call(
        tied,
        out_shape=shape((RADIX, 2 * LANES + 8, LANES)),
        in_specs=[ANY] * 2,
        out_specs=ANY,
        input_output_aliases={0: 0},
        name="tied",
    )(back, early[0, :8, :LANES] + late[0, :8, :LANES])
    lines = lax.all_to_all(back, "facet", split_axis=0, concat_axis=0, tiled=True)
    for_image, for_ahead, first_row, first_column = call(
        tile_ready,
        (
            shape((CHANNELS, LANES, 2 * LANES)),
            shape((CHANNELS, LANES, 2 * LANES)),
            shape((CHANNELS, 2 * LANES)),
            shape((CHANNELS, LANES)),
        ),
        [SM] + [VM] * 9,
        (VM,) * 4,
        [],
    )(where, *pieces, early, late, dual_field, above, left)
    below = passed_along(first_row, "facet", -1)
    right = passed_along(first_column, "chan", -1)
    slopes = call(
        rows_back,
        shape((CHANNELS, LANES + 8, 2 * LANES)),
        [VM] * 2 + [ANY] * 2,
        VM,
        [
            pltpu.VMEM((RADIX, LANES, 256), f32),
            pltpu.VMEM((LANES, LANES), f32),
            pltpu.VMEM((768, 256), bf16),
        ],
    )(lines, twiddle, below, right)
    gradient = lax.all_to_all(slopes, "chan", split_axis=0, concat_axis=0, tiled=True)
    return call(
        finish,
        (shape((CHANNELS, LANES, 2 * LANES)), shape((CHANNELS, 2, LANES, 2 * LANES), bf16)),
        [VM] * 6,
        (HBM, HBM),
        [
            pltpu.VMEM((CHANNELS, LANES + 8, 2 * LANES), f32),
            pltpu.VMEM((LANES, LANES), f32),
            pltpu.VMEM((CHANNELS, LANES, 2 * LANES), f32),
            pltpu.VMEM((CHANNELS, 2, LANES, 2 * LANES), bf16),
            DMA((8,)),
            DMA((8,)),
        ],
    )(gradient, for_image, for_ahead, dual_field, below, right)


def solution(mesh):
    placed = (
        P("chan", "facet", None),
        P("chan", None, "facet"),
        P("chan", None, None, "facet"),
        P(None, None, "facet", "chan"),
    )
    return jax.shard_map(
        shards,
        mesh=mesh,
        in_specs=placed,
        out_specs=(P(None, "facet", "chan"), P(None, None, "facet", "chan")),
        check_vma=False,
    )
```

```python
from functools import partial
import math

import jax
import jax.numpy as jnp
import numpy as np
from jax import lax
from jax.experimental import pallas as pl
from jax.experimental.pallas import tpu as pltpu
from jax.sharding import PartitionSpec as P

GRID = 2048
RADIX = 16
LANES = 128
CHANNELS = 8
EARLY = 64

step_primal = 0.5
step_dual = 0.5
clip_radius = 4.0

MIB = 1024 * 1024


def host_tables():
    index = np.arange(LANES)
    turn = 2.0 * np.pi * np.arange(RADIX + 8)[:, None] * index[None, :] / GRID
    twiddle = np.stack([np.cos(turn), np.sin(turn)]).astype(np.float32)
    place = np.zeros((LANES, LANES))
    for at in range(LANES):
        place[at, 16 * (at % 8) + at // 8] = 1.0
    return twiddle, place


def c_add(a, b):
    return (a[0] + b[0], b[1] if a[1] is None else a[1] if b[1] is None else a[1] + b[1])


def c_sub(a, b):
    imag = None
    if a[1] is not None and b[1] is not None:
        imag = a[1] - b[1]
    elif a[1] is not None:
        imag = a[1]
    elif b[1] is not None:
        imag = -b[1]
    return (a[0] - b[0], imag)


def add_turned(a, b, sign):
    real = a[0] if b[1] is None else (a[0] - b[1] if sign > 0 else a[0] + b[1])
    if a[1] is None:
        imag = b[0] if sign > 0 else -b[0]
    else:
        imag = a[1] + b[0] if sign > 0 else a[1] - b[0]
    return (real, imag)


def four(a, b, c, d, sign):
    sum_even, diff_even = c_add(a, c), c_sub(a, c)
    sum_odd, diff_odd = c_add(b, d), c_sub(b, d)
    return (
        c_add(sum_even, sum_odd),
        add_turned(diff_even, diff_odd, sign),
        c_sub(sum_even, sum_odd),
        add_turned(diff_even, diff_odd, -sign),
    )


def turned(a, power, sign):
    power = power % 16
    if power == 0:
        return a
    cos, sin = math.cos(2 * math.pi * power / 16), sign * math.sin(2 * math.pi * power / 16)
    real, imag = a
    if imag is None:
        if power == 4:
            return (jnp.zeros_like(real), real if sign > 0 else -real)
        return (real * cos, real * sin)
    if power == 4:
        return (-imag, real) if sign > 0 else (imag, -real)
    if abs(abs(cos) - abs(sin)) < 1e-9:
        root = math.sqrt(0.5)
        cs, ss = (1 if cos > 0 else -1), (1 if sin > 0 else -1)
        new_real = (real if cs > 0 else -real) - (imag if ss > 0 else -imag)
        new_imag = (real if ss > 0 else -real) + (imag if cs > 0 else -imag)
        return (new_real * root, new_imag * root)
    return (real * cos - imag * sin, real * sin + imag * cos)


def sixteen(values, sign):
    inner = [four(*(values[n0 + 4 * n1] for n1 in range(4)), sign) for n0 in range(4)]
    out = [None] * 16
    for k1 in range(4):
        parts = [turned(inner[n0][k1], n0 * k1, sign) for n0 in range(4)]
        for k2, value in enumerate(four(*parts, sign)):
            out[k1 + 4 * k2] = value
    return out


def split(value):
    high = value.astype(jnp.bfloat16)
    low = (value - high.astype(jnp.float32)).astype(jnp.bfloat16)
    return high, low


def dot(a, b, dims):
    return lax.dot_general(a, b, (dims, ((), ())), preferred_element_type=jnp.float32)


def fetched(source, target, semaphore):
    copy = pltpu.make_async_copy(source, target, semaphore)
    copy.start()
    return copy


def fill_table(table, twiddle, sign, transposed):
    shape = (LANES, LANES)
    row, col = (lax.broadcasted_iota(jnp.int32, shape, n) for n in range(2))
    at = jnp.bitwise_and(row * col, LANES - 1)
    cos, sin = (
        jnp.take_along_axis(
            jnp.broadcast_to(twiddle[n, RADIX : RADIX + 1, :], shape), at, axis=1
        )
        for n in range(2)
    )
    for n, value in enumerate((cos, sign * sin, -sign * sin, cos)):
        high, low = split(value)
        into, out = ((n // 2, n % 2), (n % 2, n // 2))[transposed]
        for m, half in enumerate((high, high, low)):
            if transposed:
                lane = 256 * m + LANES * out
                table[LANES * into : LANES * into + LANES, lane : lane + LANES] = half
            else:
                at_row = 256 * m + LANES * into
                table[at_row : at_row + LANES, LANES * out : LANES * out + LANES] = half


def three_pass(pair, table, dims):
    high = pair[:, :256] if dims[0][0] == 1 else pair[:256, :]
    return dot(pair, table[:512, :], dims) + dot(high, table[512:, :], dims)


def store_pair(held, rows, real, imag):
    high_r, low_r = split(real)
    high_i, low_i = split(imag)
    held[rows, 0:LANES] = high_r
    held[rows, LANES : 2 * LANES] = high_i
    held[rows, 2 * LANES : 3 * LANES] = low_r
    held[rows, 3 * LANES : 4 * LANES] = low_i


def cross_ready(where, image, *pieces):
    for k in range(4):
        to = (where[0] // 2 + k) % 4
        pieces[k][...] = image[:, pl.ds(pl.multiple_of(to * 512, 512), 512)]


def swap_ready(where, *refs):
    pieces, early, late = refs[:4], refs[-2], refs[-1]
    lanes = pl.ds(pl.multiple_of((1 - where[0] % 2) * 256, 256), 256)
    for k in range(4):
        early[k] = pieces[k][:EARLY, lanes]
        late[k] = pieces[k][EARLY:, lanes]


def rows_forward(
    image_in, twiddle_in, out, image, twiddle, out_v, held, table, in_sems, sems
):
    chunk = 16
    steps = LANES // chunk

    def incoming(step):
        rows = pl.ds(step * chunk, chunk)
        return pltpu.make_async_copy(image_in.at[rows, :], image.at[rows, :], in_sems.at[step])

    get_twiddle = fetched(twiddle_in, twiddle, in_sems.at[steps])
    for step in range(steps):
        incoming(step).start()
    get_twiddle.wait()
    fill_table(table, twiddle, -1, True)

    def body(step):
        incoming(step).wait()
        at = step * chunk
        values = [
            (image[pl.ds(at, chunk), b * LANES : (b + 1) * LANES], None) for b in range(RADIX)
        ]
        mixed = sixteen(values, -1)
        for f in range(RADIX):
            real, imag = mixed[f]
            if imag is None:
                imag = jnp.zeros_like(real)
            cos = twiddle[0, f : f + 1, :] * (1.0 / GRID)
            sin = twiddle[1, f : f + 1, :] * (1.0 / GRID)
            store_pair(
                held,
                pl.ds(f * LANES + at, chunk),
                real * cos + imag * sin,
                imag * cos - real * sin,
            )

    for step in range(steps):
        body(step)
    dims = ((1,), (1,))
    sent = []
    for g in range(RADIX // 2):
        pair = held[256 * g : 256 * g + 256, :]
        result = dot(table[:, :512], pair, dims) + dot(table[:, 512:], pair[:, :256], dims)
        for h in range(2):
            for c in range(2):
                block = result[c * LANES : (c + 1) * LANES, h * LANES : (h + 1) * LANES]
                out_v[:, c, 2 * g + h] = block.reshape(RADIX, 8, LANES)
        both = pl.ds(2 * g, 2)
        sent.append(fetched(out_v.at[:, :, both], out.at[:, :, both], sems.at[g]))
    for copy in sent:
        copy.wait()


def data_prepared(weights, measured, place, twiddle, out, forward, inverse, mark, held):
    mark[...] = jnp.zeros_like(mark)
    fill_table(forward, twiddle, -1, False)
    fill_table(inverse, twiddle, 1, False)
    for n in range(3):
        source = weights[...] if n == 0 else measured[n - 1]
        held[...] = source.astype(jnp.float32)
        for f in range(RADIX):
            rows = held[pl.ds(f, LANES, stride=RADIX), :].astype(jnp.bfloat16)
            out[n, f] = dot(place[...], rows, ((1,), (1,))).astype(jnp.bfloat16)


def columns(
    cols_in, data_in, twiddle_in, forward_in, inverse_in, out_all,
    cols, data, twiddle, forward, inverse, out, held_all, in_sems, chunk_sems, out_sems,
):
    chunk = 64
    steps = LANES // chunk
    dims = ((1,), (0,))

    def incoming_cols(step):
        rows = pl.ds(step * chunk, chunk)
        imag_rows = pl.ds(LANES + step * chunk, chunk)
        return [
            pltpu.make_async_copy(cols_in.at[:, r, :], cols.at[:, r, :], chunk_sems.at[step, n])
            for n, r in enumerate((rows, imag_rows))
        ]

    def incoming(step):
        rows = pl.ds(step * chunk, chunk)
        return pltpu.make_async_copy(
            data_in.at[:, :, rows, :], data.at[:, :, rows, :], chunk_sems.at[step, 2]
        )

    def outgoing(step, c):
        rows = pl.ds(c * LANES + step * chunk, chunk)
        return pltpu.make_async_copy(
            out.at[:, rows, :], out_all.at[:, rows, :], out_sems.at[step, c]
        )

    for copy in incoming_cols(0):
        copy.start()
    get_twiddle = fetched(twiddle_in, twiddle, in_sems.at[2])
    get_forward = fetched(forward_in, forward, in_sems.at[0])
    incoming(0).start()
    get_inverse = fetched(inverse_in, inverse, in_sems.at[1])
    for step in range(1, steps):
        for copy in incoming_cols(step):
            copy.start()
        incoming(step).start()
    out[:, 2 * LANES :, :] = jnp.zeros((RADIX, 8, LANES), jnp.float32)
    lane_at = lax.broadcasted_iota(jnp.int32, (8, LANES), 1)
    get_twiddle.wait()

    for step in range(steps):
        held = held_all.at[step % 2]
        at = step * chunk
        here = pl.ds(at, chunk)
        for copy in incoming_cols(step):
            copy.wait()
        imag_here = pl.ds(LANES + at, chunk)
        mixed = sixteen([(cols[b, here, :], cols[b, imag_here, :]) for b in range(RADIX)], -1)
        for f in range(RADIX):
            real, imag = mixed[f]
            cos, sin = twiddle[0, f : f + 1, :], twiddle[1, f : f + 1, :]
            rows = slice(f * chunk, (f + 1) * chunk)
            store_pair(held, rows, real * cos + imag * sin, imag * cos - real * sin)
        if step == 0:
            get_forward.wait()
            get_inverse.wait()
        spectrum = three_pass(held[...], forward, dims)
        incoming(step).wait()
        for f in range(RADIX):
            rows = slice(f * chunk, (f + 1) * chunk)
            weight = data[0, f, here, :].astype(jnp.float32)
            real = weight * spectrum[rows, :LANES] - data[1, f, here, :].astype(jnp.float32)
            imag = weight * spectrum[rows, LANES:] - data[2, f, here, :].astype(jnp.float32)
            store_pair(held, rows, real, imag)
        back = three_pass(held[...], inverse, dims)
        values = []
        for f in range(RADIX):
            rows = slice(f * chunk, (f + 1) * chunk)
            real, imag = back[rows, :LANES], back[rows, LANES:]
            cos, sin = twiddle[0, f : f + 1, :], twiddle[1, f : f + 1, :]
            values.append((real * cos - imag * sin, imag * cos + real * sin))
        mixed = sixteen(values, 1)
        for b in range(RADIX):
            for c in range(2):
                out[b, (here, imag_here)[c], :] = mixed[b][c]
                if b > 0:
                    edge = out[b - 1, 2 * LANES :, :]
                    for i in range(chunk // 8):
                        first = mixed[b][c][8 * i : 8 * i + 8, 0:1]
                        at_lane = lane_at == c * RADIX + step * (chunk // 8) + i
                        edge = jnp.where(at_lane, first, edge)
                    out[b - 1, 2 * LANES :, :] = edge
        for c in range(2):
            outgoing(step, c).start()
    rows = pl.ds(2 * LANES, 8)
    edges = fetched(out.at[:, rows, :], out_all.at[:, rows, :], in_sems.at[0])
    for step in range(steps):
        for c in range(2):
            outgoing(step, c).wait()
    edges.wait()


def arrived(early, late, out):
    out[...] = early[0, :8, :LANES] + late[0, :8, :LANES]


def tied(value, after, out):
    pass


def rows_back(lines, twiddle, after_one, after_two, out, held, side_v, table):
    fill_table(table, twiddle, 1, False)
    dims = ((0,), (0,))
    for f in range(RADIX):
        real = lines[:, 8 * f : 8 * f + 8, :].reshape(LANES, LANES)
        imag = lines[:, LANES + 8 * f : LANES + 8 * f + 8, :].reshape(LANES, LANES)
        high_r, low_r = split(real)
        high_i, low_i = split(imag)
        pair = jnp.concatenate([high_r, high_i, low_r, low_i], axis=0)
        held[f] = three_pass(pair, table, dims)
    high, low = split(lines[:, 2 * LANES :, :].reshape(LANES, LANES))
    edge = (
        dot(high, table[0:LANES, :], dims)
        + dot(low, table[0:LANES, :], dims)
        + dot(high, table[512 : 512 + LANES, :], dims)
    )
    edge_r = edge[:RADIX, :LANES] - edge[RADIX : 2 * RADIX, LANES:]
    edge_i = edge[:RADIX, LANES:] + edge[RADIX : 2 * RADIX, :LANES]
    scale = 1.0 / GRID
    cos, sin = twiddle[0, :RADIX] * scale, twiddle[1, :RADIX] * scale
    edge_r, edge_i = edge_r * cos - edge_i * sin, edge_i * cos + edge_r * sin
    mixed = sixteen([(edge_r[f : f + 1], edge_i[f : f + 1]) for f in range(RADIX)], 1)
    for d in range(CHANNELS):
        out[d, LANES : LANES + 1, :] = jnp.concatenate(
            [mixed[2 * d][0], mixed[2 * d + 1][0]], axis=1
        )
    chunk = 16
    steps = LANES // chunk
    lane_at = lax.broadcasted_iota(jnp.int32, (chunk, LANES), 1)

    def body(step):
        at = step * chunk
        here = pl.ds(at, chunk)
        values = []
        for f in range(RADIX):
            real, imag = held[f, here, :LANES], held[f, here, LANES:]
            cos, sin = twiddle[0, f : f + 1, :] * scale, twiddle[1, f : f + 1, :] * scale
            values.append((real * cos - imag * sin, imag * cos + real * sin))
        mixed = sixteen(values, 1)
        side = jnp.zeros((chunk, LANES), jnp.float32)
        for b in range(RADIX):
            low_lane = (b % 2) * LANES
            out[b // 2, here, low_lane : low_lane + LANES] = mixed[b][0]
            if b > 0 and b % 2 == 0:
                side = jnp.where(lane_at == b // 2 - 1, mixed[b][0][:, 0:1], side)
        side_v[here, :] = side

    for step in range(steps):
        body(step)
    beside = side_v[...].T
    for d in range(CHANNELS):
        out[d, LANES + 1 : LANES + 2, :LANES] = beside[d : d + 1, :]


def dual_edges(dual, last_row, last_column):
    rows, cols = [], []
    for c in range(CHANNELS):
        rows.append(dual[c, 0, 112:128, :].astype(jnp.float32)[15:16, :])
        cols.append(dual[c, 1, :, LANES:].astype(jnp.float32)[:, LANES - 1 :])
    last_row[...] = jnp.concatenate(rows, axis=0)
    last_column[...] = jnp.concatenate(cols, axis=1).T


def tile_ready(where, *refs):
    pieces, (early, late, dual, above, left) = refs[:4], refs[4:9]
    for_image, for_ahead, first_row, first_column = refs[9:]
    row_at = lax.broadcasted_iota(jnp.int32, (LANES, 2 * LANES), 0)
    lane_at = lax.broadcasted_iota(jnp.int32, (LANES, 2 * LANES), 1)
    for k in range(4):
        for other in range(2):
            half = where[0] % 2
            c = (where[0] // 2 + 4 - k) % 4 * 2 + (1 - half if other else half)
            p = dual[c, 0].astype(jnp.float32)
            q = dual[c, 1].astype(jnp.float32)
            beside = jnp.broadcast_to(left[pl.ds(c, 1), :], (LANES, LANES)).T[:, 0:1]
            prev_p = jnp.where(row_at == 0, above[pl.ds(c, 1), :], pltpu.roll(p, 1, 0))
            prev_q = jnp.where(lane_at == 0, beside, pltpu.roll(q, 1, 1))
            adjoint = prev_p - p + prev_q - q
            if other:
                image = jnp.concatenate([early[k], late[k]], axis=0)
            else:
                image = pieces[k][:, pl.ds(pl.multiple_of(half * 256, 256), 256)]
            ahead = image - adjoint
            for_image[c] = image - step_primal * adjoint
            for_ahead[c] = ahead
            first_row[pl.ds(c, 1), :] = ahead[0:1, :]
            first_column[pl.ds(c, 1), :] = ahead[:, :LANES].T[0:1, :]


def finish(
    gradient, for_image, for_ahead, dual, below, right, image_next, dual_next,
    ahead_v, side_v, image_v, dual_v, image_sems, dual_sems,
):
    sides = []
    leaving = []
    for c in range(CHANNELS):
        slope = gradient[c, :LANES, :]
        image_v[c] = for_image[c] - step_primal * slope
        leaving.append(fetched(image_v.at[c], image_next.at[c], image_sems.at[c]))
        ahead_v[c, :LANES, :] = for_ahead[c] - slope
        ahead_v[c, LANES : LANES + 1, :] = (
            below[c : c + 1, :] - gradient[c, LANES : LANES + 1, :]
        )
        sides.append(gradient[c, LANES + 1 : LANES + 2, :LANES])
    side_v[:, :CHANNELS] = (right[...] - jnp.concatenate(sides, axis=0)).T
    chunk = 16
    steps = LANES // chunk
    row_at = lax.broadcasted_iota(jnp.int32, (chunk, 2 * LANES), 0)
    lane_at = lax.broadcasted_iota(jnp.int32, (chunk, 2 * LANES), 1)

    def outgoing(step):
        rows = pl.ds(step * chunk, chunk)
        return pltpu.make_async_copy(
            dual_v.at[:, :, rows, :], dual_next.at[:, :, rows, :], dual_sems.at[step]
        )

    def body(step):
        at = step * chunk
        here = pl.ds(at, chunk)
        after = pl.ds(at + chunk, 8)
        firsts, seconds, total = [], [], None
        for c in range(CHANNELS):
            ahead = ahead_v[c, here, :]
            next_row = ahead_v[c, after, :][0:1, :]
            down = jnp.where(row_at == chunk - 1, next_row, pltpu.roll(ahead, chunk - 1, 0))
            beside = jnp.where(
                lane_at == 2 * LANES - 1,
                side_v[here, c : c + 1],
                pltpu.roll(ahead, 2 * LANES - 1, 1),
            )
            first = dual[c, 0, here, :].astype(jnp.float32) + step_dual * (down - ahead)
            second = dual[c, 1, here, :].astype(jnp.float32) + step_dual * (beside - ahead)
            firsts.append(first)
            seconds.append(second)
            squares = first * first + second * second
            total = squares if total is None else total + squares
        factor = 1.0 / jnp.maximum(1.0, jnp.sqrt(total) / clip_radius)
        for c in range(CHANNELS):
            dual_v[c, 0, here, :] = (firsts[c] * factor).astype(jnp.bfloat16)
            dual_v[c, 1, here, :] = (seconds[c] * factor).astype(jnp.bfloat16)
        outgoing(step).start()

    for step in range(steps):
        body(step)
    for copy in leaving:
        copy.wait()
    for step in range(steps):
        outgoing(step).wait()


def shape(dims, dtype=jnp.float32):
    return jax.ShapeDtypeStruct(dims, dtype)


def passed_along(x, axis, by):
    devices = lax.axis_size(axis)
    pairs = [(i, i + by) for i in range(devices) if 0 <= i + by < devices]
    return lax.ppermute(x, axis, pairs)


ANY = pl.BlockSpec(memory_space=pl.ANY)
HBM = pl.BlockSpec(memory_space=pltpu.HBM)
VM = pl.BlockSpec(memory_space=pltpu.VMEM)
SM = pl.BlockSpec(memory_space=pltpu.SMEM)
DMA = pltpu.SemaphoreType.DMA


def call(kernel, out_shape, in_specs, out_specs, scratch, limit=16):
    return pl.pallas_call(
        kernel,
        out_shape=out_shape,
        in_specs=in_specs,
        out_specs=out_specs,
        scratch_shapes=scratch,
        name=kernel.__name__,
        compiler_params=pltpu.CompilerParams(vmem_limit_bytes=limit * MIB),
    )


def shards(image_field, weights, measured, dual_field):
    twiddle, place = host_tables()
    place = jnp.asarray(place, jnp.bfloat16)
    twiddle = jnp.asarray(twiddle)
    image = image_field[0]
    f32, bf16 = jnp.float32, jnp.bfloat16
    where = lax.axis_index("chan").astype(jnp.int32).reshape(1)

    spread = call(
        rows_forward,
        shape((RADIX, 2, RADIX, 8, LANES)),
        [HBM, HBM],
        HBM,
        [
            pltpu.VMEM((LANES, GRID), f32),
            pltpu.VMEM((2, RADIX + 8, LANES), f32),
            pltpu.VMEM((RADIX, 2, RADIX, 8, LANES), f32),
            pltpu.VMEM((GRID, 512), bf16),
            pltpu.VMEM((256, 768), bf16),
            DMA((9,)),
            DMA((8,)),
        ],
        63,
    )(image, twiddle)
    cols = lax.all_to_all(
        spread.reshape(RADIX, 2 * LANES, LANES), "facet", split_axis=0, concat_axis=0, tiled=True
    )
    last_row, last_column = call(
        dual_edges,
        (shape((CHANNELS, 2 * LANES)), shape((CHANNELS, LANES))),
        [VM],
        (VM, VM),
        [],
    )(dual_field)
    above = passed_along(last_row, "facet", 1)
    left = passed_along(last_column, "chan", 1)
    pieces = list(
        call(cross_ready, (shape((LANES, 512)),) * 4, [SM, VM], (VM,) * 4, [])(where, image)
    )
    for k in range(1, 4):
        pairs = [(2 * x + z, (x + k) % 4 * 2 + z) for x in range(4) for z in range(2)]
        pieces[k] = lax.ppermute(pieces[k], "chan", pairs)
    data, forward, inverse, mark = call(
        data_prepared,
        (
            shape((3, RADIX, LANES, LANES), bf16),
            shape((768, 256), bf16),
            shape((768, 256), bf16),
            shape((8, LANES)),
        ),
        [VM] * 4,
        (VM,) * 4,
        [pltpu.VMEM((GRID, LANES), f32)],
        63,
    )(weights[0], measured[0], place, twiddle)
    early, late = call(
        swap_ready,
        (shape((4, EARLY, 256)), shape((4, LANES - EARLY, 256))),
        [SM] + [VM] * 4 + [ANY] * 2,
        (VM, VM),
        [],
    )(where, *pieces, mark, last_row)
    other_zl = [(i, i ^ 1) for i in range(8)]
    early = lax.ppermute(early, "chan", other_zl)
    cols, late, above, left, data, forward, inverse = lax.optimization_barrier(
        (cols, late, above, left, data, forward, inverse)
    )
    late = lax.ppermute(late, "chan", other_zl)
    data, forward, inverse = (
        pltpu.with_memory_space_constraint(x, pltpu.HBM) for x in (data, forward, inverse)
    )
    back = call(
        columns,
        shape((RADIX, 2 * LANES + 8, LANES)),
        [HBM] * 5,
        HBM,
        [
            pltpu.VMEM((RADIX, 2 * LANES, LANES), f32),
            pltpu.VMEM((3, RADIX, LANES, LANES), bf16),
            pltpu.VMEM((2, RADIX + 8, LANES), f32),
            pltpu.VMEM((768, 256), bf16),
            pltpu.VMEM((768, 256), bf16),
            pltpu.VMEM((RADIX, 2 * LANES + 8, LANES), f32),
            pltpu.VMEM((2, RADIX * 64, 512), bf16),
            DMA((3,)),
            DMA((2, 3)),
            DMA((2, 2)),
        ],
        63,
    )(cols, data, twiddle, forward, inverse)
    mark = call(arrived, shape((8, LANES)), [VM, VM], VM, [])(early, late)
    back = pl.pallas_call(
        tied,
        out_shape=shape((RADIX, 2 * LANES + 8, LANES)),
        in_specs=[ANY] * 2,
        out_specs=ANY,
        input_output_aliases={0: 0},
        name="tied",
    )(back, mark)
    lines = lax.all_to_all(back, "facet", split_axis=0, concat_axis=0, tiled=True)
    for_image, for_ahead, first_row, first_column = call(
        tile_ready,
        (
            shape((CHANNELS, LANES, 2 * LANES)),
            shape((CHANNELS, LANES, 2 * LANES)),
            shape((CHANNELS, 2 * LANES)),
            shape((CHANNELS, LANES)),
        ),
        [SM] + [VM] * 9,
        (VM,) * 4,
        [],
    )(where, *pieces, early, late, dual_field, above, left)
    below = passed_along(first_row, "facet", -1)
    right = passed_along(first_column, "chan", -1)
    slopes = call(
        rows_back,
        shape((CHANNELS, LANES + 8, 2 * LANES)),
        [VM] * 2 + [ANY] * 2,
        VM,
        [
            pltpu.VMEM((RADIX, LANES, 256), f32),
            pltpu.VMEM((LANES, LANES), f32),
            pltpu.VMEM((768, 256), bf16),
        ],
    )(lines, twiddle, below, right)
    gradient = lax.all_to_all(slopes, "chan", split_axis=0, concat_axis=0, tiled=True)
    return call(
        finish,
        (shape((CHANNELS, LANES, 2 * LANES)), shape((CHANNELS, 2, LANES, 2 * LANES), bf16)),
        [VM] * 6,
        (HBM, HBM),
        [
            pltpu.VMEM((CHANNELS, LANES + 8, 2 * LANES), f32),
            pltpu.VMEM((LANES, LANES), f32),
            pltpu.VMEM((CHANNELS, LANES, 2 * LANES), f32),
            pltpu.VMEM((CHANNELS, 2, LANES, 2 * LANES), bf16),
            DMA((8,)),
            DMA((8,)),
        ],
    )(gradient, for_image, for_ahead, dual_field, below, right)


def solution(mesh):
    placed = (
        P("chan", "facet", None),
        P("chan", None, "facet"),
        P("chan", None, None, "facet"),
        P(None, None, "facet", "chan"),
    )
    return jax.shard_map(
        shards,
        mesh=mesh,
        in_specs=placed,
        out_specs=(P(None, "facet", "chan"), P(None, None, "facet", "chan")),
        check_vma=False,
    )
```

```python
from functools import partial
import math

import jax
import jax.numpy as jnp
import numpy as np
from jax import lax
from jax.experimental import pallas as pl
from jax.experimental.pallas import tpu as pltpu
from jax.sharding import PartitionSpec as P

GRID = 2048
RADIX = 16
LANES = 128
CHANNELS = 8
EARLY = 64

step_primal = 0.5
step_dual = 0.5
clip_radius = 4.0

MIB = 1024 * 1024


def host_tables():
    index = np.arange(LANES)
    turn = 2.0 * np.pi * np.arange(RADIX + 8)[:, None] * index[None, :] / GRID
    twiddle = np.stack([np.cos(turn), np.sin(turn)]).astype(np.float32)
    place = np.zeros((LANES, LANES))
    for at in range(LANES):
        place[at, 16 * (at % 8) + at // 8] = 1.0
    return twiddle, place


def c_add(a, b):
    return (a[0] + b[0], b[1] if a[1] is None else a[1] if b[1] is None else a[1] + b[1])


def c_sub(a, b):
    imag = None
    if a[1] is not None and b[1] is not None:
        imag = a[1] - b[1]
    elif a[1] is not None:
        imag = a[1]
    elif b[1] is not None:
        imag = -b[1]
    return (a[0] - b[0], imag)


def add_turned(a, b, sign):
    real = a[0] if b[1] is None else (a[0] - b[1] if sign > 0 else a[0] + b[1])
    if a[1] is None:
        imag = b[0] if sign > 0 else -b[0]
    else:
        imag = a[1] + b[0] if sign > 0 else a[1] - b[0]
    return (real, imag)


def four(a, b, c, d, sign):
    sum_even, diff_even = c_add(a, c), c_sub(a, c)
    sum_odd, diff_odd = c_add(b, d), c_sub(b, d)
    return (
        c_add(sum_even, sum_odd),
        add_turned(diff_even, diff_odd, sign),
        c_sub(sum_even, sum_odd),
        add_turned(diff_even, diff_odd, -sign),
    )


def turned(a, power, sign):
    power = power % 16
    if power == 0:
        return a
    cos, sin = math.cos(2 * math.pi * power / 16), sign * math.sin(2 * math.pi * power / 16)
    real, imag = a
    if imag is None:
        if power == 4:
            return (jnp.zeros_like(real), real if sign > 0 else -real)
        return (real * cos, real * sin)
    if power == 4:
        return (-imag, real) if sign > 0 else (imag, -real)
    if abs(abs(cos) - abs(sin)) < 1e-9:
        root = math.sqrt(0.5)
        cs, ss = (1 if cos > 0 else -1), (1 if sin > 0 else -1)
        new_real = (real if cs > 0 else -real) - (imag if ss > 0 else -imag)
        new_imag = (real if ss > 0 else -real) + (imag if cs > 0 else -imag)
        return (new_real * root, new_imag * root)
    return (real * cos - imag * sin, real * sin + imag * cos)


def sixteen(values, sign):
    inner = [four(*(values[n0 + 4 * n1] for n1 in range(4)), sign) for n0 in range(4)]
    out = [None] * 16
    for k1 in range(4):
        parts = [turned(inner[n0][k1], n0 * k1, sign) for n0 in range(4)]
        for k2, value in enumerate(four(*parts, sign)):
            out[k1 + 4 * k2] = value
    return out


def split(value):
    high = value.astype(jnp.bfloat16)
    low = (value - high.astype(jnp.float32)).astype(jnp.bfloat16)
    return high, low


def dot(a, b, dims):
    return lax.dot_general(a, b, (dims, ((), ())), preferred_element_type=jnp.float32)


def fetched(source, target, semaphore):
    copy = pltpu.make_async_copy(source, target, semaphore)
    copy.start()
    return copy


def fill_table(table, twiddle, sign, transposed):
    shape = (LANES, LANES)
    row, col = (lax.broadcasted_iota(jnp.int32, shape, n) for n in range(2))
    at = jnp.bitwise_and(row * col, LANES - 1)
    cos, sin = (
        jnp.take_along_axis(
            jnp.broadcast_to(twiddle[n, RADIX : RADIX + 1, :], shape), at, axis=1
        )
        for n in range(2)
    )
    for n, value in enumerate((cos, sign * sin, -sign * sin, cos)):
        high, low = split(value)
        into, out = ((n // 2, n % 2), (n % 2, n // 2))[transposed]
        for m, half in enumerate((high, high, low)):
            if transposed:
                lane = 256 * m + LANES * out
                table[LANES * into : LANES * into + LANES, lane : lane + LANES] = half
            else:
                at_row = 256 * m + LANES * into
                table[at_row : at_row + LANES, LANES * out : LANES * out + LANES] = half


def three_pass(pair, table, dims):
    high = pair[:, :256] if dims[0][0] == 1 else pair[:256, :]
    return dot(pair, table[:512, :], dims) + dot(high, table[512:, :], dims)


def store_pair(held, rows, real, imag):
    high_r, low_r = split(real)
    high_i, low_i = split(imag)
    held[rows, 0:LANES] = high_r
    held[rows, LANES : 2 * LANES] = high_i
    held[rows, 2 * LANES : 3 * LANES] = low_r
    held[rows, 3 * LANES : 4 * LANES] = low_i


def cross_ready(where, image, *pieces):
    for k in range(4):
        to = (where[0] // 2 + k) % 4
        pieces[k][...] = image[:, pl.ds(pl.multiple_of(to * 512, 512), 512)]


def swap_ready(where, *refs):
    pieces, early, late = refs[:4], refs[-2], refs[-1]
    lanes = pl.ds(pl.multiple_of((1 - where[0] % 2) * 256, 256), 256)
    for k in range(4):
        early[k] = pieces[k][:EARLY, lanes]
        late[k] = pieces[k][EARLY:, lanes]


def rows_forward(
    image_in, twiddle_in, out, image, twiddle, out_v, held, table, in_sems, sems
):
    chunk = 16
    steps = LANES // chunk

    def incoming(step):
        rows = pl.ds(step * chunk, chunk)
        return pltpu.make_async_copy(image_in.at[rows, :], image.at[rows, :], in_sems.at[step])

    get_twiddle = fetched(twiddle_in, twiddle, in_sems.at[steps])
    for step in range(steps):
        incoming(step).start()
    get_twiddle.wait()
    fill_table(table, twiddle, -1, True)

    def body(step):
        incoming(step).wait()
        at = step * chunk
        values = [
            (image[pl.ds(at, chunk), b * LANES : (b + 1) * LANES], None) for b in range(RADIX)
        ]
        mixed = sixteen(values, -1)
        for f in range(RADIX):
            real, imag = mixed[f]
            if imag is None:
                imag = jnp.zeros_like(real)
            cos = twiddle[0, f : f + 1, :] * (1.0 / GRID)
            sin = twiddle[1, f : f + 1, :] * (1.0 / GRID)
            store_pair(
                held,
                pl.ds(f * LANES + at, chunk),
                real * cos + imag * sin,
                imag * cos - real * sin,
            )

    for step in range(steps):
        body(step)
    dims = ((1,), (1,))
    sent = []
    for g in range(RADIX // 2):
        pair = held[256 * g : 256 * g + 256, :]
        result = dot(table[:, :512], pair, dims) + dot(table[:, 512:], pair[:, :256], dims)
        for h in range(2):
            for c in range(2):
                block = result[c * LANES : (c + 1) * LANES, h * LANES : (h + 1) * LANES]
                out_v[:, c, 2 * g + h] = block.reshape(RADIX, 8, LANES)
        both = pl.ds(2 * g, 2)
        sent.append(fetched(out_v.at[:, :, both], out.at[:, :, both], sems.at[g]))
    for copy in sent:
        copy.wait()


def data_prepared(weights, measured, place, twiddle, out, forward, inverse, mark, held):
    mark[...] = jnp.zeros_like(mark)
    fill_table(forward, twiddle, -1, False)
    fill_table(inverse, twiddle, 1, False)
    for n in range(3):
        source = weights[...] if n == 0 else measured[n - 1]
        held[...] = source.astype(jnp.float32)
        for f in range(RADIX):
            rows = held[pl.ds(f, LANES, stride=RADIX), :].astype(jnp.bfloat16)
            out[n, f] = dot(place[...], rows, ((1,), (1,))).astype(jnp.bfloat16)


def columns(
    cols_in, data_in, twiddle_in, forward_in, inverse_in, out_all,
    cols, data, twiddle, forward, inverse, out, held_all, in_sems, chunk_sems, out_sems,
):
    chunk = 64
    steps = LANES // chunk
    dims = ((1,), (0,))

    def incoming_cols(step):
        rows = pl.ds(step * chunk, chunk)
        imag_rows = pl.ds(LANES + step * chunk, chunk)
        return [
            pltpu.make_async_copy(cols_in.at[:, r, :], cols.at[:, r, :], chunk_sems.at[step, n])
            for n, r in enumerate((rows, imag_rows))
        ]

    def incoming(step):
        rows = pl.ds(step * chunk, chunk)
        return pltpu.make_async_copy(
            data_in.at[:, :, rows, :], data.at[:, :, rows, :], chunk_sems.at[step, 2]
        )

    def outgoing(step, c):
        rows = pl.ds(c * LANES + step * chunk, chunk)
        return pltpu.make_async_copy(
            out.at[:, rows, :], out_all.at[:, rows, :], out_sems.at[step, c]
        )

    for copy in incoming_cols(0):
        copy.start()
    get_twiddle = fetched(twiddle_in, twiddle, in_sems.at[2])
    get_forward = fetched(forward_in, forward, in_sems.at[0])
    incoming(0).start()
    get_inverse = fetched(inverse_in, inverse, in_sems.at[1])
    for step in range(1, steps):
        for copy in incoming_cols(step):
            copy.start()
        incoming(step).start()
    out[:, 2 * LANES :, :] = jnp.zeros((RADIX, 8, LANES), jnp.float32)
    lane_at = lax.broadcasted_iota(jnp.int32, (8, LANES), 1)
    get_twiddle.wait()

    for step in range(steps):
        held = held_all.at[step % 2]
        at = step * chunk
        here = pl.ds(at, chunk)
        for copy in incoming_cols(step):
            copy.wait()
        imag_here = pl.ds(LANES + at, chunk)
        mixed = sixteen([(cols[b, here, :], cols[b, imag_here, :]) for b in range(RADIX)], -1)
        for f in range(RADIX):
            real, imag = mixed[f]
            cos, sin = twiddle[0, f : f + 1, :], twiddle[1, f : f + 1, :]
            rows = slice(f * chunk, (f + 1) * chunk)
            store_pair(held, rows, real * cos + imag * sin, imag * cos - real * sin)
        if step == 0:
            get_forward.wait()
            get_inverse.wait()
        spectrum = three_pass(held[...], forward, dims)
        incoming(step).wait()
        for f in range(RADIX):
            rows = slice(f * chunk, (f + 1) * chunk)
            weight = data[0, f, here, :].astype(jnp.float32)
            real = weight * spectrum[rows, :LANES] - data[1, f, here, :].astype(jnp.float32)
            imag = weight * spectrum[rows, LANES:] - data[2, f, here, :].astype(jnp.float32)
            store_pair(held, rows, real, imag)
        back = three_pass(held[...], inverse, dims)
        values = []
        for f in range(RADIX):
            rows = slice(f * chunk, (f + 1) * chunk)
            real, imag = back[rows, :LANES], back[rows, LANES:]
            cos, sin = twiddle[0, f : f + 1, :], twiddle[1, f : f + 1, :]
            values.append((real * cos - imag * sin, imag * cos + real * sin))
        mixed = sixteen(values, 1)
        for b in range(RADIX):
            for c in range(2):
                out[b, (here, imag_here)[c], :] = mixed[b][c]
                if b > 0:
                    edge = out[b - 1, 2 * LANES :, :]
                    for i in range(chunk // 8):
                        first = mixed[b][c][8 * i : 8 * i + 8, 0:1]
                        at_lane = lane_at == c * RADIX + step * (chunk // 8) + i
                        edge = jnp.where(at_lane, first, edge)
                    out[b - 1, 2 * LANES :, :] = edge
        for c in range(2):
            outgoing(step, c).start()
    rows = pl.ds(2 * LANES, 8)
    edges = fetched(out.at[:, rows, :], out_all.at[:, rows, :], in_sems.at[0])
    for step in range(steps):
        for c in range(2):
            outgoing(step, c).wait()
    edges.wait()


def arrived(early, late, out):
    out[...] = early[0, :8, :LANES] + late[0, :8, :LANES]


def tied(value, after, out):
    pass


def rows_back(lines, twiddle, after_one, after_two, out, held, side_v, table):
    fill_table(table, twiddle, 1, False)
    dims = ((0,), (0,))
    for f in range(RADIX):
        real = lines[:, 8 * f : 8 * f + 8, :].reshape(LANES, LANES)
        imag = lines[:, LANES + 8 * f : LANES + 8 * f + 8, :].reshape(LANES, LANES)
        high_r, low_r = split(real)
        high_i, low_i = split(imag)
        pair = jnp.concatenate([high_r, high_i, low_r, low_i], axis=0)
        held[f] = three_pass(pair, table, dims)
    high, low = split(lines[:, 2 * LANES :, :].reshape(LANES, LANES))
    edge = (
        dot(high, table[0:LANES, :], dims)
        + dot(low, table[0:LANES, :], dims)
        + dot(high, table[512 : 512 + LANES, :], dims)
    )
    edge_r = edge[:RADIX, :LANES] - edge[RADIX : 2 * RADIX, LANES:]
    edge_i = edge[:RADIX, LANES:] + edge[RADIX : 2 * RADIX, :LANES]
    scale = 1.0 / GRID
    cos, sin = twiddle[0, :RADIX] * scale, twiddle[1, :RADIX] * scale
    edge_r, edge_i = edge_r * cos - edge_i * sin, edge_i * cos + edge_r * sin
    mixed = sixteen([(edge_r[f : f + 1], edge_i[f : f + 1]) for f in range(RADIX)], 1)
    for d in range(CHANNELS):
        out[d, LANES : LANES + 1, :] = jnp.concatenate(
            [mixed[2 * d][0], mixed[2 * d + 1][0]], axis=1
        )
    chunk = 16
    steps = LANES // chunk
    lane_at = lax.broadcasted_iota(jnp.int32, (chunk, LANES), 1)

    def body(step):
        at = step * chunk
        here = pl.ds(at, chunk)
        values = []
        for f in range(RADIX):
            real, imag = held[f, here, :LANES], held[f, here, LANES:]
            cos, sin = twiddle[0, f : f + 1, :] * scale, twiddle[1, f : f + 1, :] * scale
            values.append((real * cos - imag * sin, imag * cos + real * sin))
        mixed = sixteen(values, 1)
        side = jnp.zeros((chunk, LANES), jnp.float32)
        for b in range(RADIX):
            low_lane = (b % 2) * LANES
            out[b // 2, here, low_lane : low_lane + LANES] = mixed[b][0]
            if b > 0 and b % 2 == 0:
                side = jnp.where(lane_at == b // 2 - 1, mixed[b][0][:, 0:1], side)
        side_v[here, :] = side

    for step in range(steps):
        body(step)
    beside = side_v[...].T
    for d in range(CHANNELS):
        out[d, LANES + 1 : LANES + 2, :LANES] = beside[d : d + 1, :]


def dual_edges(dual, last_row, last_column):
    rows, cols = [], []
    for c in range(CHANNELS):
        rows.append(dual[c, 0, 112:128, :].astype(jnp.float32)[15:16, :])
        cols.append(dual[c, 1, :, LANES:].astype(jnp.float32)[:, LANES - 1 :])
    last_row[...] = jnp.concatenate(rows, axis=0)
    last_column[...] = jnp.concatenate(cols, axis=1).T


def tile_ready(where, *refs):
    pieces, (early, late, dual, above, left) = refs[:4], refs[4:9]
    for_image, for_ahead, first_row, first_column = refs[9:]
    row_at = lax.broadcasted_iota(jnp.int32, (LANES, 2 * LANES), 0)
    lane_at = lax.broadcasted_iota(jnp.int32, (LANES, 2 * LANES), 1)
    for k in range(4):
        for other in range(2):
            half = where[0] % 2
            c = (where[0] // 2 + 4 - k) % 4 * 2 + (1 - half if other else half)
            p = dual[c, 0].astype(jnp.float32)
            q = dual[c, 1].astype(jnp.float32)
            beside = jnp.broadcast_to(left[pl.ds(c, 1), :], (LANES, LANES)).T[:, 0:1]
            prev_p = jnp.where(row_at == 0, above[pl.ds(c, 1), :], pltpu.roll(p, 1, 0))
            prev_q = jnp.where(lane_at == 0, beside, pltpu.roll(q, 1, 1))
            adjoint = prev_p - p + prev_q - q
            if other:
                image = jnp.concatenate([early[k], late[k]], axis=0)
            else:
                image = pieces[k][:, pl.ds(pl.multiple_of(half * 256, 256), 256)]
            ahead = image - adjoint
            for_image[c] = image - step_primal * adjoint
            for_ahead[c] = ahead
            first_row[pl.ds(c, 1), :] = ahead[0:1, :]
            first_column[pl.ds(c, 1), :] = ahead[:, :LANES].T[0:1, :]


def finish(
    gradient, for_image, for_ahead, dual, below, right, image_next, dual_next,
    ahead_v, side_v, image_v, dual_v, image_sems, dual_sems,
):
    sides = []
    leaving = []
    for c in range(CHANNELS):
        slope = gradient[c, :LANES, :]
        image_v[c] = for_image[c] - step_primal * slope
        leaving.append(fetched(image_v.at[c], image_next.at[c], image_sems.at[c]))
        ahead_v[c, :LANES, :] = for_ahead[c] - slope
        ahead_v[c, LANES : LANES + 1, :] = (
            below[c : c + 1, :] - gradient[c, LANES : LANES + 1, :]
        )
        sides.append(gradient[c, LANES + 1 : LANES + 2, :LANES])
    side_v[:, :CHANNELS] = (right[...] - jnp.concatenate(sides, axis=0)).T
    chunk = 16
    steps = LANES // chunk
    row_at = lax.broadcasted_iota(jnp.int32, (chunk, 2 * LANES), 0)
    lane_at = lax.broadcasted_iota(jnp.int32, (chunk, 2 * LANES), 1)

    def outgoing(step):
        rows = pl.ds(step * chunk, chunk)
        return pltpu.make_async_copy(
            dual_v.at[:, :, rows, :], dual_next.at[:, :, rows, :], dual_sems.at[step]
        )

    def body(step):
        at = step * chunk
        here = pl.ds(at, chunk)
        after = pl.ds(at + chunk, 8)
        firsts, seconds, total = [], [], None
        for c in range(CHANNELS):
            ahead = ahead_v[c, here, :]
            next_row = ahead_v[c, after, :][0:1, :]
            down = jnp.where(row_at == chunk - 1, next_row, pltpu.roll(ahead, chunk - 1, 0))
            beside = jnp.where(
                lane_at == 2 * LANES - 1,
                side_v[here, c : c + 1],
                pltpu.roll(ahead, 2 * LANES - 1, 1),
            )
            first = dual[c, 0, here, :].astype(jnp.float32) + step_dual * (down - ahead)
            second = dual[c, 1, here, :].astype(jnp.float32) + step_dual * (beside - ahead)
            firsts.append(first)
            seconds.append(second)
            squares = first * first + second * second
            total = squares if total is None else total + squares
        factor = 1.0 / jnp.maximum(1.0, jnp.sqrt(total) / clip_radius)
        for c in range(CHANNELS):
            dual_v[c, 0, here, :] = (firsts[c] * factor).astype(jnp.bfloat16)
            dual_v[c, 1, here, :] = (seconds[c] * factor).astype(jnp.bfloat16)
        outgoing(step).start()

    for step in range(steps):
        body(step)
    for copy in leaving:
        copy.wait()
    for step in range(steps):
        outgoing(step).wait()


def shape(dims, dtype=jnp.float32):
    return jax.ShapeDtypeStruct(dims, dtype)


def passed_along(x, axis, by):
    devices = lax.axis_size(axis)
    pairs = [(i, i + by) for i in range(devices) if 0 <= i + by < devices]
    return lax.ppermute(x, axis, pairs)


ANY = pl.BlockSpec(memory_space=pl.ANY)
HBM = pl.BlockSpec(memory_space=pltpu.HBM)
VM = pl.BlockSpec(memory_space=pltpu.VMEM)
SM = pl.BlockSpec(memory_space=pltpu.SMEM)
DMA = pltpu.SemaphoreType.DMA


def call(kernel, out_shape, in_specs, out_specs, scratch, limit=16):
    return pl.pallas_call(
        kernel,
        out_shape=out_shape,
        in_specs=in_specs,
        out_specs=out_specs,
        scratch_shapes=scratch,
        name=kernel.__name__,
        compiler_params=pltpu.CompilerParams(vmem_limit_bytes=limit * MIB),
    )


def shards(image_field, weights, measured, dual_field):
    twiddle, place = host_tables()
    place = jnp.asarray(place, jnp.bfloat16)
    twiddle = jnp.asarray(twiddle)
    image = image_field[0]
    f32, bf16 = jnp.float32, jnp.bfloat16
    where = lax.axis_index("chan").astype(jnp.int32).reshape(1)

    spread = call(
        rows_forward,
        shape((RADIX, 2, RADIX, 8, LANES)),
        [HBM, HBM],
        HBM,
        [
            pltpu.VMEM((LANES, GRID), f32),
            pltpu.VMEM((2, RADIX + 8, LANES), f32),
            pltpu.VMEM((RADIX, 2, RADIX, 8, LANES), f32),
            pltpu.VMEM((GRID, 512), bf16),
            pltpu.VMEM((256, 768), bf16),
            DMA((9,)),
            DMA((8,)),
        ],
        63,
    )(image, twiddle)
    cols = lax.all_to_all(
        spread.reshape(RADIX, 2 * LANES, LANES), "facet", split_axis=0, concat_axis=0, tiled=True
    )
    last_row, last_column = call(
        dual_edges,
        (shape((CHANNELS, 2 * LANES)), shape((CHANNELS, LANES))),
        [VM],
        (VM, VM),
        [],
    )(dual_field)
    above = passed_along(last_row, "facet", 1)
    left = passed_along(last_column, "chan", 1)
    pieces = list(
        call(cross_ready, (shape((LANES, 512)),) * 4, [SM, VM], (VM,) * 4, [])(where, image)
    )
    for k in range(1, 4):
        pairs = [(2 * x + z, (x + k) % 4 * 2 + z) for x in range(4) for z in range(2)]
        pieces[k] = lax.ppermute(pieces[k], "chan", pairs)
    data, forward, inverse, mark = call(
        data_prepared,
        (
            shape((3, RADIX, LANES, LANES), bf16),
            shape((768, 256), bf16),
            shape((768, 256), bf16),
            shape((8, LANES)),
        ),
        [VM] * 4,
        (VM,) * 4,
        [pltpu.VMEM((GRID, LANES), f32)],
        63,
    )(weights[0], measured[0], place, twiddle)
    early, late = call(
        swap_ready,
        (shape((4, EARLY, 256)), shape((4, LANES - EARLY, 256))),
        [SM] + [VM] * 4 + [HBM, ANY],
        (VM, VM),
        [],
    )(where, *pieces, pltpu.with_memory_space_constraint(mark, pltpu.HBM), last_row)
    other_zl = [(i, i ^ 1) for i in range(8)]
    early = lax.ppermute(early, "chan", other_zl)
    cols, late, above, left, data, forward, inverse = lax.optimization_barrier(
        (cols, late, above, left, data, forward, inverse)
    )
    late = lax.ppermute(late, "chan", other_zl)
    data, forward, inverse = (
        pltpu.with_memory_space_constraint(x, pltpu.HBM) for x in (data, forward, inverse)
    )
    back = call(
        columns,
        shape((RADIX, 2 * LANES + 8, LANES)),
        [HBM] * 5,
        HBM,
        [
            pltpu.VMEM((RADIX, 2 * LANES, LANES), f32),
            pltpu.VMEM((3, RADIX, LANES, LANES), bf16),
            pltpu.VMEM((2, RADIX + 8, LANES), f32),
            pltpu.VMEM((768, 256), bf16),
            pltpu.VMEM((768, 256), bf16),
            pltpu.VMEM((RADIX, 2 * LANES + 8, LANES), f32),
            pltpu.VMEM((2, RADIX * 64, 512), bf16),
            DMA((3,)),
            DMA((2, 3)),
            DMA((2, 2)),
        ],
        63,
    )(cols, data, twiddle, forward, inverse)
    mark = call(arrived, shape((8, LANES)), [VM, VM], VM, [])(early, late)
    back = pl.pallas_call(
        tied,
        out_shape=shape((RADIX, 2 * LANES + 8, LANES)),
        in_specs=[ANY] * 2,
        out_specs=ANY,
        input_output_aliases={0: 0},
        name="tied",
    )(back, mark)
    lines = lax.all_to_all(back, "facet", split_axis=0, concat_axis=0, tiled=True)
    for_image, for_ahead, first_row, first_column = call(
        tile_ready,
        (
            shape((CHANNELS, LANES, 2 * LANES)),
            shape((CHANNELS, LANES, 2 * LANES)),
            shape((CHANNELS, 2 * LANES)),
            shape((CHANNELS, LANES)),
        ),
        [SM] + [VM] * 9,
        (VM,) * 4,
        [],
    )(where, *pieces, early, late, dual_field, above, left)
    below = passed_along(first_row, "facet", -1)
    right = passed_along(first_column, "chan", -1)
    slopes = call(
        rows_back,
        shape((CHANNELS, LANES + 8, 2 * LANES)),
        [VM] * 2 + [ANY] * 2,
        VM,
        [
            pltpu.VMEM((RADIX, LANES, 256), f32),
            pltpu.VMEM((LANES, LANES), f32),
            pltpu.VMEM((768, 256), bf16),
        ],
    )(lines, twiddle, below, right)
    gradient = lax.all_to_all(slopes, "chan", split_axis=0, concat_axis=0, tiled=True)
    return call(
        finish,
        (shape((CHANNELS, LANES, 2 * LANES)), shape((CHANNELS, 2, LANES, 2 * LANES), bf16)),
        [VM] * 6,
        (HBM, HBM),
        [
            pltpu.VMEM((CHANNELS, LANES + 8, 2 * LANES), f32),
            pltpu.VMEM((LANES, LANES), f32),
            pltpu.VMEM((CHANNELS, LANES, 2 * LANES), f32),
            pltpu.VMEM((CHANNELS, 2, LANES, 2 * LANES), bf16),
            DMA((8,)),
            DMA((8,)),
        ],
    )(gradient, for_image, for_ahead, dual_field, below, right)


def solution(mesh):
    placed = (
        P("chan", "facet", None),
        P("chan", None, "facet"),
        P("chan", None, None, "facet"),
        P(None, None, "facet", "chan"),
    )
    return jax.shard_map(
        shards,
        mesh=mesh,
        in_specs=placed,
        out_specs=(P(None, "facet", "chan"), P(None, None, "facet", "chan")),
        check_vma=False,
    )
```
